128 devices in a mesh: patch: 32 (over y, z, x_lo), level: 4 (over x_hi, core).
Axes of the slice: x: 4 (x_hi: 2, x_lo: 2; x = x_hi * 2 + x_lo), y: 4, z: 4, core: 2. Of those that a mesh axis runs over, the one named last changes fastest.
Arguments:
- fields: float32 [6, 64, 32768], P(None, None, ('patch', 'level')), may hold values from -6 to 6
- inv_jacobian: float32 [32768], P(('patch', 'level')), may hold values from 0.5 to 2
- diff_matrix: float32 [3, 64, 64], replicated, may hold values from -0.75 to 0.75
- face_interp: float32 [6, 16, 64], replicated, may hold values from -0.75 to 0.75
- lift_matrix: float32 [6, 64, 16], replicated, may hold values from -1.5 to 1.5
- flux_couple: float32 [6, 6, 6], replicated, may hold values from -2.5 to 2.5
- neighbours: int32 [6, 32768], P(None, ('patch', 'level')), may hold values from 0 to 287
- send_index: int32 [2, 2048], P(None, ('patch', 'level')), may hold values from 0 to 255
- bound_coef: float32 [6], replicated, may hold values from 0.5 to 1.5
- current_coef: float32 [6], replicated, may hold values from -1 to 1
- time_interp: float32 [64], replicated, may hold values from -2 to 2
- current_history: bfloat16 [64, 16384], P(None, ('patch', 'level')), may hold values from -6 to 6
- group_weight: bfloat16 [128, 16384], P(None, ('patch', 'level')), may hold values from -0.1875 to 0.1875
- projection: bfloat16 [16384, 512], P(('patch', 'level')), may hold values from -6 to 6
- kernels: bfloat16 [4, 32, 16, 64], P('level', 'patch'), may hold values from -0.75 to 0.75
- pair_dest: int32 [4, 32, 16], P('level', 'patch'), may hold values from 0 to 31, as said below
- pair_count: int32 [4, 32], P('level', 'patch'), may hold values from 8 to 16
Outputs:
- field_rate: float32 [6, 64, 32768], P(None, None, ('patch', 'level'))
- boundary_field: float32 [64, 16384], P(None, ('patch', 'level'))
The draws below stay inside these ranges and needn't reach their ends.
Inputs may be any that keep to these rules, and one draw needn't show every extreme that they name: `pair_dest`: in each row the 16 entries are distinct patches, none the row's own patch. Only the first pair_count slots of a group are live. `neighbours`: indices below 256 are the device's own elements, then 16 ghosts from the device below and 16 from the device above along patch+level, wrapping. `send_index`: local element indices of the device.
All inputs are finite; a program needn't handle non-finite values.
Results may differ from the reference program's by a relative error of at most 0.0049.
Values may be sent and summed in bfloat16 or wider, within the bound.
No kernel may reach another device: no remote copies, remote signals or barrier semaphores. Data moves between devices by JAX's collectives and lax.ppermute only.
A program may use at most 192 MiB of HBM per device.

```python
import math
import jax
import jax.numpy as jnp
from jax import lax

NP = 64
NFP = 16
BE = 8
E_DEV = 256
HALO = 16
NT = 64
NDIR = 512
B_DEV = 128
GROUPS = 128
PAIRS = 16
ELEMS = 32768
BASIS = 16384
N_PATCH = 32
N_LEVEL = 4
DEVICES = 128


def draw_pair_dest(key, part):
    scores = jax.random.randint(key, (N_LEVEL, N_PATCH, N_PATCH - 1), 0, 1048576)
    scores = scores * N_PATCH + jnp.arange(N_PATCH - 1)[None, None, :]
    order = jnp.argsort(scores, axis=-1, stable=True).astype(jnp.int32)
    offsets = order[:, :, :PAIRS] + 1
    anchor = jnp.arange(N_PATCH, dtype=jnp.int32)[None, :, None]
    return ((anchor + offsets) % N_PATCH).astype(jnp.int32)


def plant(values, stream_key, least, top_value):
    index_at = [jax.random.randint(jax.random.fold_in(stream_key, axis), (), 0, length) for axis, length in enumerate(values.shape)]
    main_axis = values.shape.index(max(values.shape))
    beside = index_at[:main_axis] + [(index_at[main_axis] + 1) % values.shape[main_axis]] + index_at[main_axis + 1:]
    return values.at[tuple(index_at)].set(least).at[tuple(beside)].set(top_value)


def spiked(drawn, key, source, target, blocks, factor):
    owner, partner = [(jnp.arange(drawn.shape[axis_at]) // (drawn.shape[axis_at] // blocks)).reshape([-1 if axis == axis_at else 1 for axis in range(drawn.ndim)]) for axis_at in (source, target)]
    chosen = jax.random.permutation(key, blocks)[partner]
    strong = (owner == chosen) | (owner == (partner + blocks // 2) % blocks)
    return jnp.where(strong, factor * drawn, drawn)


def shard_levels(own_key, extent, shards, least, high):
    gain = 1.0
    for dim, shards_of in shards:
        draws = jax.random.uniform(jax.random.fold_in(jax.random.fold_in(own_key, 6), dim), (shards_of,), jnp.float32, least / len(shards), high / len(shards))
        gain = gain * jnp.repeat(jnp.exp(draws), extent[dim] // shards_of).reshape((-1,) + (1,) * (len(extent) - 1 - dim))
    return gain


def normal_values(stream_key, shape, deviation, most, shards=(), held_as=jnp.bfloat16):
    entries = jax.random.normal(stream_key, shape, jnp.float32) * deviation
    if len(shards) > 0:
        entries = shard_levels(stream_key, shape, shards, -0.22, 0.18) * entries
    return jnp.clip(entries, min=-most, max=most).astype(held_as)


def gaussian_with(key, dims, width, reach, split, heavy, kind=jnp.bfloat16):
    values = width * jax.random.normal(key, dims, jnp.float32)
    if split:
        values = values * shard_levels(key, dims, split, -0.22, 0.18)
    return jnp.clip(spiked(values, jax.random.fold_in(key, 3), *heavy), -reach, reach).astype(kind)


def setup_inputs(seed: int = 0) -> dict:
    arg_keys = jax.random.split(jax.random.key(seed), 18)
    fields = normal_values(arg_keys[0], (6, NP, ELEMS), 1.0, 6.0, ((2, 128),), jnp.float32)
    inv_jacobian = jnp.clip(jnp.exp(math.log(2.0) - 1.3862944 * jax.random.uniform(arg_keys[1], (ELEMS,), jnp.float32) ** shard_levels(arg_keys[1], (ELEMS,), ((0, 128),), -0.2, 0.2)), 0.5, 2.0)
    diff_matrix = normal_values(arg_keys[2], (3, NP, NP), NP ** -0.5, 0.75, (), jnp.float32)
    face_interp = normal_values(arg_keys[3], (6, NFP, NP), NP ** -0.5, 0.75, (), jnp.float32)
    lift_matrix = normal_values(arg_keys[4], (6, NP, NFP), NFP ** -0.5, 1.5, (), jnp.float32)
    flux_couple = normal_values(arg_keys[5], (6, 6, 6), 6 ** -0.5, 2.5, (), jnp.float32)
    neighbours = plant(jax.random.randint(arg_keys[6], (6, ELEMS), 0, E_DEV + 2 * HALO), jax.random.fold_in(arg_keys[6], 1), 0, (E_DEV + 2 * HALO) - 1).astype(jnp.int32)
    send_index = plant(jax.random.randint(arg_keys[7], (2, HALO * DEVICES), 0, E_DEV), jax.random.fold_in(arg_keys[7], 1), 0, E_DEV - 1).astype(jnp.int32)
    bound_coef = jnp.clip(jax.random.uniform(arg_keys[8], (6,), jnp.float32, 0.5, 1.5), 0.5, 1.5)
    current_coef = jnp.clip(jax.random.uniform(arg_keys[9], (6,), jnp.float32, -1.0, 1.0), -1.0, 1.0)
    time_interp = normal_values(arg_keys[10], (NT,), 8 ** -0.5, 2.0, (), jnp.float32)
    current_history = normal_values(arg_keys[11], (NT, BASIS), 1.0, 6.0, ((1, 128),))
    group_weight = gaussian_with(arg_keys[12], (GROUPS, BASIS), BASIS ** -0.5, 0.1875, ((1, 128),), (1, 0, 128, 5.5))
    projection = normal_values(arg_keys[13], (BASIS, NDIR), 1.0, 6.0, ((0, 128),))
    kernels = normal_values(arg_keys[14], (N_LEVEL, N_PATCH, PAIRS, NT), NT ** -0.5, 0.75, ((0, 4), (1, 32)))
    pair_dest = draw_pair_dest(jax.random.fold_in(arg_keys[17], 71), 0)
    pair_count = plant(jax.random.randint(arg_keys[16], (N_LEVEL, N_PATCH), PAIRS // 2, PAIRS + 1), jax.random.fold_in(arg_keys[16], 1), PAIRS // 2, PAIRS).astype(jnp.int32)
    return dict(fields=fields, inv_jacobian=inv_jacobian, diff_matrix=diff_matrix, face_interp=face_interp, lift_matrix=lift_matrix, flux_couple=flux_couple, neighbours=neighbours, send_index=send_index, bound_coef=bound_coef, current_coef=current_coef, time_interp=time_interp, current_history=current_history, group_weight=group_weight, projection=projection, kernels=kernels, pair_dest=pair_dest, pair_count=pair_count)


HIGH = lax.Precision.HIGHEST

def toeplitz(rows):
    count = rows.shape[-1]
    lagged = jnp.arange(count)[:, None] - jnp.arange(count)[None, :]
    picked = jnp.take(rows, jnp.clip(lagged, 0, count - 1), axis=-1)
    return jnp.where(lagged >= 0, picked, jnp.zeros_like(picked))

def own_traces(face_interp, local):
    return jnp.einsum('fqn,cne->fcqe', face_interp, local, precision=HIGH)

def element_rate(local, pool, scale, links, exterior, face_interp, lift_matrix, flux_couple, diff_matrix, own):
    opposite = face_interp[jnp.array([1, 0, 3, 2, 5, 4])]
    across = pool[:, :, links]
    neighbour = jnp.einsum('fqn,cnfe->fcqe', opposite, across, precision=HIGH)
    padded = jnp.pad(exterior, ((0, 0), (0, 0), (0, local.shape[2] - exterior.shape[2])))
    isbound = (jnp.arange(6)[:, None, None, None] == 5) & (jnp.arange(local.shape[2])[None, None, None, :] < BE)
    neighbour = jnp.where(isbound, padded[None], neighbour)
    flux = jnp.einsum('fcd,fdqe->fcqe', flux_couple, neighbour - own, precision=HIGH)
    surface = jnp.einsum('fnq,fcqe->cne', lift_matrix, flux, precision=HIGH)
    grads = jnp.einsum('rmn,cne->rcme', diff_matrix, local, precision=HIGH) * scale
    electric = jnp.stack([grads[1, 5] - grads[2, 4], grads[2, 3] - grads[0, 5], grads[0, 4] - grads[1, 3]])
    magnetic = -jnp.stack([grads[1, 2] - grads[2, 1], grads[2, 0] - grads[0, 2], grads[0, 1] - grads[1, 0]])
    return jnp.concatenate([electric, magnetic], axis=0) + surface

def reference(fields, inv_jacobian, diff_matrix, face_interp, lift_matrix, flux_couple, neighbours, send_index, bound_coef, current_coef, time_interp, current_history, group_weight, projection, kernels, pair_dest, pair_count):
    devices = N_PATCH * N_LEVEL
    local = fields.reshape(6, NP, devices, E_DEV).transpose(2, 0, 1, 3)
    listed = send_index.reshape(2, devices, HALO).transpose(1, 0, 2).reshape(devices, 2 * HALO)
    packed = jax.vmap(lambda block, index: block[:, :, index])(local, listed)
    lower = jnp.roll(packed, 1, axis=0)[..., HALO:]
    upper = jnp.roll(packed, -1, axis=0)[..., :HALO]
    pool = jnp.concatenate([local, lower, upper], axis=-1)
    links = neighbours.reshape(6, devices, E_DEV).transpose(1, 0, 2)
    scales = inv_jacobian.reshape(devices, E_DEV)
    own = jax.vmap(lambda block: own_traces(face_interp, block))(local)
    newest = jnp.einsum('c,dcqe->deq', current_coef, own[:, 5, :, :, :BE], precision=HIGH)
    newest = newest.reshape(1, devices * B_DEV).astype(jnp.bfloat16)
    currents = jnp.concatenate([current_history[1:], newest], axis=0)

    def one_group(row):
        weighted = (currents.astype(jnp.float32) * row.astype(jnp.float32)[None, :]).astype(jnp.bfloat16)
        return jnp.dot(weighted, projection, preferred_element_type=jnp.float32).astype(jnp.bfloat16)
    rays = lax.map(one_group, group_weight)
    live = jnp.arange(PAIRS)[None, None, :] < pair_count[:, :, None]
    slots = (pair_dest[:, :, None, :] == jnp.arange(N_PATCH)[None, None, :, None]) & live[:, :, None, :]
    table = jnp.einsum('lpqj,lpjt->lpqt', slots.astype(jnp.float32), kernels.astype(jnp.float32), precision=HIGH)
    blocks = toeplitz(table)
    sources = rays.reshape(N_PATCH, N_LEVEL, NT, NDIR).transpose(1, 0, 2, 3).astype(jnp.float32)
    incoming = jnp.einsum('lpqts,lpsk->lqtk', blocks, sources, precision=HIGH)
    incoming = incoming.transpose(1, 0, 2, 3).reshape(devices, NT, NDIR).astype(jnp.bfloat16)

    def add_group(total, pair):
        block, row = pair
        image = jnp.dot(block, projection.T, preferred_element_type=jnp.float32)
        return (total + image * row.astype(jnp.float32)[None, :], None)
    start = jnp.zeros((NT, devices * B_DEV), jnp.float32)
    boundary_field, _ = lax.scan(add_group, start, (incoming, group_weight))
    boundary_field = boundary_field * (1.0 / jnp.sqrt(jnp.float32(NDIR)))
    interp = jnp.dot(time_interp, boundary_field, precision=HIGH).reshape(devices, BE, NFP)
    exterior = bound_coef[None, :, None, None] * interp.transpose(0, 2, 1)[:, None]
    rates = jax.vmap(lambda a, b, c, d, e, f: element_rate(a, b, c, d, e, face_interp, lift_matrix, flux_couple, diff_matrix, f))(local, pool, scales, links, exterior, own)
    field_rate = rates.transpose(1, 2, 0, 3).reshape(6, NP, devices * E_DEV)
    return (field_rate, boundary_field)
```

```python
import functools

import jax
import jax.numpy as jnp
import numpy as np
from jax import lax
from jax.experimental import pallas as pl
from jax.experimental.pallas import tpu as pltpu
from jax.sharding import Mesh, PartitionSpec as P

F32 = jnp.float32
BF16 = jnp.bfloat16
HIGH = lax.Precision.HIGHEST
AXES = ("y", "z", "xl", "xh", "c")
VMEM = pl.BlockSpec(memory_space=pltpu.VMEM)
SMEM = pl.BlockSpec(memory_space=pltpu.SMEM)
ROW_C, ROW_W, ROW_T, ROWS = 128, 192, 256, 272
NN = (((1,), (0,)), ((), ()))
NT = (((1,), (1,)), ((), ()))
TN = (((0,), (0,)), ((), ()))


def iota(shape, dim):
    return lax.broadcasted_iota(jnp.int32, shape, dim)


def mm(a, b, dims=NN, precision=None):
    return lax.dot_general(a, b, dims, precision=precision, preferred_element_type=F32)


def one_hot(mask, dtype=F32):
    return jnp.where(mask, 1.0, 0.0).astype(dtype)


def halves(x):
    high = x.astype(BF16)
    return high, (x - high.astype(F32)).astype(BF16)


def lane_blocks_swapped(parts):
    parts = list(parts)
    shape = parts[0].shape
    block = iota(shape, 1) // 16
    for m in (4, 2, 1):
        upper = (block & m) != 0
        for j in range(8):
            if j & m:
                continue
            a, b = parts[j], parts[j + m]
            parts[j] = jnp.where(upper, pltpu.roll(b, 16 * m, 1), a)
            parts[j + m] = jnp.where(upper, b, pltpu.roll(a, 128 - 16 * m, 1))
    return parts


def pack_kernel(
    core_ref, send_ref, dest_ref, count_ref, coef_ref,
    fields_ref, interp_ref, history_ref, weight_ref, projection_ref, kernels_ref,
    message_ref, on_ref, off_ref,
):
    core = core_ref[0]
    elements = fields_ref.shape[2]
    flat = fields_ref[...].reshape(384, elements).astype(BF16)

    def picked(row):
        rows, lanes = iota((16, elements), 0), iota((16, elements), 1)
        wanted = jnp.zeros((16, elements), jnp.int32)
        for i in range(16):
            wanted = jnp.where(rows == i, send_ref[row, i], wanted)
        return mm(one_hot(lanes == wanted, BF16), flat, NT).astype(BF16)

    on_ref[...] = picked(1 - core)
    off_ref[...] = picked(core)
    mixed = jnp.zeros((64, 128), F32)
    for c in range(6):
        mixed = mixed + coef_ref[c] * fields_ref[c, :, 0:128]
    spread = one_hot(iota((128, 128), 1) // 16 == iota((128, 128), 0))
    chosen = one_hot(iota((16, 128), 1) % 16 == iota((16, 128), 0))
    by_element = mm(mixed, spread, NN, HIGH)
    by_node = mm(interp_ref[5], chosen, TN, HIGH)
    newest = jnp.sum(by_element * by_node, axis=0, keepdims=True)
    old = pltpu.roll(history_ref[...].astype(F32), 63, 0)
    currents = jnp.where(iota((64, 128), 0) == 63, newest, old).astype(BF16)
    lane_patch = iota((16, 128), 1) % 32
    wanted = jnp.full((16, 128), -1, jnp.int32)
    for j in range(16):
        to = jnp.where(j < count_ref[0, 0], dest_ref[0, 0, j], -1)
        wanted = jnp.where(iota((16, 128), 0) == j, to, wanted)
    spread_kernels = mm(kernels_ref[0, 0], one_hot(wanted == lane_patch, BF16), TN)
    group_of = iota((8, 128), 1) // 32
    table = []
    for h in range(2):
        rows = jnp.zeros((8, 128), F32)
        for a in range(4):
            at = 32 * h + 8 * a
            rows = jnp.where(group_of == a, spread_kernels[at : at + 8], rows)
        table.append(rows)
    table = jnp.concatenate(table, axis=0).astype(BF16)
    weights = []
    for level in range(4):
        pick = one_hot(iota((32, 128), 1) == 4 * iota((32, 128), 0) + level, BF16)
        weights.append(mm(pick, weight_ref[...]).astype(BF16))
    for i in range(8):
        z, xh = i // 2, i % 2
        message_ref[i, 0:128, :] = projection_ref[:, 128 * z : 128 * z + 128]
        message_ref[i, ROW_C : ROW_C + 64, :] = currents
        message_ref[i, ROW_W : ROW_W + 32, :] = weights[2 * xh]
        message_ref[i, ROW_W + 32 : ROW_W + 64, :] = weights[2 * xh + 1]
        message_ref[i, ROW_T:ROWS, :] = table


def own_weights(ref, i, core):
    return ref[i, pl.ds(pl.multiple_of(ROW_W + 32 * core, 32), 32), :]


def rays_kernel(core_ref, mine_ref, other_ref, out_ref, c_ref, w_ref, p_ref):
    core = core_ref[0]
    for i in range(8):
        for s, ref in ((0, mine_ref), (1, other_ref)):
            at = 256 * i + 128 * s
            c_ref[:, at : at + 128] = ref[i, ROW_C : ROW_C + 64, :].astype(F32)
            w_ref[:, at : at + 128] = own_weights(ref, i, core).astype(F32)
            p_ref[at : at + 128, :] = ref[i, 0:128, :]

    def step(high, carry):
        c = c_ref[pl.ds(pl.multiple_of(8 * high, 8), 8), :]
        w = w_ref[...]
        rows = [(c[t : t + 1] * w).astype(BF16) for t in range(8)]
        product = mm(jnp.concatenate(rows, axis=0), p_ref[...])
        parts = lane_blocks_swapped([product[32 * t : 32 * t + 32] for t in range(8)])
        for r in range(8):
            out_ref[r, pl.ds(pl.multiple_of(32 * high, 32), 32), :] = parts[r].astype(BF16)
        return carry

    lax.fori_loop(0, 8, step, 0)
    half = core_ref[1]
    for r in range(8):
        for z in range(4):
            out_ref[r, 256 + 16 * z : 272 + 16 * z, :] = mine_ref[2 * z + half, ROW_T:ROWS, :]


def translate_kernel(got_ref, out_ref, h_ref, s_ref):
    total = got_ref[0, 0:256, :].astype(F32)
    for r in range(1, 8):
        total = total + got_ref[r, 0:256, :].astype(F32)
    rays = total.astype(BF16).astype(F32)
    for r in range(8):
        y, xl = r // 2, r % 2
        for z in range(4):
            patch = 8 * y + 2 * z + xl
            tile = got_ref[r, 256 + 16 * z : 272 + 16 * z, :].astype(F32)
            for h in range(2):
                h_ref[h, pl.ds(patch, 8, stride=32), :] = tile[8 * h : 8 * h + 8]
    table = jnp.concatenate([h_ref[0], h_ref[1]], axis=1).astype(BF16)
    by_high = [rays[32 * t : 32 * t + 32] for t in range(8)]
    lane = iota((32, 128), 1)
    columns = []
    for t in range(8):
        rows = [by_high[t]]
        for b in range(1, 8):
            here = pltpu.roll(by_high[t], 16 * b, 1)
            before = pltpu.roll(by_high[t - 1], 16 * b, 1) if t > 0 else jnp.zeros((32, 128), F32)
            rows.append(jnp.where(lane < 16 * b, before, here))
        columns.append(jnp.concatenate(rows, axis=0).astype(BF16))
    lagged = [mm(table, column, TN) for column in columns]
    for t in range(8):
        incoming = lagged[t][0:32]
        for a in range(1, t + 1):
            incoming = incoming + lagged[t - a][32 * a : 32 * a + 32]
        s_ref[pl.ds(t, 32, stride=8), :] = incoming
    incoming = s_ref[...].astype(BF16)
    for r in range(8):
        out_ref[r] = incoming


def image_kernel(core_ref, got_ref, mine_ref, other_ref, own_ref, partner_ref, rows_ref):
    core = core_ref[0]
    parts = lane_blocks_swapped([got_ref[r].astype(F32) for r in range(8)])
    for t in range(8):
        rows_ref[256 * t : 256 * t + 256, :] = parts[t].astype(BF16)

    def step(i, carry):
        for ref, out in ((mine_ref, own_ref), (other_ref, partner_ref)):
            image = mm(rows_ref[...], ref[i, 0:128, :], NT)
            weight = own_weights(ref, i, core).astype(F32)
            weight = jnp.broadcast_to(weight[:, None, :], (32, 8, 128))
            for t in range(8):
                block = image[256 * t : 256 * t + 256].reshape(32, 8, 128)
                out[i, 8 * t : 8 * t + 8, :] = jnp.sum(block * weight, axis=0)
        return carry

    lax.fori_loop(0, 8, step, 0)


def element_kernel(
    core_ref, couple_ref, fields_ref, scale_ref, diff_ref, interp_ref, lift_ref, links_ref,
    on_ref, off_ref, out_ref,
):
    core = core_ref[0]
    elements = fields_ref.shape[2]
    interp = interp_ref[...].reshape(96, 64)
    diff = diff_ref[...].reshape(192, 64)
    ghosts = jnp.concatenate([on_ref[...], off_ref[...]], axis=0).astype(F32)
    own, ghost = [], []
    grads = []
    for c in range(6):
        local = fields_ref[c]
        own.append(mm(interp, local, NN, HIGH))
        ghost.append(mm(interp, ghosts[:, 64 * c : 64 * c + 64], NT, HIGH))
        grads.append(mm(diff, local, NN, HIGH))
    surface = [jnp.zeros((64, elements), F32) for _ in range(6)]
    bound = iota((16, elements), 1) < 8
    for f in range(6):
        at, to = 16 * f, 16 * (f ^ 1)
        pool = jnp.concatenate([own[c][to : to + 16] for c in range(6)], axis=0)
        beyond = jnp.concatenate([ghost[c][to : to + 16] for c in range(6)], axis=0)
        links = links_ref[f : f + 1, :]
        inside = one_hot(iota((elements, elements), 0) == links, BF16)
        outer = links - elements
        outer = jnp.where(core == 0, outer ^ 16, outer)
        outside = one_hot(iota((32, elements), 0) == outer, BF16)
        high, low = halves(pool)
        ghost_high, ghost_low = halves(beyond)
        across = mm(high, inside) + mm(low, inside) + mm(ghost_high, outside) + mm(ghost_low, outside)
        jumps = []
        for c in range(6):
            there = across[16 * c : 16 * c + 16]
            if f == 5:
                there = jnp.where(bound, 0.0, there)
            jumps.append(there - own[c][at : at + 16])
        for c in range(6):
            flux = couple_ref[f, c, 0] * jumps[0]
            for k in range(1, 6):
                flux = flux + couple_ref[f, c, k] * jumps[k]
            surface[c] = surface[c] + mm(lift_ref[f], flux, NN, HIGH)

    def grad(r, c):
        return grads[c][64 * r : 64 * r + 64]

    curls = (
        grad(1, 5) - grad(2, 4),
        grad(2, 3) - grad(0, 5),
        grad(0, 4) - grad(1, 3),
        grad(2, 1) - grad(1, 2),
        grad(0, 2) - grad(2, 0),
        grad(1, 0) - grad(0, 1),
    )
    scale = scale_ref[...]
    for c in range(6):
        out_ref[c] = curls[c] * scale + surface[c]


def finish_kernel(
    bound_ref, couple_ref, parts_ref, rate_ref, lift_ref, time_ref, rate_out, field_out,
):
    total = parts_ref[0]
    for i in range(1, 8):
        total = total + parts_ref[i]
    total = total * jnp.float32(1.0 / np.sqrt(np.float32(512)))
    for t in range(8):
        field_out[pl.ds(t, 8, stride=8), :] = total[8 * t : 8 * t + 8]
    now = mm(time_ref[...], field_out[...], NN, HIGH)
    node = iota((16, 128), 1) % 16 == iota((16, 128), 0)
    by_node = jnp.where(node, now, 0.0)
    collect = one_hot(iota((128, 128), 0) // 16 == iota((128, 128), 1))
    lifted = mm(lift_ref[5], mm(by_node, collect, NN, HIGH), NN, HIGH)
    for c in range(6):
        factor = couple_ref[5, c, 0] * bound_ref[0]
        for k in range(1, 6):
            factor = factor + couple_ref[5, c, k] * bound_ref[k]
        rate_out[c, :, 0:128] = rate_ref[c, :, 0:128] + factor * lifted
        rate_out[c, :, 128:256] = rate_ref[c, :, 128:256]


def call(kernel, out, in_specs, scratch=(), **options):
    return pl.pallas_call(
        kernel,
        out_shape=out,
        in_specs=in_specs,
        out_specs=jax.tree.map(lambda _: VMEM, out),
        scratch_shapes=list(scratch),
        **options,
    )


def shaped(shape, dtype):
    return jax.ShapeDtypeStruct(shape, dtype)


def per_device(
    fields, inv_jacobian, diff_matrix, face_interp, lift_matrix, flux_couple, neighbours,
    send_index, bound_coef, current_coef, time_interp, current_history, group_weight, projection,
    kernels, pair_dest, pair_count,
):
    place = jnp.stack([lax.axis_index("c"), lax.axis_index("xh")]).astype(jnp.int32)
    message, on_chip, off_chip = call(
        pack_kernel,
        (shaped((8, ROWS, 128), BF16), shaped((16, 384), BF16), shaped((16, 384), BF16)),
        [SMEM] * 5 + [VMEM] * 6,
    )(
        place, send_index, pair_dest, pair_count, current_coef,
        fields, face_interp, current_history, group_weight, projection, kernels,
    )
    devices = 128
    across = [(d, (d + 1 if d % 2 else d - 1) % devices) for d in range(devices)]
    off_chip = lax.ppermute(off_chip, AXES, across)
    on_chip = lax.ppermute(on_chip, "c", [(0, 1), (1, 0)])
    mine = lax.all_to_all(message, ("z", "xh"), 0, 0, tiled=True)
    other = lax.ppermute(mine, "c", [(0, 1), (1, 0)])
    rate = call(
        element_kernel, shaped((6, 64, 256), F32), [SMEM] * 2 + [VMEM] * 8
    )(
        place, flux_couple, fields, inv_jacobian.reshape(1, -1), diff_matrix, face_interp,
        lift_matrix, neighbours, on_chip, off_chip,
    )
    partial = call(
        rays_kernel,
        shaped((8, 320, 128), BF16),
        [SMEM, VMEM, VMEM],
        (pltpu.VMEM((64, 2048), F32), pltpu.VMEM((32, 2048), F32), pltpu.VMEM((2048, 128), BF16)),
    )(place, mine, other)
    partial = lax.all_to_all(partial, ("y", "xl"), 0, 0, tiled=True)
    incoming = call(
        translate_kernel,
        shaped((8, 256, 128), BF16),
        [VMEM],
        (pltpu.VMEM((2, 256, 128), F32), pltpu.VMEM((256, 128), F32)),
    )(partial)
    incoming = lax.all_to_all(incoming, ("y", "xl"), 0, 0, tiled=True)
    own, partner = call(
        image_kernel,
        (shaped((8, 64, 128), F32), shaped((8, 64, 128), F32)),
        [SMEM, VMEM, VMEM, VMEM],
        (pltpu.VMEM((2048, 128), BF16),),
    )(place, incoming, mine, other)
    parts = own + lax.ppermute(partner, "c", [(0, 1), (1, 0)])
    parts = lax.all_to_all(parts, ("z", "xh"), 0, 0, tiled=True)
    return call(
        finish_kernel,
        (shaped((6, 64, 256), F32), shaped((64, 128), F32)),
        [SMEM] * 2 + [VMEM] * 4,
    )(bound_coef, flux_couple, parts, rate, lift_matrix, time_interp.reshape(1, -1))


def solution(mesh):
    mesh = Mesh(np.asarray(mesh.devices).reshape(4, 4, 2, 2, 2), AXES)
    patch, level = ("y", "z", "xl"), ("xh", "c")
    placed = (
        P(None, None, AXES), P(AXES), P(), P(), P(), P(), P(None, AXES), P(None, AXES), P(), P(),
        P(), P(None, AXES), P(None, AXES), P(AXES, None), P(level, patch, None, None),
        P(level, patch, None), P(level, patch),
    )
    return jax.shard_map(
        per_device,
        mesh=mesh,
        in_specs=placed,
        out_specs=(P(None, None, AXES), P(None, AXES)),
        check_vma=False,
    )
```

```python
import functools

import jax
import jax.numpy as jnp
import numpy as np
from jax import lax
from jax.experimental import pallas as pl
from jax.experimental.pallas import tpu as pltpu
from jax.sharding import Mesh, PartitionSpec as P

F32 = jnp.float32
BF16 = jnp.bfloat16
HIGH = lax.Precision.HIGHEST
AXES = ("y", "z", "xl", "xh", "c")
VMEM = pl.BlockSpec(memory_space=pltpu.VMEM)
SMEM = pl.BlockSpec(memory_space=pltpu.SMEM)
ROW_C, ROW_W, ROW_T, ROWS = 256, 320, 352, 368
NN = (((1,), (0,)), ((), ()))
NT = (((1,), (1,)), ((), ()))
TN = (((0,), (0,)), ((), ()))


def iota(shape, dim):
    return lax.broadcasted_iota(jnp.int32, shape, dim)


def mm(a, b, dims=NN, precision=None):
    return lax.dot_general(a, b, dims, precision=precision, preferred_element_type=F32)


def one_hot(mask, dtype=F32):
    return jnp.where(mask, 1.0, 0.0).astype(dtype)


def halves(x):
    high = x.astype(BF16)
    return high, (x - high.astype(F32)).astype(BF16)


def lane_blocks_swapped(parts):
    parts = list(parts)
    shape = parts[0].shape
    block = iota(shape, 1) // 16
    for m in (4, 2, 1):
        upper = (block & m) != 0
        for j in range(8):
            if j & m:
                continue
            a, b = parts[j], parts[j + m]
            parts[j] = jnp.where(upper, pltpu.roll(b, 16 * m, 1), a)
            parts[j + m] = jnp.where(upper, b, pltpu.roll(a, 128 - 16 * m, 1))
    return parts


def pack_kernel(
    place_ref, send_ref, dest_ref, count_ref, coef_ref,
    fields_ref, interp_ref, history_ref, weight_ref, projection_ref, kernels_ref,
    message_ref, on_ref, off_ref,
):
    core = place_ref[0]
    elements = fields_ref.shape[2]
    flat = fields_ref[...].reshape(384, elements).astype(BF16)

    def picked(row):
        rows, lanes = iota((16, elements), 0), iota((16, elements), 1)
        wanted = jnp.zeros((16, elements), jnp.int32)
        for i in range(16):
            wanted = jnp.where(rows == i, send_ref[row, i], wanted)
        return mm(one_hot(lanes == wanted, BF16), flat, NT).astype(BF16)

    on_ref[...] = picked(1 - core)
    off_ref[...] = picked(core)
    mixed = jnp.zeros((64, 128), F32)
    for c in range(6):
        mixed = mixed + coef_ref[c] * fields_ref[c, :, 0:128]
    spread = one_hot(iota((128, 128), 1) // 16 == iota((128, 128), 0))
    chosen = one_hot(iota((16, 128), 1) % 16 == iota((16, 128), 0))
    by_element = mm(mixed, spread, NN, HIGH)
    by_node = mm(interp_ref[5], chosen, TN, HIGH)
    newest = jnp.sum(by_element * by_node, axis=0, keepdims=True)
    old = pltpu.roll(history_ref[...].astype(F32), 63, 0)
    currents = jnp.where(iota((64, 128), 0) == 63, newest, old).astype(BF16)
    lane_patch = iota((16, 128), 1) % 32
    wanted = jnp.full((16, 128), -1, jnp.int32)
    for j in range(16):
        to = jnp.where(j < count_ref[0, 0], dest_ref[0, 0, j], -1)
        wanted = jnp.where(iota((16, 128), 0) == j, to, wanted)
    spread_kernels = mm(kernels_ref[0, 0], one_hot(wanted == lane_patch, BF16), TN)
    group_of = iota((8, 128), 1) // 32
    table = []
    for h in range(2):
        rows = jnp.zeros((8, 128), F32)
        for a in range(4):
            at = 32 * h + 8 * a
            rows = jnp.where(group_of == a, spread_kernels[at : at + 8], rows)
        table.append(rows)
    table = jnp.concatenate(table, axis=0).astype(BF16)
    weights = []
    for level in range(4):
        pick = one_hot(iota((32, 128), 1) == 4 * iota((32, 128), 0) + level, BF16)
        weights.append(mm(pick, weight_ref[...]).astype(BF16))
    for i in range(8):
        z, xh = i // 2, i % 2
        at = 256 * (z // 2)
        message_ref[i, 0:128, :] = projection_ref[:, at : at + 128]
        message_ref[i, 128:256, :] = projection_ref[:, at + 128 : at + 256]
        message_ref[i, ROW_C : ROW_C + 64, :] = currents
        message_ref[i, ROW_W : ROW_W + 32, :] = weights[2 * xh + z % 2]
        message_ref[i, ROW_T:ROWS, :] = table


def rays_kernel(place_ref, got_ref, keep_ref, send_ref, c_ref, w_ref, p_ref):
    core, half = place_ref[0], place_ref[1]
    mine = pl.multiple_of(128 * core, 128)
    theirs = pl.multiple_of(128 * (1 - core), 128)
    for i in range(8):
        at = 128 * i
        c_ref[:, at : at + 128] = got_ref[i, ROW_C : ROW_C + 64, :].astype(F32)
        w_ref[:, at : at + 128] = got_ref[i, ROW_W : ROW_W + 32, :].astype(F32)
        p_ref[at : at + 128, 0:128] = got_ref[i, pl.ds(mine, 128), :]
        p_ref[at : at + 128, 128:256] = got_ref[i, pl.ds(theirs, 128), :]

    def step(high, carry):
        c = c_ref[pl.ds(pl.multiple_of(8 * high, 8), 8), :]
        w = w_ref[...]
        rows = [(c[t : t + 1] * w).astype(BF16) for t in range(8)]
        product = mm(jnp.concatenate(rows, axis=0), p_ref[...])
        at = pl.multiple_of(32 * high, 32)
        kept = lane_blocks_swapped([product[32 * t : 32 * t + 32, 0:128] for t in range(8)])
        sent = lane_blocks_swapped([product[32 * t : 32 * t + 32, 128:256] for t in range(8)])
        for r in range(8):
            keep_ref[r, pl.ds(at, 32), :] = kept[r]
            send_ref[r, pl.ds(at, 32), :] = sent[r].astype(BF16)
        return carry

    lax.fori_loop(0, 8, step, 0)
    for z in range(4):
        send_ref[z, 256:272, :] = got_ref[2 * z + half, ROW_T:ROWS, :]


def joined_kernel(place_ref, keep_ref, send_ref, came_ref, out_ref):
    has_tables = place_ref[0] == place_ref[2]
    tables = []
    for z in range(4):
        here, there = send_ref[z, 256:272, :], came_ref[z, 256:272, :]
        tables.append(jnp.where(has_tables, here.astype(F32), there.astype(F32)).astype(BF16))
    tables = jnp.concatenate(tables, axis=0)
    for r in range(8):
        out_ref[r, 0:256, :] = (keep_ref[r] + came_ref[r, 0:256, :].astype(F32)).astype(BF16)
        out_ref[r, 256:320, :] = tables


def translate_kernel(got_ref, out_ref, h_ref, s_ref):
    total = got_ref[0, 0:256, :].astype(F32)
    for r in range(1, 8):
        total = total + got_ref[r, 0:256, :].astype(F32)
    rays = total.astype(BF16).astype(F32)
    for r in range(8):
        y, xl = r // 2, r % 2
        for z in range(4):
            patch = 8 * y + 2 * z + xl
            tile = got_ref[r, 256 + 16 * z : 272 + 16 * z, :].astype(F32)
            for h in range(2):
                h_ref[h, pl.ds(patch, 8, stride=32), :] = tile[8 * h : 8 * h + 8]
    table = jnp.concatenate([h_ref[0], h_ref[1]], axis=1).astype(BF16)
    by_high = [rays[32 * t : 32 * t + 32] for t in range(8)]
    lane = iota((32, 128), 1)
    columns = []
    for t in range(8):
        rows = [by_high[t]]
        for b in range(1, 8):
            here = pltpu.roll(by_high[t], 16 * b, 1)
            before = pltpu.roll(by_high[t - 1], 16 * b, 1) if t > 0 else jnp.zeros((32, 128), F32)
            rows.append(jnp.where(lane < 16 * b, before, here))
        columns.append(jnp.concatenate(rows, axis=0).astype(BF16))
    lagged = [mm(table, column, TN) for column in columns]
    for t in range(8):
        incoming = lagged[t][0:32]
        for a in range(1, t + 1):
            incoming = incoming + lagged[t - a][32 * a : 32 * a + 32]
        s_ref[pl.ds(t, 32, stride=8), :] = incoming
    incoming = s_ref[...].astype(BF16)
    for r in range(8):
        out_ref[r] = incoming


def image_kernel(place_ref, here_ref, there_ref, got_ref, out_ref, rows_ref, p_ref):
    core = place_ref[0]
    mine = pl.multiple_of(128 * core, 128)
    theirs = pl.multiple_of(128 * (1 - core), 128)
    for h, ref in ((0, here_ref), (1, there_ref)):
        parts = lane_blocks_swapped([ref[r].astype(F32) for r in range(8)])
        for t in range(8):
            rows_ref[256 * t : 256 * t + 256, 128 * h : 128 * h + 128] = parts[t].astype(BF16)

    def step(i, carry):
        for s in range(2):
            p_ref[128 * s : 128 * s + 128, 0:128] = got_ref[2 * i + s, pl.ds(mine, 128), :]
            p_ref[128 * s : 128 * s + 128, 128:256] = got_ref[2 * i + s, pl.ds(theirs, 128), :]
        image = mm(rows_ref[...], p_ref[...], NT)
        for s in range(2):
            weight = got_ref[2 * i + s, ROW_W : ROW_W + 32, :].astype(F32)
            weight = jnp.broadcast_to(weight[:, None, :], (32, 8, 128))
            for t in range(8):
                block = image[256 * t : 256 * t + 256, 128 * s : 128 * s + 128]
                block = block.reshape(32, 8, 128) * weight
                out_ref[2 * i + s, 8 * t : 8 * t + 8, :] = jnp.sum(block, axis=0)
        return carry

    lax.fori_loop(0, 4, step, 0)


def element_kernel(
    place_ref, couple_ref, fields_ref, scale_ref, diff_ref, interp_ref, lift_ref, links_ref,
    on_ref, off_ref, out_ref,
):
    core = place_ref[0]
    elements = fields_ref.shape[2]
    interp = interp_ref[...].reshape(96, 64)
    diff = diff_ref[...].reshape(192, 64)
    ghosts = jnp.concatenate([on_ref[...], off_ref[...]], axis=0).astype(F32)
    own, ghost = [], []
    grads = []
    for c in range(6):
        local = fields_ref[c]
        own.append(mm(interp, local, NN, HIGH))
        ghost.append(mm(interp, ghosts[:, 64 * c : 64 * c + 64], NT, HIGH))
        grads.append(mm(diff, local, NN, HIGH))
    surface = [jnp.zeros((64, elements), F32) for _ in range(6)]
    bound = iota((16, elements), 1) < 8
    for f in range(6):
        at, to = 16 * f, 16 * (f ^ 1)
        pool = jnp.concatenate([own[c][to : to + 16] for c in range(6)], axis=0)
        beyond = jnp.concatenate([ghost[c][to : to + 16] for c in range(6)], axis=0)
        links = links_ref[f : f + 1, :]
        inside = one_hot(iota((elements, elements), 0) == links, BF16)
        outer = links - elements
        outer = jnp.where(core == 0, outer ^ 16, outer)
        outside = one_hot(iota((32, elements), 0) == outer, BF16)
        high, low = halves(pool)
        ghost_high, ghost_low = halves(beyond)
        across = mm(high, inside) + mm(low, inside) + mm(ghost_high, outside) + mm(ghost_low, outside)
        jumps = []
        for c in range(6):
            there = across[16 * c : 16 * c + 16]
            if f == 5:
                there = jnp.where(bound, 0.0, there)
            jumps.append(there - own[c][at : at + 16])
        for c in range(6):
            flux = couple_ref[f, c, 0] * jumps[0]
            for k in range(1, 6):
                flux = flux + couple_ref[f, c, k] * jumps[k]
            surface[c] = surface[c] + mm(lift_ref[f], flux, NN, HIGH)

    def grad(r, c):
        return grads[c][64 * r : 64 * r + 64]

    curls = (
        grad(1, 5) - grad(2, 4),
        grad(2, 3) - grad(0, 5),
        grad(0, 4) - grad(1, 3),
        grad(2, 1) - grad(1, 2),
        grad(0, 2) - grad(2, 0),
        grad(1, 0) - grad(0, 1),
    )
    scale = scale_ref[...]
    for c in range(6):
        out_ref[c] = curls[c] * scale + surface[c]


def finish_kernel(
    bound_ref, couple_ref, parts_ref, rate_ref, lift_ref, time_ref, rate_out, field_out,
):
    total = parts_ref[0]
    for i in range(1, 8):
        total = total + parts_ref[i]
    total = total * jnp.float32(1.0 / np.sqrt(np.float32(512)))
    for t in range(8):
        field_out[pl.ds(t, 8, stride=8), :] = total[8 * t : 8 * t + 8]
    now = mm(time_ref[...], field_out[...], NN, HIGH)
    node = iota((16, 128), 1) % 16 == iota((16, 128), 0)
    by_node = jnp.where(node, now, 0.0)
    collect = one_hot(iota((128, 128), 0) // 16 == iota((128, 128), 1))
    lifted = mm(lift_ref[5], mm(by_node, collect, NN, HIGH), NN, HIGH)
    for c in range(6):
        factor = couple_ref[5, c, 0] * bound_ref[0]
        for k in range(1, 6):
            factor = factor + couple_ref[5, c, k] * bound_ref[k]
        rate_out[c, :, 0:128] = rate_ref[c, :, 0:128] + factor * lifted
        rate_out[c, :, 128:256] = rate_ref[c, :, 128:256]


def call(kernel, out, in_specs, scratch=(), **options):
    return pl.pallas_call(
        kernel,
        out_shape=out,
        in_specs=in_specs,
        out_specs=jax.tree.map(lambda _: VMEM, out),
        scratch_shapes=list(scratch),
        **options,
    )


def shaped(shape, dtype):
    return jax.ShapeDtypeStruct(shape, dtype)


def vmem(shape, dtype):
    return pltpu.VMEM(shape, dtype)


def per_device(
    fields, inv_jacobian, diff_matrix, face_interp, lift_matrix, flux_couple, neighbours,
    send_index, bound_coef, current_coef, time_interp, current_history, group_weight, projection,
    kernels, pair_dest, pair_count,
):
    place = jnp.stack([lax.axis_index("c"), lax.axis_index("xh"), lax.axis_index("z") % 2])
    place = place.astype(jnp.int32)
    message, on_chip, off_chip = call(
        pack_kernel,
        (vmem((8, ROWS, 128), BF16), vmem((16, 384), BF16), vmem((16, 384), BF16)),
        [SMEM] * 5 + [VMEM] * 6,
    )(
        place, send_index, pair_dest, pair_count, current_coef,
        fields, face_interp, current_history, group_weight, projection, kernels,
    )
    devices = 128
    beside = [(0, 1), (1, 0)]
    across = [(d, (d + 1 if d % 2 else d - 1) % devices) for d in range(devices)]
    off_chip = lax.ppermute(off_chip, AXES, across)
    on_chip = lax.ppermute(on_chip, "c", beside)
    got = lax.all_to_all(message, ("z", "xh"), 0, 0, tiled=True)
    got, off_chip, on_chip = lax.optimization_barrier((got, off_chip, on_chip))
    rate = call(
        element_kernel, shaped((6, 64, 256), F32), [SMEM] * 2 + [VMEM] * 8
    )(
        place, flux_couple, fields, inv_jacobian.reshape(1, -1), diff_matrix, face_interp,
        lift_matrix, neighbours, on_chip, off_chip,
    )
    keep, send = call(
        rays_kernel,
        (vmem((8, 256, 128), F32), vmem((8, 272, 128), BF16)),
        [SMEM, VMEM],
        (pltpu.VMEM((64, 1024), F32), pltpu.VMEM((32, 1024), F32), pltpu.VMEM((1024, 256), BF16)),
    )(place, got)
    came = lax.ppermute(send, "c", beside)
    partial = call(
        joined_kernel, vmem((8, 320, 128), BF16), [SMEM, VMEM, VMEM, VMEM]
    )(place, keep, send, came)
    partial = lax.all_to_all(partial, ("y", "xl"), 0, 0, tiled=True)
    incoming = call(
        translate_kernel,
        vmem((8, 256, 128), BF16),
        [VMEM],
        (pltpu.VMEM((2, 256, 128), F32), pltpu.VMEM((256, 128), F32)),
    )(partial)
    incoming = lax.all_to_all(incoming, ("y", "xl"), 0, 0, tiled=True)
    beyond = lax.ppermute(incoming, "c", beside)
    parts = call(
        image_kernel,
        vmem((8, 64, 128), F32),
        [SMEM, VMEM, VMEM, VMEM],
        (pltpu.VMEM((2048, 256), BF16), pltpu.VMEM((256, 256), BF16)),
    )(place, incoming, beyond, got)
    parts = lax.all_to_all(parts, ("z", "xh"), 0, 0, tiled=True)
    return call(
        finish_kernel,
        (shaped((6, 64, 256), F32), shaped((64, 128), F32)),
        [SMEM] * 2 + [VMEM] * 4,
    )(bound_coef, flux_couple, parts, rate, lift_matrix, time_interp.reshape(1, -1))


def solution(mesh):
    mesh = Mesh(np.asarray(mesh.devices).reshape(4, 4, 2, 2, 2), AXES)
    patch, level = ("y", "z", "xl"), ("xh", "c")
    placed = (
        P(None, None, AXES), P(AXES), P(), P(), P(), P(), P(None, AXES), P(None, AXES), P(), P(),
        P(), P(None, AXES), P(None, AXES), P(AXES, None), P(level, patch, None, None),
        P(level, patch, None), P(level, patch),
    )
    return jax.shard_map(
        per_device,
        mesh=mesh,
        in_specs=placed,
        out_specs=(P(None, None, AXES), P(None, AXES)),
        check_vma=False,
    )
```

```python
import functools

import jax
import jax.numpy as jnp
import numpy as np
from jax import lax
from jax.experimental import pallas as pl
from jax.experimental.pallas import tpu as pltpu
from jax.sharding import Mesh, PartitionSpec as P

F32 = jnp.float32
BF16 = jnp.bfloat16
HIGH = lax.Precision.HIGHEST
AXES = ("y", "z", "xl", "xh", "c")
VMEM = pl.BlockSpec(memory_space=pltpu.VMEM)
SMEM = pl.BlockSpec(memory_space=pltpu.SMEM)
ROW_C, ROW_W, ROW_T, ROWS = 256, 320, 352, 368
NN = (((1,), (0,)), ((), ()))
NT = (((1,), (1,)), ((), ()))
TN = (((0,), (0,)), ((), ()))


def iota(shape, dim):
    return lax.broadcasted_iota(jnp.int32, shape, dim)


def mm(a, b, dims=NN, precision=None):
    return lax.dot_general(a, b, dims, precision=precision, preferred_element_type=F32)


def one_hot(mask, dtype=F32):
    return jnp.where(mask, 1.0, 0.0).astype(dtype)


def halves(x):
    high = x.astype(BF16)
    return high, (x - high.astype(F32)).astype(BF16)


def lane_blocks_swapped(parts):
    parts = list(parts)
    shape = parts[0].shape
    block = iota(shape, 1) // 16
    for m in (4, 2, 1):
        upper = (block & m) != 0
        for j in range(8):
            if j & m:
                continue
            a, b = parts[j], parts[j + m]
            parts[j] = jnp.where(upper, pltpu.roll(b, 16 * m, 1), a)
            parts[j + m] = jnp.where(upper, b, pltpu.roll(a, 128 - 16 * m, 1))
    return parts


def pack_kernel(
    place_ref, send_ref, dest_ref, count_ref, coef_ref,
    fields_ref, interp_ref, history_ref, weight_ref, projection_ref, kernels_ref,
    message_ref, on_ref, off_ref,
):
    core = place_ref[0]
    elements = fields_ref.shape[2]
    flat = fields_ref[...].reshape(384, elements).astype(BF16)

    def picked(row):
        rows, lanes = iota((16, elements), 0), iota((16, elements), 1)
        wanted = jnp.zeros((16, elements), jnp.int32)
        for i in range(16):
            wanted = jnp.where(rows == i, send_ref[row, i], wanted)
        return mm(one_hot(lanes == wanted, BF16), flat, NT).astype(BF16)

    on_ref[...] = picked(1 - core)
    off_ref[...] = picked(core)
    mixed = jnp.zeros((64, 128), F32)
    for c in range(6):
        mixed = mixed + coef_ref[c] * fields_ref[c, :, 0:128]
    spread = one_hot(iota((128, 128), 1) // 16 == iota((128, 128), 0))
    chosen = one_hot(iota((16, 128), 1) % 16 == iota((16, 128), 0))
    by_element = mm(mixed, spread, NN, HIGH)
    by_node = mm(interp_ref[5], chosen, TN, HIGH)
    newest = jnp.sum(by_element * by_node, axis=0, keepdims=True)
    old = pltpu.roll(history_ref[...].astype(F32), 63, 0)
    currents = jnp.where(iota((64, 128), 0) == 63, newest, old).astype(BF16)
    lane_patch = iota((16, 128), 1) % 32
    wanted = jnp.full((16, 128), -1, jnp.int32)
    for j in range(16):
        to = jnp.where(j < count_ref[0, 0], dest_ref[0, 0, j], -1)
        wanted = jnp.where(iota((16, 128), 0) == j, to, wanted)
    spread_kernels = mm(kernels_ref[0, 0], one_hot(wanted == lane_patch, BF16), TN)
    group_of = iota((8, 128), 1) // 32
    table = []
    for h in range(2):
        rows = jnp.zeros((8, 128), F32)
        for a in range(4):
            at = 32 * h + 8 * a
            rows = jnp.where(group_of == a, spread_kernels[at : at + 8], rows)
        table.append(rows)
    table = jnp.concatenate(table, axis=0).astype(BF16)
    weights = []
    for level in range(4):
        pick = one_hot(iota((32, 128), 1) == 4 * iota((32, 128), 0) + level, BF16)
        weights.append(mm(pick, weight_ref[...]).astype(BF16))
    for i in range(8):
        z, xh = i // 2, i % 2
        at = 256 * (z // 2)
        message_ref[i, 0:128, :] = projection_ref[:, at : at + 128]
        message_ref[i, 128:256, :] = projection_ref[:, at + 128 : at + 256]
        message_ref[i, ROW_C : ROW_C + 64, :] = currents
        message_ref[i, ROW_W : ROW_W + 32, :] = weights[2 * xh + z % 2]
        message_ref[i, ROW_T:ROWS, :] = table


def rays_kernel(place_ref, got_ref, keep_ref, send_ref, c_ref, w_ref, p_ref):
    core, half = place_ref[0], place_ref[1]
    mine = pl.multiple_of(128 * core, 128)
    theirs = pl.multiple_of(128 * (1 - core), 128)
    for i in range(8):
        at = 128 * i
        c_ref[:, at : at + 128] = got_ref[i, ROW_C : ROW_C + 64, :].astype(F32)
        w_ref[:, at : at + 128] = got_ref[i, ROW_W : ROW_W + 32, :].astype(F32)
        p_ref[at : at + 128, 0:128] = got_ref[i, pl.ds(mine, 128), :]
        p_ref[at : at + 128, 128:256] = got_ref[i, pl.ds(theirs, 128), :]

    def step(high, carry):
        c = c_ref[pl.ds(pl.multiple_of(8 * high, 8), 8), :]
        w = w_ref[...]
        rows = [(c[t : t + 1] * w).astype(BF16) for t in range(8)]
        product = mm(jnp.concatenate(rows, axis=0), p_ref[...])
        at = pl.multiple_of(32 * high, 32)
        kept = lane_blocks_swapped([product[32 * t : 32 * t + 32, 0:128] for t in range(8)])
        sent = lane_blocks_swapped([product[32 * t : 32 * t + 32, 128:256] for t in range(8)])
        for r in range(8):
            keep_ref[r, pl.ds(at, 32), :] = kept[r]
            send_ref[r, pl.ds(at, 32), :] = sent[r].astype(BF16)
        return carry

    lax.fori_loop(0, 8, step, 0)
    for z in range(4):
        send_ref[z, 256:272, :] = got_ref[2 * z + half, ROW_T:ROWS, :]


def joined_kernel(place_ref, keep_ref, send_ref, came_ref, out_ref):
    has_tables = place_ref[0] == place_ref[2]
    tables = []
    for z in range(4):
        here, there = send_ref[z, 256:272, :], came_ref[z, 256:272, :]
        tables.append(jnp.where(has_tables, here.astype(F32), there.astype(F32)).astype(BF16))
    tables = jnp.concatenate(tables, axis=0)
    for r in range(8):
        out_ref[r, 0:256, :] = (keep_ref[r] + came_ref[r, 0:256, :].astype(F32)).astype(BF16)
        out_ref[r, 256:320, :] = tables


def translate_kernel(got_ref, out_ref, h_ref, s_ref):
    total = got_ref[0, 0:256, :].astype(F32)
    for r in range(1, 8):
        total = total + got_ref[r, 0:256, :].astype(F32)
    rays = total.astype(BF16).astype(F32)
    for r in range(8):
        y, xl = r // 2, r % 2
        for z in range(4):
            patch = 8 * y + 2 * z + xl
            tile = got_ref[r, 256 + 16 * z : 272 + 16 * z, :].astype(F32)
            for h in range(2):
                h_ref[h, pl.ds(patch, 8, stride=32), :] = tile[8 * h : 8 * h + 8]
    table = jnp.concatenate([h_ref[0], h_ref[1]], axis=1).astype(BF16)
    by_high = [rays[32 * t : 32 * t + 32] for t in range(8)]
    lane = iota((32, 128), 1)
    columns = []
    for t in range(8):
        rows = [by_high[t]]
        for b in range(1, 8):
            here = pltpu.roll(by_high[t], 16 * b, 1)
            before = pltpu.roll(by_high[t - 1], 16 * b, 1) if t > 0 else jnp.zeros((32, 128), F32)
            rows.append(jnp.where(lane < 16 * b, before, here))
        columns.append(jnp.concatenate(rows, axis=0).astype(BF16))
    lagged = [mm(table, column, TN) for column in columns]
    for t in range(8):
        incoming = lagged[t][0:32]
        for a in range(1, t + 1):
            incoming = incoming + lagged[t - a][32 * a : 32 * a + 32]
        s_ref[pl.ds(t, 32, stride=8), :] = incoming
    incoming = s_ref[...].astype(BF16)
    for r in range(8):
        out_ref[r] = incoming


def image_kernel(place_ref, here_ref, there_ref, got_ref, out_ref, rows_ref, p_ref):
    core = place_ref[0]
    mine = pl.multiple_of(128 * core, 128)
    theirs = pl.multiple_of(128 * (1 - core), 128)
    for h, ref in ((0, here_ref), (1, there_ref)):
        parts = lane_blocks_swapped([ref[r].astype(F32) for r in range(8)])
        for t in range(8):
            rows_ref[256 * t : 256 * t + 256, 128 * h : 128 * h + 128] = parts[t].astype(BF16)

    def step(i, carry):
        for s in range(2):
            p_ref[128 * s : 128 * s + 128, 0:128] = got_ref[2 * i + s, pl.ds(mine, 128), :]
            p_ref[128 * s : 128 * s + 128, 128:256] = got_ref[2 * i + s, pl.ds(theirs, 128), :]
        image = mm(rows_ref[...], p_ref[...], NT)
        for s in range(2):
            weight = got_ref[2 * i + s, ROW_W : ROW_W + 32, :].astype(F32)
            weight = jnp.broadcast_to(weight[:, None, :], (32, 8, 128))
            for t in range(8):
                block = image[256 * t : 256 * t + 256, 128 * s : 128 * s + 128]
                block = block.reshape(32, 8, 128) * weight
                out_ref[2 * i + s, 8 * t : 8 * t + 8, :] = jnp.sum(block, axis=0)
        return carry

    lax.fori_loop(0, 4, step, 0)


def element_kernel(
    place_ref, couple_ref, fields_ref, scale_ref, diff_ref, interp_ref, lift_ref, links_ref,
    on_ref, off_ref, out_ref, first_ref,
):
    core = place_ref[0]
    elements = fields_ref.shape[2]
    interp = interp_ref[...].reshape(96, 64)
    diff = diff_ref[...].reshape(192, 64)
    ghosts = jnp.concatenate([on_ref[...], off_ref[...]], axis=0).astype(F32)
    own, ghost = [], []
    grads = []
    for c in range(6):
        local = fields_ref[c]
        own.append(mm(interp, local, NN, HIGH))
        ghost.append(mm(interp, ghosts[:, 64 * c : 64 * c + 64], NT, HIGH))
        grads.append(mm(diff, local, NN, HIGH))
    surface = [jnp.zeros((64, elements), F32) for _ in range(6)]
    bound = iota((16, elements), 1) < 8
    for f in range(6):
        at, to = 16 * f, 16 * (f ^ 1)
        pool = jnp.concatenate([own[c][to : to + 16] for c in range(6)], axis=0)
        beyond = jnp.concatenate([ghost[c][to : to + 16] for c in range(6)], axis=0)
        links = links_ref[f : f + 1, :]
        inside = one_hot(iota((elements, elements), 0) == links, BF16)
        outer = links - elements
        outer = jnp.where(core == 0, outer ^ 16, outer)
        outside = one_hot(iota((32, elements), 0) == outer, BF16)
        high, low = halves(pool)
        ghost_high, ghost_low = halves(beyond)
        across = mm(high, inside) + mm(low, inside) + mm(ghost_high, outside) + mm(ghost_low, outside)
        jumps = []
        for c in range(6):
            there = across[16 * c : 16 * c + 16]
            if f == 5:
                there = jnp.where(bound, 0.0, there)
            jumps.append(there - own[c][at : at + 16])
        for c in range(6):
            flux = couple_ref[f, c, 0] * jumps[0]
            for k in range(1, 6):
                flux = flux + couple_ref[f, c, k] * jumps[k]
            surface[c] = surface[c] + mm(lift_ref[f], flux, TN, HIGH)

    def grad(r, c):
        return grads[c][64 * r : 64 * r + 64]

    curls = (
        grad(1, 5) - grad(2, 4),
        grad(2, 3) - grad(0, 5),
        grad(0, 4) - grad(1, 3),
        grad(2, 1) - grad(1, 2),
        grad(0, 2) - grad(2, 0),
        grad(1, 0) - grad(0, 1),
    )
    scale = scale_ref[...]
    for c in range(6):
        value = curls[c] * scale + surface[c]
        out_ref[c] = value
        first_ref[c] = value[:, 0:128]


def finish_kernel(
    bound_ref, couple_ref, parts_ref, first_ref, lift_ref, time_ref, rate_ref, rate_out,
    field_out, tile_ref, sem,
):
    del rate_ref
    total = parts_ref[0]
    for i in range(1, 8):
        total = total + parts_ref[i]
    total = total * jnp.float32(1.0 / np.sqrt(np.float32(512)))
    for t in range(8):
        field_out[pl.ds(t, 8, stride=8), :] = total[8 * t : 8 * t + 8]
    now = mm(time_ref[...], field_out[...], NN, HIGH)
    node = iota((16, 128), 1) % 16 == iota((16, 128), 0)
    by_node = jnp.where(node, now, 0.0)
    collect = one_hot(iota((128, 128), 0) // 16 == iota((128, 128), 1))
    lifted = mm(lift_ref[5], mm(by_node, collect, NN, HIGH), TN, HIGH)
    for c in range(6):
        factor = couple_ref[5, c, 0] * bound_ref[0]
        for k in range(1, 6):
            factor = factor + couple_ref[5, c, k] * bound_ref[k]
        tile_ref[c] = first_ref[c] + factor * lifted
    copy = pltpu.make_async_copy(tile_ref, rate_out.at[:, :, pl.ds(0, 128)], sem)
    copy.start()
    copy.wait()


def call(kernel, out, in_specs, scratch=(), out_specs=None, **options):
    run = pl.pallas_call(
        kernel,
        out_shape=out,
        in_specs=in_specs,
        out_specs=jax.tree.map(lambda _: VMEM, out) if out_specs is None else out_specs,
        scratch_shapes=list(scratch),
        **options,
    )
    return run


def held(x):
    return pltpu.with_memory_space_constraint(x, pltpu.VMEM)


def shaped(shape, dtype):
    return jax.ShapeDtypeStruct(shape, dtype)


def vmem(shape, dtype):
    return pltpu.VMEM(shape, dtype)


def per_device(
    fields, inv_jacobian, diff_matrix, face_interp, lift_matrix, flux_couple, neighbours,
    send_index, bound_coef, current_coef, time_interp, current_history, group_weight, projection,
    kernels, pair_dest, pair_count,
):
    place = jnp.stack([lax.axis_index("c"), lax.axis_index("xh"), lax.axis_index("z") % 2])
    place = place.astype(jnp.int32)
    message, on_chip, off_chip = call(
        pack_kernel,
        (vmem((8, ROWS, 128), BF16), vmem((16, 384), BF16), vmem((16, 384), BF16)),
        [SMEM] * 5 + [VMEM] * 6,
    )(
        place, send_index, pair_dest, pair_count, current_coef,
        fields, face_interp, current_history, group_weight, projection, kernels,
    )
    devices = 128
    beside = [(0, 1), (1, 0)]
    across = [(d, (d + 1 if d % 2 else d - 1) % devices) for d in range(devices)]
    off_chip = lax.ppermute(off_chip, AXES, across)
    on_chip = lax.ppermute(on_chip, "c", beside)
    got = lax.all_to_all(message, ("z", "xh"), 0, 0, tiled=True)
    got, off_chip, on_chip = lax.optimization_barrier((got, off_chip, on_chip))
    got = held(got)
    keep, send = call(
        rays_kernel,
        (vmem((8, 256, 128), F32), vmem((8, 272, 128), BF16)),
        [SMEM, VMEM],
        (pltpu.VMEM((64, 1024), F32), pltpu.VMEM((32, 1024), F32), pltpu.VMEM((1024, 256), BF16)),
    )(place, got)
    came = lax.ppermute(send, "c", beside)
    partial = call(
        joined_kernel, vmem((8, 320, 128), BF16), [SMEM, VMEM, VMEM, VMEM]
    )(place, held(keep), held(send), held(came))
    partial, on_chip, off_chip = lax.optimization_barrier((partial, on_chip, off_chip))
    lift = lift_matrix.transpose(0, 2, 1)
    rate, first = call(
        element_kernel,
        (shaped((6, 64, 256), F32), vmem((6, 64, 128), F32)),
        [SMEM] * 2 + [VMEM] * 8,
    )(
        place, flux_couple, fields, inv_jacobian.reshape(1, -1), diff_matrix, face_interp,
        lift, neighbours, held(on_chip), held(off_chip),
    )
    partial = lax.all_to_all(partial, ("y", "xl"), 0, 0, tiled=True)
    partial, rate, first = lax.optimization_barrier((partial, rate, first))
    incoming = call(
        translate_kernel,
        vmem((8, 256, 128), BF16),
        [VMEM],
        (pltpu.VMEM((2, 256, 128), F32), pltpu.VMEM((256, 128), F32)),
    )(held(partial))
    incoming = lax.all_to_all(incoming, ("y", "xl"), 0, 0, tiled=True)
    beyond = lax.ppermute(incoming, "c", beside)
    parts = call(
        image_kernel,
        vmem((8, 64, 128), F32),
        [SMEM, VMEM, VMEM, VMEM],
        (pltpu.VMEM((2048, 256), BF16), pltpu.VMEM((256, 256), BF16)),
    )(place, held(incoming), held(beyond), got)
    parts = lax.all_to_all(parts, ("z", "xh"), 0, 0, tiled=True)
    anywhere = pl.BlockSpec(memory_space=pl.ANY)
    return call(
        finish_kernel,
        (shaped((6, 64, 256), F32), shaped((64, 128), F32)),
        [SMEM] * 2 + [VMEM] * 4 + [anywhere],
        (pltpu.VMEM((6, 64, 128), F32), pltpu.SemaphoreType.DMA),
        out_specs=(anywhere, VMEM),
        input_output_aliases={6: 0},
    )(bound_coef, flux_couple, held(parts), held(first), lift, time_interp.reshape(1, -1), rate)


def solution(mesh):
    mesh = Mesh(np.asarray(mesh.devices).reshape(4, 4, 2, 2, 2), AXES)
    patch, level = ("y", "z", "xl"), ("xh", "c")
    placed = (
        P(None, None, AXES), P(AXES), P(), P(), P(), P(), P(None, AXES), P(None, AXES), P(), P(),
        P(), P(None, AXES), P(None, AXES), P(AXES, None), P(level, patch, None, None),
        P(level, patch, None), P(level, patch),
    )
    return jax.shard_map(
        per_device,
        mesh=mesh,
        in_specs=placed,
        out_specs=(P(None, None, AXES), P(None, AXES)),
        check_vma=False,
    )
```

```python
import functools

import jax
import jax.numpy as jnp
import numpy as np
from jax import lax
from jax.experimental import pallas as pl
from jax.experimental.pallas import tpu as pltpu
from jax.sharding import Mesh, PartitionSpec as P

F32 = jnp.float32
BF16 = jnp.bfloat16
HIGH = lax.Precision.HIGHEST
AXES = ("y", "z", "xl", "xh", "c")
VMEM = pl.BlockSpec(memory_space=pltpu.VMEM)
SMEM = pl.BlockSpec(memory_space=pltpu.SMEM)
ROW_C, ROW_W, ROW_T, ROWS = 256, 320, 352, 368
NN = (((1,), (0,)), ((), ()))
NT = (((1,), (1,)), ((), ()))
TN = (((0,), (0,)), ((), ()))


def iota(shape, dim):
    return lax.broadcasted_iota(jnp.int32, shape, dim)


def mm(a, b, dims=NN, precision=None):
    return lax.dot_general(a, b, dims, precision=precision, preferred_element_type=F32)


def one_hot(mask, dtype=F32):
    return jnp.where(mask, 1.0, 0.0).astype(dtype)


def halves(x):
    high = x.astype(BF16)
    return high, (x - high.astype(F32)).astype(BF16)


def lane_blocks_swapped(parts):
    parts = list(parts)
    shape = parts[0].shape
    block = iota(shape, 1) // 16
    for m in (4, 2, 1):
        upper = (block & m) != 0
        for j in range(8):
            if j & m:
                continue
            a, b = parts[j], parts[j + m]
            parts[j] = jnp.where(upper, pltpu.roll(b, 16 * m, 1), a)
            parts[j + m] = jnp.where(upper, b, pltpu.roll(a, 128 - 16 * m, 1))
    return parts


def pack_kernel(
    place_ref, send_ref, dest_ref, count_ref, coef_ref,
    fields_ref, interp_ref, history_ref, weight_ref, projection_ref, kernels_ref,
    message_ref, on_ref, off_ref,
):
    core = place_ref[0]
    elements = fields_ref.shape[2]
    flat = fields_ref[...].reshape(384, elements).astype(BF16)

    def picked(row):
        rows, lanes = iota((16, elements), 0), iota((16, elements), 1)
        wanted = jnp.zeros((16, elements), jnp.int32)
        for i in range(16):
            wanted = jnp.where(rows == i, send_ref[row, i], wanted)
        return mm(one_hot(lanes == wanted, BF16), flat, NT).astype(BF16)

    on_ref[...] = picked(1 - core)
    off_ref[...] = picked(core)
    mixed = jnp.zeros((64, 128), F32)
    for c in range(6):
        mixed = mixed + coef_ref[c] * fields_ref[c, :, 0:128]
    spread = one_hot(iota((128, 128), 1) // 16 == iota((128, 128), 0))
    chosen = one_hot(iota((16, 128), 1) % 16 == iota((16, 128), 0))
    by_element = mm(mixed, spread, NN, HIGH)
    by_node = mm(interp_ref[5], chosen, TN, HIGH)
    newest = jnp.sum(by_element * by_node, axis=0, keepdims=True)
    old = pltpu.roll(history_ref[...].astype(F32), 63, 0)
    currents = jnp.where(iota((64, 128), 0) == 63, newest, old).astype(BF16)
    lane_patch = iota((16, 128), 1) % 32
    wanted = jnp.full((16, 128), -1, jnp.int32)
    for j in range(16):
        to = jnp.where(j < count_ref[0, 0], dest_ref[0, 0, j], -1)
        wanted = jnp.where(iota((16, 128), 0) == j, to, wanted)
    spread_kernels = mm(kernels_ref[0, 0], one_hot(wanted == lane_patch, BF16), TN)
    group_of = iota((8, 128), 1) // 32
    table = []
    for h in range(2):
        rows = jnp.zeros((8, 128), F32)
        for a in range(4):
            at = 32 * h + 8 * a
            rows = jnp.where(group_of == a, spread_kernels[at : at + 8], rows)
        table.append(rows)
    table = jnp.concatenate(table, axis=0).astype(BF16)
    weights = []
    for level in range(4):
        pick = one_hot(iota((32, 128), 1) == 4 * iota((32, 128), 0) + level, BF16)
        weights.append(mm(pick, weight_ref[...]).astype(BF16))
    for i in range(8):
        z, xh = i // 2, i % 2
        at = 256 * (z // 2)
        message_ref[i, 0:128, :] = projection_ref[:, at : at + 128]
        message_ref[i, 128:256, :] = projection_ref[:, at + 128 : at + 256]
        message_ref[i, ROW_C : ROW_C + 64, :] = currents
        message_ref[i, ROW_W : ROW_W + 32, :] = weights[2 * xh + z % 2]
        message_ref[i, ROW_T:ROWS, :] = table


def rays_kernel(
    place_ref, got_ref, on_ref, keep_ref, send_ref, saved_ref, c_ref, w_ref, p_ref, sem,
):
    save = pltpu.make_async_copy(got_ref, saved_ref, sem)
    save.start()
    core, half = place_ref[0], place_ref[1]
    mine = pl.multiple_of(128 * core, 128)
    theirs = pl.multiple_of(128 * (1 - core), 128)
    for i in range(8):
        at = 128 * i
        c_ref[:, at : at + 128] = got_ref[i, ROW_C : ROW_C + 64, :].astype(F32)
        w_ref[:, at : at + 128] = got_ref[i, ROW_W : ROW_W + 32, :].astype(F32)
        p_ref[at : at + 128, 0:128] = got_ref[i, pl.ds(mine, 128), :]
        p_ref[at : at + 128, 128:256] = got_ref[i, pl.ds(theirs, 128), :]

    def step(pair, carry):
        c = c_ref[pl.ds(pl.multiple_of(16 * pair, 16), 16), :]
        w = w_ref[...]
        rows = [(c[t : t + 1] * w).astype(BF16) for t in range(16)]
        product = mm(jnp.concatenate(rows, axis=0), p_ref[...])
        for s in range(2):
            at = pl.multiple_of(64 * pair + 32 * s, 32)
            part = [product[256 * s + 32 * t : 256 * s + 32 * t + 32] for t in range(8)]
            kept = lane_blocks_swapped([x[:, 0:128] for x in part])
            sent = lane_blocks_swapped([x[:, 128:256] for x in part])
            for r in range(8):
                keep_ref[r, pl.ds(at, 32), :] = kept[r]
                send_ref[r, pl.ds(at, 32), :] = sent[r].astype(BF16)
        return carry

    lax.fori_loop(0, 4, step, 0)
    for z in range(4):
        send_ref[z, 256:272, :] = got_ref[2 * z + half, ROW_T:ROWS, :]
    for i in range(3):
        send_ref[4 + i, 256:272, :] = on_ref[:, 128 * i : 128 * i + 128]
    save.wait()


def joined_kernel(place_ref, keep_ref, send_ref, came_ref, out_ref, on_ref):
    has_tables = place_ref[0] == place_ref[2]
    tables = []
    for z in range(4):
        here, there = send_ref[z, 256:272, :], came_ref[z, 256:272, :]
        tables.append(jnp.where(has_tables, here.astype(F32), there.astype(F32)).astype(BF16))
    tables = jnp.concatenate(tables, axis=0)
    for r in range(8):
        out_ref[r, 0:256, :] = (keep_ref[r] + came_ref[r, 0:256, :].astype(F32)).astype(BF16)
        out_ref[r, 256:320, :] = tables
    for i in range(3):
        on_ref[:, 128 * i : 128 * i + 128] = came_ref[4 + i, 256:272, :]


def translate_kernel(got_ref, out_ref, h_ref, s_ref):
    total = got_ref[0, 0:256, :].astype(F32)
    for r in range(1, 8):
        total = total + got_ref[r, 0:256, :].astype(F32)
    rays = total.astype(BF16).astype(F32)
    for r in range(8):
        y, xl = r // 2, r % 2
        for z in range(4):
            patch = 8 * y + 2 * z + xl
            tile = got_ref[r, 256 + 16 * z : 272 + 16 * z, :].astype(F32)
            for h in range(2):
                h_ref[h, pl.ds(patch, 8, stride=32), :] = tile[8 * h : 8 * h + 8]
    table = jnp.concatenate([h_ref[0], h_ref[1]], axis=1).astype(BF16)
    by_high = [rays[32 * t : 32 * t + 32] for t in range(8)]
    lane = iota((32, 128), 1)
    columns = []
    for t in range(8):
        rows = [by_high[t]]
        for b in range(1, 8):
            here = pltpu.roll(by_high[t], 16 * b, 1)
            before = pltpu.roll(by_high[t - 1], 16 * b, 1) if t > 0 else jnp.zeros((32, 128), F32)
            rows.append(jnp.where(lane < 16 * b, before, here))
        columns.append(jnp.concatenate(rows, axis=0).astype(BF16))
    lagged = [mm(table, column, TN) for column in columns]
    for t in range(8):
        incoming = lagged[t][0:32]
        for a in range(1, t + 1):
            incoming = incoming + lagged[t - a][32 * a : 32 * a + 32]
        s_ref[pl.ds(t, 32, stride=8), :] = incoming
    incoming = s_ref[...].astype(BF16)
    for r in range(8):
        out_ref[r] = incoming


def image_kernel(
    place_ref, here_ref, there_ref, saved_ref, out_ref, rows_ref, p_ref, got_ref, sem,
):
    load = pltpu.make_async_copy(saved_ref, got_ref, sem)
    load.start()
    core = place_ref[0]
    mine = pl.multiple_of(128 * core, 128)
    theirs = pl.multiple_of(128 * (1 - core), 128)
    for h, ref in ((0, here_ref), (1, there_ref)):
        parts = lane_blocks_swapped([ref[r].astype(F32) for r in range(8)])
        for t in range(8):
            rows_ref[256 * t : 256 * t + 256, 128 * h : 128 * h + 128] = parts[t].astype(BF16)
    load.wait()

    def step(i, carry):
        for s in range(2):
            p_ref[128 * s : 128 * s + 128, 0:128] = got_ref[2 * i + s, pl.ds(mine, 128), :]
            p_ref[128 * s : 128 * s + 128, 128:256] = got_ref[2 * i + s, pl.ds(theirs, 128), :]
        image = mm(rows_ref[...], p_ref[...], NT)
        for s in range(2):
            weight = got_ref[2 * i + s, ROW_W : ROW_W + 32, :].astype(F32)
            weight = jnp.broadcast_to(weight[:, None, :], (32, 8, 128))
            for t in range(8):
                block = image[256 * t : 256 * t + 256, 128 * s : 128 * s + 128]
                block = block.reshape(32, 8, 128) * weight
                out_ref[2 * i + s, 8 * t : 8 * t + 8, :] = jnp.sum(block, axis=0)
        return carry

    lax.fori_loop(0, 4, step, 0)


def element_kernel(
    place_ref, couple_ref, bound_ref, fields_ref, scale_ref, diff_ref, interp_ref, lift_ref,
    links_ref, time_ref, on_ref, off_ref, out_ref, first_ref, nodes_ref, times_ref, factor_ref,
):
    core = place_ref[0]
    elements = fields_ref.shape[2]
    both = jnp.concatenate([interp_ref[...].reshape(96, 64), diff_ref[...].reshape(192, 64)], axis=0)
    both_high, both_low = halves(both)
    both = jnp.concatenate([both_high, both_high, both_low], axis=1)
    ghosts = jnp.concatenate([on_ref[...], off_ref[...]], axis=0)
    own, ghost, grads = [], [], []
    for c in range(6):
        high, low = halves(fields_ref[c])
        product = mm(both, jnp.concatenate([high, low, high], axis=0))
        own.append(product[0:96])
        grads.append(product[96:288])
        beyond = ghosts[:, 64 * c : 64 * c + 64]
        ghost.append(mm(both_high[0:96], beyond, NT) + mm(both_low[0:96], beyond, NT))
    fluxes = [[] for _ in range(6)]
    bound = iota((16, elements), 1) < 8
    for f in range(6):
        at, to = 16 * f, 16 * (f ^ 1)
        pool = jnp.concatenate([own[c][to : to + 16] for c in range(6)], axis=0)
        beyond = jnp.concatenate([ghost[c][to : to + 16] for c in range(6)], axis=0)
        links = links_ref[f : f + 1, :]
        inside = one_hot(iota((elements, elements), 0) == links, BF16)
        outer = links - elements
        outer = jnp.where(core == 0, outer ^ 16, outer)
        outside = one_hot(iota((32, elements), 0) == outer, BF16)
        across = mm(jnp.concatenate(halves(pool), axis=0), inside)
        across = across + mm(jnp.concatenate(halves(beyond), axis=0), outside)
        across = across[0:96] + across[96:192]
        jumps = []
        for c in range(6):
            there = across[16 * c : 16 * c + 16]
            if f == 5:
                there = jnp.where(bound, 0.0, there)
            jumps.append(there - own[c][at : at + 16])
        for c in range(6):
            flux = couple_ref[f, c, 0] * jumps[0]
            for k in range(1, 6):
                flux = flux + couple_ref[f, c, k] * jumps[k]
            fluxes[c].append(flux)
    lift = lift_ref[...].reshape(96, 64)
    lift_high, lift_low = halves(lift)

    def grad(r, c):
        return grads[c][64 * r : 64 * r + 64]

    curls = (
        grad(1, 5) - grad(2, 4),
        grad(2, 3) - grad(0, 5),
        grad(0, 4) - grad(1, 3),
        grad(2, 1) - grad(1, 2),
        grad(0, 2) - grad(2, 0),
        grad(1, 0) - grad(0, 1),
    )
    scale = scale_ref[...]
    for c in range(6):
        high, low = halves(jnp.concatenate(fluxes[c], axis=0))
        surface = mm(lift_high, high, TN) + mm(lift_high, low, TN) + mm(lift_low, high, TN)
        value = curls[c] * scale + surface
        out_ref[c] = value
        first_ref[c] = value[:, 0:128]
    chosen = one_hot(iota((16, 128), 1) % 16 == iota((16, 128), 0))
    nodes_ref[...] = mm(lift_ref[5], chosen, TN, HIGH)
    row, sample = iota((64, 64), 0), iota((64, 64), 1)
    times = jnp.where(row % 8 * 8 + row // 8 == sample, time_ref[...], 0.0)
    times_ref[...] = jnp.broadcast_to(jnp.sum(times, axis=1, keepdims=True), (64, 128))
    for c in range(6):
        factor = couple_ref[5, c, 0] * bound_ref[0]
        for k in range(1, 6):
            factor = factor + couple_ref[5, c, k] * bound_ref[k]
        factor_ref[c] = jnp.full((8, 128), factor, F32)


def finish_kernel(
    parts_ref, first_ref, nodes_ref, times_ref, factor_ref, rate_ref, rate_out, field_out,
    tile_ref, sem,
):
    del rate_ref
    total = parts_ref[0]
    for i in range(1, 8):
        total = total + parts_ref[i]
    total = total * jnp.float32(1.0 / np.sqrt(np.float32(512)))
    for t in range(8):
        field_out[pl.ds(t, 8, stride=8), :] = total[8 * t : 8 * t + 8]
    now = jnp.sum(times_ref[...] * total, axis=0, keepdims=True)
    collect = one_hot(iota((256, 128), 0) % 128 // 16 == iota((256, 128), 1), BF16)
    lifted = mm(jnp.concatenate(halves(nodes_ref[...] * now), axis=1), collect)
    for c in range(6):
        tile_ref[c] = first_ref[c] + factor_ref[c, 0:1, :] * lifted
    copy = pltpu.make_async_copy(tile_ref, rate_out.at[:, :, pl.ds(0, 128)], sem)
    copy.start()
    copy.wait()


def call(kernel, out, in_specs, scratch=(), out_specs=None, **options):
    run = pl.pallas_call(
        kernel,
        out_shape=out,
        in_specs=in_specs,
        out_specs=jax.tree.map(lambda _: VMEM, out) if out_specs is None else out_specs,
        scratch_shapes=list(scratch),
        compiler_params=pltpu.CompilerParams(vmem_limit_bytes=24 << 20),
        **options,
    )
    return run


def held(x):
    return pltpu.with_memory_space_constraint(x, pltpu.VMEM)


def shaped(shape, dtype):
    return jax.ShapeDtypeStruct(shape, dtype)


def vmem(shape, dtype):
    return pltpu.VMEM(shape, dtype)


def per_device(
    fields, inv_jacobian, diff_matrix, face_interp, lift_matrix, flux_couple, neighbours,
    send_index, bound_coef, current_coef, time_interp, current_history, group_weight, projection,
    kernels, pair_dest, pair_count,
):
    place = jnp.stack([lax.axis_index("c"), lax.axis_index("xh"), lax.axis_index("z") % 2])
    place = place.astype(jnp.int32)
    message, on_chip, off_chip = call(
        pack_kernel,
        (vmem((8, ROWS, 128), BF16), vmem((16, 384), BF16), vmem((16, 384), BF16)),
        [SMEM] * 5 + [VMEM] * 6,
    )(
        place, send_index, pair_dest, pair_count, current_coef,
        fields, face_interp, current_history, group_weight, projection, kernels,
    )
    devices = 128
    beside = [(0, 1), (1, 0)]
    across = [(d, (d + 1 if d % 2 else d - 1) % devices) for d in range(devices)]
    anywhere = pl.BlockSpec(memory_space=pl.ANY)
    got = lax.all_to_all(message, ("z", "xh"), 0, 0, tiled=True)
    keep, send, saved = call(
        rays_kernel,
        (
            vmem((8, 256, 128), F32), vmem((8, 272, 128), BF16),
            pltpu.HBM((8, ROWS, 128), BF16),
        ),
        [SMEM, VMEM, VMEM],
        (
            pltpu.VMEM((64, 1024), F32), pltpu.VMEM((32, 1024), F32),
            pltpu.VMEM((1024, 256), BF16), pltpu.SemaphoreType.DMA,
        ),
        out_specs=(VMEM, VMEM, pl.BlockSpec(memory_space=pltpu.HBM)),
    )(place, held(got), held(on_chip))
    send, off_chip = lax.optimization_barrier((send, off_chip))
    came = lax.ppermute(send, "c", beside)
    off_chip = lax.ppermute(off_chip, AXES, across)
    partial, on_chip = call(
        joined_kernel,
        (vmem((8, 320, 128), BF16), vmem((16, 384), BF16)),
        [SMEM, VMEM, VMEM, VMEM],
    )(place, held(keep), held(send), held(came))
    partial = lax.all_to_all(partial, ("y", "xl"), 0, 0, tiled=True)
    incoming = call(
        translate_kernel,
        vmem((8, 256, 128), BF16),
        [VMEM],
        (pltpu.VMEM((2, 256, 128), F32), pltpu.VMEM((256, 128), F32)),
    )(held(partial))
    incoming = lax.all_to_all(incoming, ("y", "xl"), 0, 0, tiled=True)
    beyond = lax.ppermute(incoming, "c", beside)
    parts = call(
        image_kernel,
        vmem((8, 64, 128), F32),
        [SMEM, VMEM, VMEM, pl.BlockSpec(memory_space=pltpu.HBM)],
        (
            pltpu.VMEM((2048, 256), BF16), pltpu.VMEM((256, 256), BF16),
            pltpu.VMEM((8, ROWS, 128), BF16), pltpu.SemaphoreType.DMA,
        ),
    )(place, held(incoming), held(beyond), saved)
    parts, on_chip, off_chip = lax.optimization_barrier((parts, on_chip, off_chip))
    rate, first, nodes, times, factor = call(
        element_kernel,
        (
            shaped((6, 64, 256), F32), vmem((6, 64, 128), F32), vmem((64, 128), F32),
            vmem((64, 128), F32), vmem((6, 8, 128), F32),
        ),
        [SMEM] * 3 + [VMEM] * 9,
    )(
        place, flux_couple, bound_coef, fields, inv_jacobian.reshape(1, -1), diff_matrix,
        face_interp, lift_matrix.transpose(0, 2, 1), neighbours, time_interp.reshape(1, -1),
        held(on_chip), held(off_chip),
    )
    parts = lax.all_to_all(parts, ("z", "xh"), 0, 0, tiled=True)
    return call(
        finish_kernel,
        (shaped((6, 64, 256), F32), shaped((64, 128), F32)),
        [VMEM] * 5 + [anywhere],
        (pltpu.VMEM((6, 64, 128), F32), pltpu.SemaphoreType.DMA),
        out_specs=(anywhere, VMEM),
        input_output_aliases={5: 0},
    )(held(parts), held(first), held(nodes), held(times), held(factor), rate)


def solution(mesh):
    mesh = Mesh(np.asarray(mesh.devices).reshape(4, 4, 2, 2, 2), AXES)
    patch, level = ("y", "z", "xl"), ("xh", "c")
    placed = (
        P(None, None, AXES), P(AXES), P(), P(), P(), P(), P(None, AXES), P(None, AXES), P(), P(),
        P(), P(None, AXES), P(None, AXES), P(AXES, None), P(level, patch, None, None),
        P(level, patch, None), P(level, patch),
    )
    return jax.shard_map(
        per_device,
        mesh=mesh,
        in_specs=placed,
        out_specs=(P(None, None, AXES), P(None, AXES)),
        check_vma=False,
    )
```

```python
import jax
import jax.numpy as jnp
import numpy as np
from jax import lax
from jax.experimental import pallas as pl
from jax.experimental.pallas import tpu as pltpu
from jax.sharding import Mesh, PartitionSpec as P


F32 = jnp.float32
BF16 = jnp.bfloat16
HIGH = lax.Precision.HIGHEST
AXES = ("y", "z", "xl", "xh", "c")
VMEM = pl.BlockSpec(memory_space=pltpu.VMEM)
SMEM = pl.BlockSpec(memory_space=pltpu.SMEM)
ROW_C, ROW_W, ROW_T, ROWS = 256, 320, 352, 368
NN = (((1,), (0,)), ((), ()))
NT = (((1,), (1,)), ((), ()))
TN = (((0,), (0,)), ((), ()))


def iota(shape, dim):
    return lax.broadcasted_iota(jnp.int32, shape, dim)


def mm(a, b, dims=NN, precision=None):
    return lax.dot_general(a, b, dims, precision=precision, preferred_element_type=F32)


def one_hot(mask, dtype=F32):
    return jnp.where(mask, 1.0, 0.0).astype(dtype)


def halves(x):
    high = x.astype(BF16)
    return high, (x - high.astype(F32)).astype(BF16)


def lane_blocks_swapped(parts):
    parts = list(parts)
    shape = parts[0].shape
    block = iota(shape, 1) // 16
    for m in (4, 2, 1):
        upper = (block & m) != 0
        for j in range(8):
            if j & m:
                continue
            a, b = parts[j], parts[j + m]
            parts[j] = jnp.where(upper, pltpu.roll(b, 16 * m, 1), a)
            parts[j + m] = jnp.where(upper, b, pltpu.roll(a, 128 - 16 * m, 1))
    return parts


def pack_kernel(
    send_ref, dest_ref, count_ref, coef_ref,
    fields_ref, interp_ref, history_ref, weight_ref, projection_ref, kernels_ref,
    message_ref, on_ref, off_ref,
):
    core = lax.axis_index("c")
    elements = fields_ref.shape[2]
    flat = fields_ref[...].reshape(384, elements).astype(BF16)

    def picked(row):
        rows, lanes = iota((16, elements), 0), iota((16, elements), 1)
        wanted = jnp.zeros((16, elements), jnp.int32)
        for i in range(16):
            wanted = jnp.where(rows == i, send_ref[row, i], wanted)
        return mm(one_hot(lanes == wanted, BF16), flat, NT).astype(BF16)

    on_ref[...] = picked(1 - core)
    off_ref[...] = picked(core)
    mixed = jnp.zeros((64, 128), F32)
    for c in range(6):
        mixed = mixed + coef_ref[c] * fields_ref[c, :, 0:128]
    spread = one_hot(iota((128, 128), 1) // 16 == iota((128, 128), 0))
    chosen = one_hot(iota((16, 128), 1) % 16 == iota((16, 128), 0))
    by_element = mm(mixed, spread, NN, HIGH)
    by_node = mm(interp_ref[5], chosen, TN, HIGH)
    newest = jnp.sum(by_element * by_node, axis=0, keepdims=True)
    old = pltpu.roll(history_ref[...].astype(F32), 63, 0)
    currents = jnp.where(iota((64, 128), 0) == 63, newest, old).astype(BF16)
    lane_patch = iota((16, 128), 1) % 32
    wanted = jnp.full((16, 128), -1, jnp.int32)
    for j in range(16):
        to = jnp.where(j < count_ref[0, 0], dest_ref[0, 0, j], -1)
        wanted = jnp.where(iota((16, 128), 0) == j, to, wanted)
    spread_kernels = mm(kernels_ref[0, 0], one_hot(wanted == lane_patch, BF16), TN)
    group_of = iota((8, 128), 1) // 32
    table = []
    for h in range(2):
        rows = jnp.zeros((8, 128), F32)
        for a in range(4):
            at = 32 * h + 8 * a
            rows = jnp.where(group_of == a, spread_kernels[at : at + 8], rows)
        table.append(rows)
    table = jnp.concatenate(table, axis=0).astype(BF16)
    weights = []
    for level in range(4):
        pick = one_hot(iota((32, 128), 1) == 4 * iota((32, 128), 0) + level, BF16)
        weights.append(mm(pick, weight_ref[...]).astype(BF16))
    for i in range(8):
        z, xh = i // 2, i % 2
        at = 256 * (z // 2)
        message_ref[i, 0:128, :] = projection_ref[:, at : at + 128]
        message_ref[i, 128:256, :] = projection_ref[:, at + 128 : at + 256]
        message_ref[i, ROW_C : ROW_C + 64, :] = currents
        message_ref[i, ROW_W : ROW_W + 32, :] = weights[2 * xh + z % 2]
        message_ref[i, ROW_T:ROWS, :] = table


def rays_kernel(got_ref, on_ref, keep_ref, send_ref, c_ref, w_ref, p_ref):
    core, half = lax.axis_index("c"), lax.axis_index("xh")
    mine = pl.multiple_of(128 * core, 128)
    theirs = pl.multiple_of(128 * (1 - core), 128)
    for i in range(8):
        at = 128 * i
        c_ref[:, at : at + 128] = got_ref[i, ROW_C : ROW_C + 64, :].astype(F32)
        w_ref[:, at : at + 128] = got_ref[i, ROW_W : ROW_W + 32, :].astype(F32)
        p_ref[at : at + 128, 0:128] = got_ref[i, pl.ds(mine, 128), :]
        p_ref[at : at + 128, 128:256] = got_ref[i, pl.ds(theirs, 128), :]

    def step(pair, carry):
        c = c_ref[pl.ds(pl.multiple_of(16 * pair, 16), 16), :]
        w = w_ref[...]
        rows = [(c[t : t + 1] * w).astype(BF16) for t in range(16)]
        product = mm(jnp.concatenate(rows, axis=0), p_ref[...])
        for s in range(2):
            at = pl.multiple_of(64 * pair + 32 * s, 32)
            part = [product[256 * s + 32 * t : 256 * s + 32 * t + 32] for t in range(8)]
            kept = lane_blocks_swapped([x[:, 0:128] for x in part])
            sent = lane_blocks_swapped([x[:, 128:256] for x in part])
            for r in range(8):
                keep_ref[r, pl.ds(at, 32), :] = kept[r]
                send_ref[r, pl.ds(at, 32), :] = sent[r].astype(BF16)
        return carry

    lax.fori_loop(0, 4, step, 0)
    for z in range(4):
        send_ref[z, 256:272, :] = got_ref[2 * z + half, ROW_T:ROWS, :]
    for i in range(3):
        send_ref[4 + i, 256:272, :] = on_ref[:, 128 * i : 128 * i + 128]


def joined_kernel(keep_ref, send_ref, came_ref, out_ref, on_ref):
    has_tables = lax.axis_index("c") == lax.axis_index("z") % 2
    tables = []
    for z in range(4):
        here, there = send_ref[z, 256:272, :], came_ref[z, 256:272, :]
        tables.append(jnp.where(has_tables, here.astype(F32), there.astype(F32)).astype(BF16))
    tables = jnp.concatenate(tables, axis=0)
    for r in range(8):
        out_ref[r, 0:256, :] = (keep_ref[r] + came_ref[r, 0:256, :].astype(F32)).astype(BF16)
        out_ref[r, 256:320, :] = tables
    for i in range(3):
        on_ref[:, 128 * i : 128 * i + 128] = came_ref[4 + i, 256:272, :]


def translate_kernel(got_ref, out_ref, h_ref, s_ref):
    total = got_ref[0, 0:256, :].astype(F32)
    for r in range(1, 8):
        total = total + got_ref[r, 0:256, :].astype(F32)
    rays = total.astype(BF16).astype(F32)
    for r in range(8):
        y, xl = r // 2, r % 2
        for z in range(4):
            patch = 8 * y + 2 * z + xl
            tile = got_ref[r, 256 + 16 * z : 272 + 16 * z, :].astype(F32)
            for h in range(2):
                h_ref[h, pl.ds(patch, 8, stride=32), :] = tile[8 * h : 8 * h + 8]
    table = jnp.concatenate([h_ref[0], h_ref[1]], axis=1).astype(BF16)
    by_high = [rays[32 * t : 32 * t + 32] for t in range(8)]
    lane = iota((32, 128), 1)
    columns = []
    for t in range(8):
        rows = [by_high[t]]
        for b in range(1, 8):
            here = pltpu.roll(by_high[t], 16 * b, 1)
            before = pltpu.roll(by_high[t - 1], 16 * b, 1) if t > 0 else jnp.zeros((32, 128), F32)
            rows.append(jnp.where(lane < 16 * b, before, here))
        columns.append(jnp.concatenate(rows, axis=0).astype(BF16))
    lagged = [mm(table, column, TN) for column in columns]
    for t in range(8):
        incoming = lagged[t][0:32]
        for a in range(1, t + 1):
            incoming = incoming + lagged[t - a][32 * a : 32 * a + 32]
        s_ref[pl.ds(t, 32, stride=8), :] = incoming
    incoming = s_ref[...].astype(BF16)
    for r in range(8):
        out_ref[r] = incoming


def image_kernel(here_ref, there_ref, got_ref, out_ref, rows_ref, p_ref):
    core = lax.axis_index("c")
    mine = pl.multiple_of(128 * core, 128)
    theirs = pl.multiple_of(128 * (1 - core), 128)
    for h, ref in ((0, here_ref), (1, there_ref)):
        parts = lane_blocks_swapped([ref[r].astype(F32) for r in range(8)])
        for t in range(8):
            rows_ref[256 * t : 256 * t + 256, 128 * h : 128 * h + 128] = parts[t].astype(BF16)

    def step(i, carry):
        for s in range(2):
            p_ref[128 * s : 128 * s + 128, 0:128] = got_ref[2 * i + s, pl.ds(mine, 128), :]
            p_ref[128 * s : 128 * s + 128, 128:256] = got_ref[2 * i + s, pl.ds(theirs, 128), :]
        image = mm(rows_ref[...], p_ref[...], NT)
        for s in range(2):
            weight = got_ref[2 * i + s, ROW_W : ROW_W + 32, :].astype(F32)
            weight = jnp.broadcast_to(weight[:, None, :], (32, 8, 128))
            for t in range(8):
                block = image[256 * t : 256 * t + 256, 128 * s : 128 * s + 128]
                block = block.reshape(32, 8, 128) * weight
                out_ref[2 * i + s, 8 * t : 8 * t + 8, :] = jnp.sum(block, axis=0)
        return carry

    lax.fori_loop(0, 4, step, 0)


def element_kernel(
    couple_ref, bound_ref, fields_ref, scale_ref, diff_ref, interp_ref, lift_ref,
    links_ref, time_ref, on_ref, off_ref, out_ref, first_ref, nodes_ref, times_ref, factor_ref,
):
    core = lax.axis_index("c")
    elements = fields_ref.shape[2]
    both = jnp.concatenate([interp_ref[...].reshape(96, 64), diff_ref[...].reshape(192, 64)], axis=0)
    both_high, both_low = halves(both)
    both = jnp.concatenate([both_high, both_high, both_low], axis=1)
    ghosts = jnp.concatenate([on_ref[...], off_ref[...]], axis=0)
    own, ghost, grads = [], [], []
    for c in range(6):
        high, low = halves(fields_ref[c])
        product = mm(both, jnp.concatenate([high, low, high], axis=0))
        own.append(product[0:96])
        grads.append(product[96:288])
        beyond = ghosts[:, 64 * c : 64 * c + 64]
        ghost.append(mm(both_high[0:96], beyond, NT) + mm(both_low[0:96], beyond, NT))
    fluxes = [[] for _ in range(6)]
    bound = iota((16, elements), 1) < 8
    for f in range(6):
        at, to = 16 * f, 16 * (f ^ 1)
        pool = jnp.concatenate([own[c][to : to + 16] for c in range(6)], axis=0)
        beyond = jnp.concatenate([ghost[c][to : to + 16] for c in range(6)], axis=0)
        links = links_ref[f : f + 1, :]
        inside = one_hot(iota((elements, elements), 0) == links, BF16)
        outer = links - elements
        outer = jnp.where(core == 0, outer ^ 16, outer)
        outside = one_hot(iota((32, elements), 0) == outer, BF16)
        across = mm(jnp.concatenate(halves(pool), axis=0), inside)
        across = across + mm(jnp.concatenate(halves(beyond), axis=0), outside)
        across = across[0:96] + across[96:192]
        jumps = []
        for c in range(6):
            there = across[16 * c : 16 * c + 16]
            if f == 5:
                there = jnp.where(bound, 0.0, there)
            jumps.append(there - own[c][at : at + 16])
        for c in range(6):
            flux = couple_ref[f, c, 0] * jumps[0]
            for k in range(1, 6):
                flux = flux + couple_ref[f, c, k] * jumps[k]
            fluxes[c].append(flux)
    lift = lift_ref[...].reshape(96, 64)
    lift_high, lift_low = halves(lift)

    def grad(r, c):
        return grads[c][64 * r : 64 * r + 64]

    curls = (
        grad(1, 5) - grad(2, 4),
        grad(2, 3) - grad(0, 5),
        grad(0, 4) - grad(1, 3),
        grad(2, 1) - grad(1, 2),
        grad(0, 2) - grad(2, 0),
        grad(1, 0) - grad(0, 1),
    )
    scale = scale_ref[...]
    for c in range(6):
        high, low = halves(jnp.concatenate(fluxes[c], axis=0))
        surface = mm(lift_high, high, TN) + mm(lift_high, low, TN) + mm(lift_low, high, TN)
        value = curls[c] * scale + surface
        out_ref[c] = value
        first_ref[c] = value[:, 0:128]
    chosen = one_hot(iota((16, 128), 1) % 16 == iota((16, 128), 0))
    nodes_ref[...] = mm(lift_ref[5], chosen, TN, HIGH)
    row, sample = iota((64, 64), 0), iota((64, 64), 1)
    times = jnp.where(row % 8 * 8 + row // 8 == sample, time_ref[...], 0.0)
    times_ref[...] = jnp.broadcast_to(jnp.sum(times, axis=1, keepdims=True), (64, 128))
    for c in range(6):
        factor = couple_ref[5, c, 0] * bound_ref[0]
        for k in range(1, 6):
            factor = factor + couple_ref[5, c, k] * bound_ref[k]
        factor_ref[c] = jnp.full((8, 128), factor, F32)


def finish_kernel(
    parts_ref, first_ref, nodes_ref, times_ref, factor_ref, rate_ref, rate_out, field_out,
    tile_ref, sem,
):
    del rate_ref
    total = parts_ref[0]
    for i in range(1, 8):
        total = total + parts_ref[i]
    total = total * jnp.float32(1.0 / np.sqrt(np.float32(512)))
    for t in range(8):
        field_out[pl.ds(t, 8, stride=8), :] = total[8 * t : 8 * t + 8]
    now = jnp.sum(times_ref[...] * total, axis=0, keepdims=True)
    collect = one_hot(iota((256, 128), 0) % 128 // 16 == iota((256, 128), 1), BF16)
    lifted = mm(jnp.concatenate(halves(nodes_ref[...] * now), axis=1), collect)
    for c in range(6):
        tile_ref[c] = first_ref[c] + factor_ref[c, 0:1, :] * lifted
    copy = pltpu.make_async_copy(tile_ref, rate_out.at[:, :, pl.ds(0, 128)], sem)
    copy.start()
    copy.wait()


def call(kernel, out, in_specs, scratch=(), out_specs=None, grant=24, **options):
    run = pl.pallas_call(
        kernel,
        out_shape=out,
        in_specs=in_specs,
        out_specs=jax.tree.map(lambda _: VMEM, out) if out_specs is None else out_specs,
        scratch_shapes=list(scratch),
        compiler_params=pltpu.CompilerParams(vmem_limit_bytes=grant << 20),
        **options,
    )
    return run


def held(x):
    return pltpu.with_memory_space_constraint(x, pltpu.VMEM)


def shaped(shape, dtype):
    return jax.ShapeDtypeStruct(shape, dtype)


def vmem(shape, dtype):
    return pltpu.VMEM(shape, dtype)


def per_device(
    fields, inv_jacobian, diff_matrix, face_interp, lift_matrix, flux_couple, neighbours,
    send_index, bound_coef, current_coef, time_interp, current_history, group_weight, projection,
    kernels, pair_dest, pair_count,
):
    message, on_chip, off_chip = call(
        pack_kernel,
        (vmem((8, ROWS, 128), BF16), vmem((16, 384), BF16), vmem((16, 384), BF16)),
        [SMEM] * 4 + [VMEM] * 6,
        grant=60,
    )(
        send_index, pair_dest, pair_count, current_coef,
        fields, face_interp, current_history, group_weight, projection, kernels,
    )
    devices = 128
    beside = [(0, 1), (1, 0)]
    across = [(d, (d + 1 if d % 2 else d - 1) % devices) for d in range(devices)]
    anywhere = pl.BlockSpec(memory_space=pl.ANY)
    off_chip = lax.ppermute(off_chip, AXES, across)
    got = lax.all_to_all(message, ("z", "xh"), 0, 0, tiled=True)
    keep, send = call(
        rays_kernel,
        (vmem((8, 256, 128), F32), vmem((8, 272, 128), BF16)),
        [VMEM] * 2,
        (pltpu.VMEM((64, 1024), F32), pltpu.VMEM((32, 1024), F32), pltpu.VMEM((1024, 256), BF16)),
    )(held(got), held(on_chip))
    came = lax.ppermute(send, "c", beside)
    partial, on_chip = call(
        joined_kernel,
        (vmem((8, 320, 128), BF16), vmem((16, 384), BF16)),
        [VMEM] * 3,
    )(held(keep), held(send), held(came))
    partial = lax.all_to_all(partial, ("y", "xl"), 0, 0, tiled=True)
    incoming = call(
        translate_kernel,
        vmem((8, 256, 128), BF16),
        [VMEM],
        (pltpu.VMEM((2, 256, 128), F32), pltpu.VMEM((256, 128), F32)),
    )(held(partial))
    incoming = lax.all_to_all(incoming, ("y", "xl"), 0, 0, tiled=True)
    beyond = lax.ppermute(incoming, "c", beside)
    parts = call(
        image_kernel,
        vmem((8, 64, 128), F32),
        [VMEM] * 3,
        (pltpu.VMEM((2048, 256), BF16), pltpu.VMEM((256, 256), BF16)),
    )(held(incoming), held(beyond), held(got))
    parts, on_chip, off_chip = lax.optimization_barrier((parts, on_chip, off_chip))
    rate, first, nodes, times, factor = call(
        element_kernel,
        (
            shaped((6, 64, 256), F32), vmem((6, 64, 128), F32), vmem((64, 128), F32),
            vmem((64, 128), F32), vmem((6, 8, 128), F32),
        ),
        [SMEM] * 2 + [VMEM] * 9,
    )(
        flux_couple, bound_coef, fields, inv_jacobian.reshape(1, -1), diff_matrix,
        face_interp, lift_matrix.transpose(0, 2, 1), neighbours, time_interp.reshape(1, -1),
        held(on_chip), held(off_chip),
    )
    parts = lax.all_to_all(parts, ("z", "xh"), 0, 0, tiled=True)
    return call(
        finish_kernel,
        (shaped((6, 64, 256), F32), shaped((64, 128), F32)),
        [VMEM] * 5 + [anywhere],
        (pltpu.VMEM((6, 64, 128), F32), pltpu.SemaphoreType.DMA),
        out_specs=(anywhere, VMEM),
        input_output_aliases={5: 0},
    )(held(parts), held(first), held(nodes), held(times), held(factor), rate)


def solution(mesh):
    mesh = Mesh(np.asarray(mesh.devices).reshape(4, 4, 2, 2, 2), AXES)
    patch, level = ("y", "z", "xl"), ("xh", "c")
    placed = (
        P(None, None, AXES), P(AXES), P(), P(), P(), P(), P(None, AXES), P(None, AXES), P(), P(),
        P(), P(None, AXES), P(None, AXES), P(AXES, None), P(level, patch, None, None),
        P(level, patch, None), P(level, patch),
    )
    return jax.shard_map(
        per_device,
        mesh=mesh,
        in_specs=placed,
        out_specs=(P(None, None, AXES), P(None, AXES)),
        check_vma=False,
    )
```

```python
import jax
import jax.numpy as jnp
import numpy as np
from jax import lax
from jax.experimental import pallas as pl
from jax.experimental.pallas import tpu as pltpu
from jax.sharding import Mesh, PartitionSpec as P


F32 = jnp.float32
BF16 = jnp.bfloat16
HIGH = lax.Precision.HIGHEST
AXES = ("y", "z", "xl", "xh", "c")
VMEM = pl.BlockSpec(memory_space=pltpu.VMEM)
SMEM = pl.BlockSpec(memory_space=pltpu.SMEM)
ROW_C, ROW_W, ROW_T, ROWS = 256, 320, 352, 368
SETS = [
    [((((y * 4 + z) * 2 + (s ^ xh)) * 2 + xh) * 2) + c for z in range(4) for xh in range(2)]
    for y in range(4)
    for s in range(2)
    for c in range(2)
]
NN = (((1,), (0,)), ((), ()))
NT = (((1,), (1,)), ((), ()))
TN = (((0,), (0,)), ((), ()))


def iota(shape, dim):
    return lax.broadcasted_iota(jnp.int32, shape, dim)


def mm(a, b, dims=NN, precision=None):
    return lax.dot_general(a, b, dims, precision=precision, preferred_element_type=F32)


def one_hot(mask, dtype=F32):
    return jnp.where(mask, 1.0, 0.0).astype(dtype)


def halves(x):
    high = x.astype(BF16)
    return high, (x - high.astype(F32)).astype(BF16)


def lane_blocks_swapped(parts):
    parts = list(parts)
    shape = parts[0].shape
    block = iota(shape, 1) // 16
    for m in (4, 2, 1):
        upper = (block & m) != 0
        for j in range(8):
            if j & m:
                continue
            a, b = parts[j], parts[j + m]
            parts[j] = jnp.where(upper, pltpu.roll(b, 16 * m, 1), a)
            parts[j + m] = jnp.where(upper, b, pltpu.roll(a, 128 - 16 * m, 1))
    return parts


def pack_kernel(
    send_ref, dest_ref, count_ref, coef_ref,
    fields_ref, interp_ref, history_ref, weight_ref, projection_ref, kernels_ref,
    message_ref, on_ref, off_ref,
):
    core = lax.axis_index("c")
    elements = fields_ref.shape[2]
    flat = fields_ref[...].reshape(384, elements).astype(BF16)

    def picked(row):
        rows, lanes = iota((16, elements), 0), iota((16, elements), 1)
        wanted = jnp.zeros((16, elements), jnp.int32)
        for i in range(16):
            wanted = jnp.where(rows == i, send_ref[row, i], wanted)
        return mm(one_hot(lanes == wanted, BF16), flat, NT).astype(BF16)

    on_ref[...] = picked(1 - core)
    off_ref[...] = picked(core)
    mixed = jnp.zeros((64, 128), F32)
    for c in range(6):
        mixed = mixed + coef_ref[c] * fields_ref[c, :, 0:128]
    spread = one_hot(iota((128, 128), 1) // 16 == iota((128, 128), 0))
    chosen = one_hot(iota((16, 128), 1) % 16 == iota((16, 128), 0))
    by_element = mm(mixed, spread, NN, HIGH)
    by_node = mm(interp_ref[5], chosen, TN, HIGH)
    newest = jnp.sum(by_element * by_node, axis=0, keepdims=True)
    old = pltpu.roll(history_ref[...].astype(F32), 63, 0)
    currents = jnp.where(iota((64, 128), 0) == 63, newest, old).astype(BF16)
    lane_patch = iota((16, 128), 1) % 32
    wanted = jnp.full((16, 128), -1, jnp.int32)
    for j in range(16):
        to = jnp.where(j < count_ref[0, 0], dest_ref[0, 0, j], -1)
        wanted = jnp.where(iota((16, 128), 0) == j, to, wanted)
    spread_kernels = mm(kernels_ref[0, 0], one_hot(wanted == lane_patch, BF16), TN)
    group_of = iota((8, 128), 1) // 32
    table = []
    for h in range(2):
        rows = jnp.zeros((8, 128), F32)
        for a in range(4):
            at = 32 * h + 8 * a
            rows = jnp.where(group_of == a, spread_kernels[at : at + 8], rows)
        table.append(rows)
    table = jnp.concatenate(table, axis=0).astype(BF16)
    weights = []
    for level in range(4):
        pick = one_hot(iota((32, 128), 1) == 4 * iota((32, 128), 0) + level, BF16)
        weights.append(mm(pick, weight_ref[...]).astype(BF16))
    for i in range(8):
        z, xh = i // 2, i % 2
        at = 256 * (z // 2)
        message_ref[i, 0:128, :] = projection_ref[:, at : at + 128]
        message_ref[i, 128:256, :] = projection_ref[:, at + 128 : at + 256]
        message_ref[i, ROW_C : ROW_C + 64, :] = currents
        message_ref[i, ROW_W : ROW_W + 32, :] = weights[2 * xh + z % 2]
        message_ref[i, ROW_T:ROWS, :] = table


def rays_kernel(got_ref, on_ref, keep_ref, send_ref, c_ref, w_ref, p_ref):
    core, half = lax.axis_index("c"), lax.axis_index("xh")
    mine = pl.multiple_of(128 * core, 128)
    theirs = pl.multiple_of(128 * (1 - core), 128)
    for i in range(8):
        at = 128 * i
        c_ref[:, at : at + 128] = got_ref[i, ROW_C : ROW_C + 64, :].astype(F32)
        w_ref[:, at : at + 128] = got_ref[i, ROW_W : ROW_W + 32, :].astype(F32)
        p_ref[at : at + 128, 0:128] = got_ref[i, pl.ds(mine, 128), :]
        p_ref[at : at + 128, 128:256] = got_ref[i, pl.ds(theirs, 128), :]

    def step(pair, carry):
        c = c_ref[pl.ds(pl.multiple_of(16 * pair, 16), 16), :]
        w = w_ref[...]
        rows = [(c[t : t + 1] * w).astype(BF16) for t in range(16)]
        product = mm(jnp.concatenate(rows, axis=0), p_ref[...])
        for s in range(2):
            at = pl.multiple_of(64 * pair + 32 * s, 32)
            part = [product[256 * s + 32 * t : 256 * s + 32 * t + 32] for t in range(8)]
            kept = lane_blocks_swapped([x[:, 0:128] for x in part])
            sent = lane_blocks_swapped([x[:, 128:256] for x in part])
            for r in range(8):
                keep_ref[r, pl.ds(at, 32), :] = kept[r]
                send_ref[r, pl.ds(at, 32), :] = sent[r].astype(BF16)
        return carry

    lax.fori_loop(0, 4, step, 0)
    for z in range(4):
        send_ref[z, 256:272, :] = got_ref[2 * z + half, ROW_T:ROWS, :]
    for i in range(3):
        send_ref[4 + i, 256:272, :] = on_ref[:, 128 * i : 128 * i + 128]


def joined_kernel(keep_ref, send_ref, came_ref, out_ref, on_ref):
    has_tables = lax.axis_index("c") == lax.axis_index("z") % 2
    tables = []
    for z in range(4):
        here, there = send_ref[z, 256:272, :], came_ref[z, 256:272, :]
        tables.append(jnp.where(has_tables, here.astype(F32), there.astype(F32)).astype(BF16))
    tables = jnp.concatenate(tables, axis=0)
    for r in range(8):
        out_ref[r, 0:256, :] = (keep_ref[r] + came_ref[r, 0:256, :].astype(F32)).astype(BF16)
        out_ref[r, 256:320, :] = tables
    for i in range(3):
        on_ref[:, 128 * i : 128 * i + 128] = came_ref[4 + i, 256:272, :]


def translate_kernel(got_ref, out_ref, h_ref, s_ref):
    total = got_ref[0, 0:256, :].astype(F32)
    for r in range(1, 8):
        total = total + got_ref[r, 0:256, :].astype(F32)
    rays = total.astype(BF16).astype(F32)
    for r in range(8):
        y, xl = r // 2, r % 2
        for z in range(4):
            patch = 8 * y + 2 * z + xl
            tile = got_ref[r, 256 + 16 * z : 272 + 16 * z, :].astype(F32)
            for h in range(2):
                h_ref[h, pl.ds(patch, 8, stride=32), :] = tile[8 * h : 8 * h + 8]
    table = jnp.concatenate([h_ref[0], h_ref[1]], axis=1).astype(BF16)
    by_high = [rays[32 * t : 32 * t + 32] for t in range(8)]
    lane = iota((32, 128), 1)
    columns = []
    for t in range(8):
        rows = [by_high[t]]
        for b in range(1, 8):
            here = pltpu.roll(by_high[t], 16 * b, 1)
            before = pltpu.roll(by_high[t - 1], 16 * b, 1) if t > 0 else jnp.zeros((32, 128), F32)
            rows.append(jnp.where(lane < 16 * b, before, here))
        columns.append(jnp.concatenate(rows, axis=0).astype(BF16))
    lagged = [mm(table, column, TN) for column in columns]
    for t in range(8):
        incoming = lagged[t][0:32]
        for a in range(1, t + 1):
            incoming = incoming + lagged[t - a][32 * a : 32 * a + 32]
        s_ref[pl.ds(t, 32, stride=8), :] = incoming
    incoming = s_ref[...].astype(BF16)
    for r in range(8):
        out_ref[r] = incoming


def image_kernel(here_ref, there_ref, got_ref, out_ref, rows_ref, p_ref):
    core = lax.axis_index("c")
    mine = pl.multiple_of(128 * core, 128)
    theirs = pl.multiple_of(128 * (1 - core), 128)
    for h, ref in ((0, here_ref), (1, there_ref)):
        parts = lane_blocks_swapped([ref[r].astype(F32) for r in range(8)])
        for t in range(8):
            rows_ref[256 * t : 256 * t + 256, 128 * h : 128 * h + 128] = parts[t].astype(BF16)

    def step(i, carry):
        for s in range(2):
            p_ref[128 * s : 128 * s + 128, 0:128] = got_ref[2 * i + s, pl.ds(mine, 128), :]
            p_ref[128 * s : 128 * s + 128, 128:256] = got_ref[2 * i + s, pl.ds(theirs, 128), :]
        image = mm(rows_ref[...], p_ref[...], NT)
        for s in range(2):
            weight = got_ref[2 * i + s, ROW_W : ROW_W + 32, :].astype(F32)
            weight = jnp.broadcast_to(weight[:, None, :], (32, 8, 128))
            for t in range(8):
                block = image[256 * t : 256 * t + 256, 128 * s : 128 * s + 128]
                block = block.reshape(32, 8, 128) * weight
                out_ref[2 * i + s, 8 * t : 8 * t + 8, :] = jnp.sum(block, axis=0)
        return carry

    lax.fori_loop(0, 4, step, 0)


def element_kernel(
    couple_ref, bound_ref, fields_ref, scale_ref, diff_ref, interp_ref, lift_ref,
    links_ref, time_ref, on_ref, off_ref, out_ref, first_ref, nodes_ref, times_ref, factor_ref,
):
    core = lax.axis_index("c")
    elements = fields_ref.shape[2]
    both = jnp.concatenate([interp_ref[...].reshape(96, 64), diff_ref[...].reshape(192, 64)], axis=0)
    both_high, both_low = halves(both)
    both = jnp.concatenate([both_high, both_high, both_low], axis=1)
    ghosts = jnp.concatenate([on_ref[...], off_ref[...]], axis=0)
    own, ghost, grads = [], [], []
    for c in range(6):
        high, low = halves(fields_ref[c])
        product = mm(both, jnp.concatenate([high, low, high], axis=0))
        own.append(product[0:96])
        grads.append(product[96:288])
        beyond = ghosts[:, 64 * c : 64 * c + 64]
        ghost.append(mm(both_high[0:96], beyond, NT) + mm(both_low[0:96], beyond, NT))
    fluxes = [[] for _ in range(6)]
    bound = iota((16, elements), 1) < 8
    for f in range(6):
        at, to = 16 * f, 16 * (f ^ 1)
        pool = jnp.concatenate([own[c][to : to + 16] for c in range(6)], axis=0)
        beyond = jnp.concatenate([ghost[c][to : to + 16] for c in range(6)], axis=0)
        links = links_ref[f : f + 1, :]
        inside = one_hot(iota((elements, elements), 0) == links, BF16)
        outer = links - elements
        outer = jnp.where(core == 0, outer ^ 16, outer)
        outside = one_hot(iota((32, elements), 0) == outer, BF16)
        across = mm(jnp.concatenate(halves(pool), axis=0), inside)
        across = across + mm(jnp.concatenate(halves(beyond), axis=0), outside)
        across = across[0:96] + across[96:192]
        jumps = []
        for c in range(6):
            there = across[16 * c : 16 * c + 16]
            if f == 5:
                there = jnp.where(bound, 0.0, there)
            jumps.append(there - own[c][at : at + 16])
        for c in range(6):
            flux = couple_ref[f, c, 0] * jumps[0]
            for k in range(1, 6):
                flux = flux + couple_ref[f, c, k] * jumps[k]
            fluxes[c].append(flux)
    lift = lift_ref[...].reshape(96, 64)
    lift_high, lift_low = halves(lift)

    def grad(r, c):
        return grads[c][64 * r : 64 * r + 64]

    curls = (
        grad(1, 5) - grad(2, 4),
        grad(2, 3) - grad(0, 5),
        grad(0, 4) - grad(1, 3),
        grad(2, 1) - grad(1, 2),
        grad(0, 2) - grad(2, 0),
        grad(1, 0) - grad(0, 1),
    )
    scale = scale_ref[...]
    for c in range(6):
        high, low = halves(jnp.concatenate(fluxes[c], axis=0))
        surface = mm(lift_high, high, TN) + mm(lift_high, low, TN) + mm(lift_low, high, TN)
        value = curls[c] * scale + surface
        out_ref[c] = value
        first_ref[c] = value[:, 0:128]
    chosen = one_hot(iota((16, 128), 1) % 16 == iota((16, 128), 0))
    nodes_ref[...] = mm(lift_ref[5], chosen, TN, HIGH)
    row, sample = iota((64, 64), 0), iota((64, 64), 1)
    times = jnp.where(row % 8 * 8 + row // 8 == sample, time_ref[...], 0.0)
    times_ref[...] = jnp.broadcast_to(jnp.sum(times, axis=1, keepdims=True), (64, 128))
    for c in range(6):
        factor = couple_ref[5, c, 0] * bound_ref[0]
        for k in range(1, 6):
            factor = factor + couple_ref[5, c, k] * bound_ref[k]
        factor_ref[c] = jnp.full((8, 128), factor, F32)


def finish_kernel(
    parts_ref, first_ref, nodes_ref, times_ref, factor_ref, rate_ref, rate_out, field_out,
    tile_ref, sem,
):
    del rate_ref
    total = parts_ref[0]
    for i in range(1, 8):
        total = total + parts_ref[i]
    total = total * jnp.float32(1.0 / np.sqrt(np.float32(512)))
    for t in range(8):
        field_out[pl.ds(t, 8, stride=8), :] = total[8 * t : 8 * t + 8]
    now = jnp.sum(times_ref[...] * total, axis=0, keepdims=True)
    collect = one_hot(iota((256, 128), 0) % 128 // 16 == iota((256, 128), 1), BF16)
    lifted = mm(jnp.concatenate(halves(nodes_ref[...] * now), axis=1), collect)
    for c in range(6):
        tile_ref[c] = first_ref[c] + factor_ref[c, 0:1, :] * lifted
    copy = pltpu.make_async_copy(tile_ref, rate_out.at[:, :, pl.ds(0, 128)], sem)
    copy.start()
    copy.wait()


def call(kernel, out, in_specs, scratch=(), out_specs=None, grant=24, **options):
    run = pl.pallas_call(
        kernel,
        out_shape=out,
        in_specs=in_specs,
        out_specs=jax.tree.map(lambda _: VMEM, out) if out_specs is None else out_specs,
        scratch_shapes=list(scratch),
        compiler_params=pltpu.CompilerParams(vmem_limit_bytes=grant << 20),
        **options,
    )
    return run


def held(x):
    return pltpu.with_memory_space_constraint(x, pltpu.VMEM)


def shaped(shape, dtype):
    return jax.ShapeDtypeStruct(shape, dtype)


def vmem(shape, dtype):
    return pltpu.VMEM(shape, dtype)


def per_device(
    fields, inv_jacobian, diff_matrix, face_interp, lift_matrix, flux_couple, neighbours,
    send_index, bound_coef, current_coef, time_interp, current_history, group_weight, projection,
    kernels, pair_dest, pair_count,
):
    message, on_chip, off_chip = call(
        pack_kernel,
        (vmem((8, ROWS, 128), BF16), vmem((16, 384), BF16), vmem((16, 384), BF16)),
        [SMEM] * 4 + [VMEM] * 6,
        grant=60,
    )(
        send_index, pair_dest, pair_count, current_coef,
        fields, face_interp, current_history, group_weight, projection, kernels,
    )
    devices = 128
    beside = [(0, 1), (1, 0)]
    across = [(d, (d + 1 if d % 2 else d - 1) % devices) for d in range(devices)]
    anywhere = pl.BlockSpec(memory_space=pl.ANY)
    off_chip = lax.ppermute(off_chip, AXES, across)
    got = lax.all_to_all(message, AXES, 0, 0, axis_index_groups=SETS, tiled=True)
    keep, send = call(
        rays_kernel,
        (vmem((8, 256, 128), F32), vmem((8, 272, 128), BF16)),
        [VMEM] * 2,
        (pltpu.VMEM((64, 1024), F32), pltpu.VMEM((32, 1024), F32), pltpu.VMEM((1024, 256), BF16)),
    )(held(got), held(on_chip))
    came = lax.ppermute(send, "c", beside)
    partial, on_chip = call(
        joined_kernel,
        (vmem((8, 320, 128), BF16), vmem((16, 384), BF16)),
        [VMEM] * 3,
    )(held(keep), held(send), held(came))
    partial = lax.all_to_all(partial, ("y", "xl"), 0, 0, tiled=True)
    incoming = call(
        translate_kernel,
        vmem((8, 256, 128), BF16),
        [VMEM],
        (pltpu.VMEM((2, 256, 128), F32), pltpu.VMEM((256, 128), F32)),
    )(held(partial))
    incoming = lax.all_to_all(incoming, ("y", "xl"), 0, 0, tiled=True)
    beyond = lax.ppermute(incoming, "c", beside)
    parts = call(
        image_kernel,
        vmem((8, 64, 128), F32),
        [VMEM] * 3,
        (pltpu.VMEM((2048, 256), BF16), pltpu.VMEM((256, 256), BF16)),
    )(held(incoming), held(beyond), held(got))
    parts, on_chip, off_chip = lax.optimization_barrier((parts, on_chip, off_chip))
    rate, first, nodes, times, factor = call(
        element_kernel,
        (
            shaped((6, 64, 256), F32), vmem((6, 64, 128), F32), vmem((64, 128), F32),
            vmem((64, 128), F32), vmem((6, 8, 128), F32),
        ),
        [SMEM] * 2 + [VMEM] * 9,
    )(
        flux_couple, bound_coef, fields, inv_jacobian.reshape(1, -1), diff_matrix,
        face_interp, lift_matrix.transpose(0, 2, 1), neighbours, time_interp.reshape(1, -1),
        held(on_chip), held(off_chip),
    )
    parts = lax.all_to_all(parts, AXES, 0, 0, axis_index_groups=SETS, tiled=True)
    return call(
        finish_kernel,
        (shaped((6, 64, 256), F32), shaped((64, 128), F32)),
        [VMEM] * 5 + [anywhere],
        (pltpu.VMEM((6, 64, 128), F32), pltpu.SemaphoreType.DMA),
        out_specs=(anywhere, VMEM),
        input_output_aliases={5: 0},
    )(held(parts), held(first), held(nodes), held(times), held(factor), rate)


def solution(mesh):
    mesh = Mesh(np.asarray(mesh.devices).reshape(4, 4, 2, 2, 2), AXES)
    patch, level = ("y", "z", "xl"), ("xh", "c")
    placed = (
        P(None, None, AXES), P(AXES), P(), P(), P(), P(), P(None, AXES), P(None, AXES), P(), P(),
        P(), P(None, AXES), P(None, AXES), P(AXES, None), P(level, patch, None, None),
        P(level, patch, None), P(level, patch),
    )
    return jax.shard_map(
        per_device,
        mesh=mesh,
        in_specs=placed,
        out_specs=(P(None, None, AXES), P(None, AXES)),
        check_vma=False,
    )
```

```python
import jax
import jax.numpy as jnp
import numpy as np
from jax import lax
from jax.experimental import pallas as pl
from jax.experimental.pallas import tpu as pltpu
from jax.sharding import Mesh, PartitionSpec as P


F32 = jnp.float32
BF16 = jnp.bfloat16
HIGH = lax.Precision.HIGHEST
AXES = ("y", "z", "xl", "xh", "c")
VMEM = pl.BlockSpec(memory_space=pltpu.VMEM)
SMEM = pl.BlockSpec(memory_space=pltpu.SMEM)
ROW_C, ROW_W, ROW_T, ROWS = 256, 320, 352, 368
SETS = [
    [((((y * 4 + z) * 2 + (s ^ xh)) * 2 + xh) * 2) + c for z in range(4) for xh in range(2)]
    for y in range(4)
    for s in range(2)
    for c in range(2)
]
NN = (((1,), (0,)), ((), ()))
NT = (((1,), (1,)), ((), ()))
TN = (((0,), (0,)), ((), ()))


def iota(shape, dim):
    return lax.broadcasted_iota(jnp.int32, shape, dim)


def mm(a, b, dims=NN, precision=None):
    return lax.dot_general(a, b, dims, precision=precision, preferred_element_type=F32)


def one_hot(mask, dtype=F32):
    return jnp.where(mask, 1.0, 0.0).astype(dtype)


def halves(x):
    high = x.astype(BF16)
    return high, (x - high.astype(F32)).astype(BF16)


def lane_blocks_swapped(parts):
    parts = list(parts)
    shape = parts[0].shape
    block = iota(shape, 1) // 16
    for m in (4, 2, 1):
        upper = (block & m) != 0
        for j in range(8):
            if j & m:
                continue
            a, b = parts[j], parts[j + m]
            parts[j] = jnp.where(upper, pltpu.roll(b, 16 * m, 1), a)
            parts[j + m] = jnp.where(upper, b, pltpu.roll(a, 128 - 16 * m, 1))
    return parts


def pack_kernel(
    send_ref, dest_ref, count_ref, coef_ref,
    fields_ref, interp_ref, history_ref, weight_ref, projection_ref, kernels_ref,
    message_ref, on_ref, off_ref,
):
    core = lax.axis_index("c")
    elements = fields_ref.shape[2]
    flat = fields_ref[...].reshape(384, elements).astype(BF16)

    def picked(row):
        rows, lanes = iota((16, elements), 0), iota((16, elements), 1)
        wanted = jnp.zeros((16, elements), jnp.int32)
        for i in range(16):
            wanted = jnp.where(rows == i, send_ref[row, i], wanted)
        return mm(one_hot(lanes == wanted, BF16), flat, NT).astype(BF16)

    on_ref[...] = picked(1 - core)
    off_ref[...] = picked(core)
    mixed = jnp.zeros((64, 128), F32)
    for c in range(6):
        mixed = mixed + coef_ref[c] * fields_ref[c, :, 0:128]
    spread = one_hot(iota((128, 128), 1) // 16 == iota((128, 128), 0))
    chosen = one_hot(iota((16, 128), 1) % 16 == iota((16, 128), 0))
    by_element = mm(mixed, spread, NN, HIGH)
    by_node = mm(interp_ref[5], chosen, TN, HIGH)
    newest = jnp.sum(by_element * by_node, axis=0, keepdims=True)
    old = pltpu.roll(history_ref[...].astype(F32), 63, 0)
    currents = jnp.where(iota((64, 128), 0) == 63, newest, old).astype(BF16)
    lane_patch = iota((16, 128), 1) % 32
    wanted = jnp.full((16, 128), -1, jnp.int32)
    for j in range(16):
        to = jnp.where(j < count_ref[0, 0], dest_ref[0, 0, j], -1)
        wanted = jnp.where(iota((16, 128), 0) == j, to, wanted)
    spread_kernels = mm(kernels_ref[0, 0], one_hot(wanted == lane_patch, BF16), TN)
    group_of = iota((8, 128), 1) // 32
    table = []
    for h in range(2):
        rows = jnp.zeros((8, 128), F32)
        for a in range(4):
            at = 32 * h + 8 * a
            rows = jnp.where(group_of == a, spread_kernels[at : at + 8], rows)
        table.append(rows)
    table = jnp.concatenate(table, axis=0).astype(BF16)
    weights = []
    for level in range(4):
        pick = one_hot(iota((32, 128), 1) == 4 * iota((32, 128), 0) + level, BF16)
        weights.append(mm(pick, weight_ref[...]).astype(BF16))
    for i in range(8):
        z, xh = i // 2, i % 2
        at = 256 * (z // 2)
        message_ref[i, 0:128, :] = projection_ref[:, at : at + 128]
        message_ref[i, 128:256, :] = projection_ref[:, at + 128 : at + 256]
        message_ref[i, ROW_C : ROW_C + 64, :] = currents
        message_ref[i, ROW_W : ROW_W + 32, :] = weights[2 * xh + z % 2]
        message_ref[i, ROW_T:ROWS, :] = table


def rays_kernel(got_ref, on_ref, keep_ref, send_ref, c_ref, w_ref, p_ref):
    core, half = lax.axis_index("c"), lax.axis_index("xh")
    mine = pl.multiple_of(128 * core, 128)
    theirs = pl.multiple_of(128 * (1 - core), 128)
    for i in range(8):
        at = 128 * i
        c_ref[i] = got_ref[i, ROW_C : ROW_C + 64, :].astype(F32)
        w_ref[i] = got_ref[i, ROW_W : ROW_W + 32, :].astype(F32)
        p_ref[at : at + 128, 0:128] = got_ref[i, pl.ds(mine, 128), :]
        p_ref[at : at + 128, 128:256] = got_ref[i, pl.ds(theirs, 128), :]
    for z in range(4):
        send_ref[z, 256:272, :] = got_ref[2 * z + half, ROW_T:ROWS, :]
    for i in range(3):
        send_ref[4 + i, 256:272, :] = on_ref[:, 128 * i : 128 * i + 128]
    for high in range(8):
        rows = []
        for t in range(8 * high, 8 * high + 8):
            row = []
            for i in range(8):
                c = c_ref[i, pl.ds(t, 8, stride=0), :]
                row.append((w_ref[i].reshape(4, 8, 128) * c[None]).reshape(32, 128))
            rows.append(jnp.concatenate(row, axis=1).astype(BF16))
        product = mm(jnp.concatenate(rows, axis=0), p_ref[...])
        part = [product[32 * t : 32 * t + 32] for t in range(8)]
        kept = lane_blocks_swapped([x[:, 0:128] for x in part])
        sent = lane_blocks_swapped([x[:, 128:256].astype(BF16) for x in part])
        for r in range(8):
            keep_ref[r, 32 * high : 32 * high + 32, :] = kept[r]
            send_ref[r, 32 * high : 32 * high + 32, :] = sent[r]


def joined_kernel(keep_ref, send_ref, came_ref, out_ref, on_ref):
    has_tables = lax.axis_index("c") == lax.axis_index("z") % 2
    tables = []
    for z in range(4):
        here, there = send_ref[z, 256:272, :], came_ref[z, 256:272, :]
        tables.append(jnp.where(has_tables, here.astype(F32), there.astype(F32)).astype(BF16))
    tables = jnp.concatenate(tables, axis=0)
    for r in range(8):
        out_ref[r, 0:256, :] = (keep_ref[r] + came_ref[r, 0:256, :].astype(F32)).astype(BF16)
        out_ref[r, 256:320, :] = tables
    for i in range(3):
        on_ref[:, 128 * i : 128 * i + 128] = came_ref[4 + i, 256:272, :]


def translate_kernel(got_ref, out_ref, h_ref, s_ref):
    total = got_ref[0, 0:256, :].astype(F32)
    for r in range(1, 8):
        total = total + got_ref[r, 0:256, :].astype(F32)
    rays = total.astype(BF16).astype(F32)
    for r in range(8):
        y, xl = r // 2, r % 2
        for z in range(4):
            patch = 8 * y + 2 * z + xl
            tile = got_ref[r, 256 + 16 * z : 272 + 16 * z, :].astype(F32)
            for h in range(2):
                h_ref[h, pl.ds(patch, 8, stride=32), :] = tile[8 * h : 8 * h + 8]
    table = jnp.concatenate([h_ref[0], h_ref[1]], axis=1).astype(BF16)
    by_high = [rays[32 * t : 32 * t + 32] for t in range(8)]
    lane = iota((32, 128), 1)
    columns = []
    for t in range(8):
        rows = [by_high[t]]
        for b in range(1, 8):
            here = pltpu.roll(by_high[t], 16 * b, 1)
            before = pltpu.roll(by_high[t - 1], 16 * b, 1) if t > 0 else jnp.zeros((32, 128), F32)
            rows.append(jnp.where(lane < 16 * b, before, here))
        columns.append(jnp.concatenate(rows, axis=0).astype(BF16))
    lagged = [mm(table, column, TN) for column in columns]
    for t in range(8):
        incoming = lagged[t][0:32]
        for a in range(1, t + 1):
            incoming = incoming + lagged[t - a][32 * a : 32 * a + 32]
        s_ref[pl.ds(t, 32, stride=8), :] = incoming
    incoming = s_ref[...].astype(BF16)
    for r in range(8):
        out_ref[r] = incoming


def image_kernel(here_ref, there_ref, got_ref, out_ref, p_ref, w_ref):
    core = lax.axis_index("c")
    mine = pl.multiple_of(128 * core, 128)
    theirs = pl.multiple_of(128 * (1 - core), 128)
    for i in range(8):
        at = 128 * i
        p_ref[at : at + 128, 0:128] = got_ref[i, pl.ds(mine, 128), :]
        p_ref[at : at + 128, 128:256] = got_ref[i, pl.ds(theirs, 128), :]
        w_ref[i] = got_ref[i, ROW_W : ROW_W + 32, :].astype(F32)
    for chunk in range(2):
        at = 128 * chunk
        rows = []
        for ref in (here_ref, there_ref):
            parts = [ref[r, at : at + 128, :] for r in range(8)]
            rows.append(jnp.concatenate(lane_blocks_swapped(parts), axis=0))
        rows = jnp.concatenate(rows, axis=1)
        for i in range(4):
            image = mm(rows, p_ref[256 * i : 256 * i + 256, :], NT)
            weight = [
                jnp.concatenate([w_ref[2 * i + s, pl.ds(q, 8, stride=0), :] for s in range(2)], axis=1)
                for q in range(16 * chunk, 16 * chunk + 16)
            ]
            for t in range(8):
                total = image[128 * t : 128 * t + 8] * weight[0]
                for q in range(1, 16):
                    at = 128 * t + 8 * q
                    total = total + image[at : at + 8] * weight[q]
                for s in range(2):
                    part = total[:, 128 * s : 128 * s + 128]
                    if chunk > 0:
                        part = part + out_ref[2 * i + s, 8 * t : 8 * t + 8, :]
                    out_ref[2 * i + s, 8 * t : 8 * t + 8, :] = part


def element_kernel(
    couple_ref, bound_ref, fields_ref, scale_ref, diff_ref, interp_ref, lift_ref,
    links_ref, time_ref, on_ref, off_ref, out_ref, first_ref, nodes_ref, times_ref, factor_ref,
):
    core = lax.axis_index("c")
    elements = fields_ref.shape[2]
    both = jnp.concatenate([interp_ref[...].reshape(96, 64), diff_ref[...].reshape(192, 64)], axis=0)
    both_high, both_low = halves(both)
    both = jnp.concatenate([both_high, both_high, both_low], axis=1)
    ghosts = jnp.concatenate([on_ref[...], off_ref[...]], axis=0)
    own, ghost, grads = [], [], []
    for c in range(6):
        high, low = halves(fields_ref[c])
        product = mm(both, jnp.concatenate([high, low, high], axis=0))
        own.append(product[0:96])
        grads.append(product[96:288])
        beyond = ghosts[:, 64 * c : 64 * c + 64]
        ghost.append(mm(both_high[0:96], beyond, NT) + mm(both_low[0:96], beyond, NT))
    fluxes = [[] for _ in range(6)]
    bound = iota((16, elements), 1) < 8
    for f in range(6):
        at, to = 16 * f, 16 * (f ^ 1)
        pool = jnp.concatenate([own[c][to : to + 16] for c in range(6)], axis=0)
        beyond = jnp.concatenate([ghost[c][to : to + 16] for c in range(6)], axis=0)
        links = links_ref[f : f + 1, :]
        inside = one_hot(iota((elements, elements), 0) == links, BF16)
        outer = links - elements
        outer = jnp.where(core == 0, outer ^ 16, outer)
        outside = one_hot(iota((32, elements), 0) == outer, BF16)
        across = mm(jnp.concatenate(halves(pool), axis=0), inside)
        across = across + mm(jnp.concatenate(halves(beyond), axis=0), outside)
        across = across[0:96] + across[96:192]
        jumps = []
        for c in range(6):
            there = across[16 * c : 16 * c + 16]
            if f == 5:
                there = jnp.where(bound, 0.0, there)
            jumps.append(there - own[c][at : at + 16])
        for c in range(6):
            flux = couple_ref[f, c, 0] * jumps[0]
            for k in range(1, 6):
                flux = flux + couple_ref[f, c, k] * jumps[k]
            fluxes[c].append(flux)
    lift = lift_ref[...].reshape(96, 64)
    lift_high, lift_low = halves(lift)

    def grad(r, c):
        return grads[c][64 * r : 64 * r + 64]

    curls = (
        grad(1, 5) - grad(2, 4),
        grad(2, 3) - grad(0, 5),
        grad(0, 4) - grad(1, 3),
        grad(2, 1) - grad(1, 2),
        grad(0, 2) - grad(2, 0),
        grad(1, 0) - grad(0, 1),
    )
    scale = scale_ref[...]
    for c in range(6):
        high, low = halves(jnp.concatenate(fluxes[c], axis=0))
        surface = mm(lift_high, high, TN) + mm(lift_high, low, TN) + mm(lift_low, high, TN)
        value = curls[c] * scale + surface
        out_ref[c] = value
        first_ref[c] = value[:, 0:128]
    chosen = one_hot(iota((16, 128), 1) % 16 == iota((16, 128), 0))
    nodes_ref[...] = mm(lift_ref[5], chosen, TN, HIGH)
    row, sample = iota((64, 64), 0), iota((64, 64), 1)
    times = jnp.where(row % 8 * 8 + row // 8 == sample, time_ref[...], 0.0)
    times_ref[...] = jnp.broadcast_to(jnp.sum(times, axis=1, keepdims=True), (64, 128))
    for c in range(6):
        factor = couple_ref[5, c, 0] * bound_ref[0]
        for k in range(1, 6):
            factor = factor + couple_ref[5, c, k] * bound_ref[k]
        factor_ref[c] = jnp.full((8, 128), factor, F32)


def finish_kernel(
    parts_ref, first_ref, nodes_ref, times_ref, factor_ref, rate_ref, rate_out, field_out,
    tile_ref, sem,
):
    del rate_ref
    total = parts_ref[0]
    for i in range(1, 8):
        total = total + parts_ref[i]
    total = total * jnp.float32(1.0 / np.sqrt(np.float32(512)))
    for t in range(8):
        field_out[pl.ds(t, 8, stride=8), :] = total[8 * t : 8 * t + 8]
    now = jnp.sum(times_ref[...] * total, axis=0, keepdims=True)
    collect = one_hot(iota((256, 128), 0) % 128 // 16 == iota((256, 128), 1), BF16)
    lifted = mm(jnp.concatenate(halves(nodes_ref[...] * now), axis=1), collect)
    for c in range(6):
        tile_ref[c] = first_ref[c] + factor_ref[c, 0:1, :] * lifted
    copy = pltpu.make_async_copy(tile_ref, rate_out.at[:, :, pl.ds(0, 128)], sem)
    copy.start()
    copy.wait()


def call(kernel, out, in_specs, scratch=(), out_specs=None, grant=24, **options):
    run = pl.pallas_call(
        kernel,
        out_shape=out,
        in_specs=in_specs,
        out_specs=jax.tree.map(lambda _: VMEM, out) if out_specs is None else out_specs,
        scratch_shapes=list(scratch),
        compiler_params=pltpu.CompilerParams(vmem_limit_bytes=grant << 20),
        **options,
    )
    return run


def held(x):
    return pltpu.with_memory_space_constraint(x, pltpu.VMEM)


def shaped(shape, dtype):
    return jax.ShapeDtypeStruct(shape, dtype)


def vmem(shape, dtype):
    return pltpu.VMEM(shape, dtype)


def per_device(
    fields, inv_jacobian, diff_matrix, face_interp, lift_matrix, flux_couple, neighbours,
    send_index, bound_coef, current_coef, time_interp, current_history, group_weight, projection,
    kernels, pair_dest, pair_count,
):
    message, on_chip, off_chip = call(
        pack_kernel,
        (vmem((8, ROWS, 128), BF16), vmem((16, 384), BF16), vmem((16, 384), BF16)),
        [SMEM] * 4 + [VMEM] * 6,
        grant=60,
    )(
        send_index, pair_dest, pair_count, current_coef,
        fields, face_interp, current_history, group_weight, projection, kernels,
    )
    devices = 128
    beside = [(0, 1), (1, 0)]
    across = [(d, (d + 1 if d % 2 else d - 1) % devices) for d in range(devices)]
    anywhere = pl.BlockSpec(memory_space=pl.ANY)
    off_chip = lax.ppermute(off_chip, AXES, across)
    got = lax.all_to_all(message, AXES, 0, 0, axis_index_groups=SETS, tiled=True)
    keep, send = call(
        rays_kernel,
        (vmem((8, 256, 128), F32), vmem((8, 272, 128), BF16)),
        [VMEM] * 2,
        (pltpu.VMEM((8, 64, 128), F32), pltpu.VMEM((8, 32, 128), F32), pltpu.VMEM((1024, 256), BF16)),
    )(held(got), held(on_chip))
    came = lax.ppermute(send, "c", beside)
    partial, on_chip = call(
        joined_kernel,
        (vmem((8, 320, 128), BF16), vmem((16, 384), BF16)),
        [VMEM] * 3,
    )(held(keep), held(send), held(came))
    partial = lax.all_to_all(partial, ("y", "xl"), 0, 0, tiled=True)
    incoming = call(
        translate_kernel,
        vmem((8, 256, 128), BF16),
        [VMEM],
        (pltpu.VMEM((2, 256, 128), F32), pltpu.VMEM((256, 128), F32)),
    )(held(partial))
    incoming = lax.all_to_all(incoming, ("y", "xl"), 0, 0, tiled=True)
    beyond = lax.ppermute(incoming, "c", beside)
    parts = call(
        image_kernel,
        vmem((8, 64, 128), F32),
        [VMEM] * 3,
        (pltpu.VMEM((1024, 256), BF16), pltpu.VMEM((8, 32, 128), F32)),
    )(held(incoming), held(beyond), held(got))
    parts, on_chip, off_chip = lax.optimization_barrier((parts, on_chip, off_chip))
    rate, first, nodes, times, factor = call(
        element_kernel,
        (
            shaped((6, 64, 256), F32), vmem((6, 64, 128), F32), vmem((64, 128), F32),
            vmem((64, 128), F32), vmem((6, 8, 128), F32),
        ),
        [SMEM] * 2 + [VMEM] * 9,
    )(
        flux_couple, bound_coef, fields, inv_jacobian.reshape(1, -1), diff_matrix,
        face_interp, lift_matrix.transpose(0, 2, 1), neighbours, time_interp.reshape(1, -1),
        held(on_chip), held(off_chip),
    )
    parts = lax.all_to_all(parts, AXES, 0, 0, axis_index_groups=SETS, tiled=True)
    return call(
        finish_kernel,
        (shaped((6, 64, 256), F32), shaped((64, 128), F32)),
        [VMEM] * 5 + [anywhere],
        (pltpu.VMEM((6, 64, 128), F32), pltpu.SemaphoreType.DMA),
        out_specs=(anywhere, VMEM),
        input_output_aliases={5: 0},
    )(held(parts), held(first), held(nodes), held(times), held(factor), rate)


def solution(mesh):
    mesh = Mesh(np.asarray(mesh.devices).reshape(4, 4, 2, 2, 2), AXES)
    patch, level = ("y", "z", "xl"), ("xh", "c")
    placed = (
        P(None, None, AXES), P(AXES), P(), P(), P(), P(), P(None, AXES), P(None, AXES), P(), P(),
        P(), P(None, AXES), P(None, AXES), P(AXES, None), P(level, patch, None, None),
        P(level, patch, None), P(level, patch),
    )
    return jax.shard_map(
        per_device,
        mesh=mesh,
        in_specs=placed,
        out_specs=(P(None, None, AXES), P(None, AXES)),
        check_vma=False,
    )
```

```python
import jax
import jax.numpy as jnp
import numpy as np
from jax import lax
from jax.experimental import pallas as pl
from jax.experimental.pallas import tpu as pltpu
from jax.sharding import Mesh, PartitionSpec as P


F32 = jnp.float32
BF16 = jnp.bfloat16
HIGH = lax.Precision.HIGHEST
AXES = ("y", "z", "xl", "xh", "c")
VMEM = pl.BlockSpec(memory_space=pltpu.VMEM)
SMEM = pl.BlockSpec(memory_space=pltpu.SMEM)
ROW_C, ROW_W, ROW_T, ROWS = 256, 320, 352, 368
SETS = [
    [((((y * 4 + z) * 2 + (s ^ xh)) * 2 + xh) * 2) + c for z in range(4) for xh in range(2)]
    for y in range(4)
    for s in range(2)
    for c in range(2)
]
NN = (((1,), (0,)), ((), ()))
NT = (((1,), (1,)), ((), ()))
TN = (((0,), (0,)), ((), ()))


def iota(shape, dim):
    return lax.broadcasted_iota(jnp.int32, shape, dim)


def mm(a, b, dims=NN, precision=None):
    return lax.dot_general(a, b, dims, precision=precision, preferred_element_type=F32)


def one_hot(mask, dtype=F32):
    return jnp.where(mask, 1.0, 0.0).astype(dtype)


def halves(x):
    high = x.astype(BF16)
    return high, (x - high.astype(F32)).astype(BF16)


def lane_blocks_swapped(parts):
    parts = list(parts)
    shape = parts[0].shape
    block = iota(shape, 1) // 16
    for m in (4, 2, 1):
        upper = (block & m) != 0
        for j in range(8):
            if j & m:
                continue
            a, b = parts[j], parts[j + m]
            parts[j] = jnp.where(upper, pltpu.roll(b, 16 * m, 1), a)
            parts[j + m] = jnp.where(upper, b, pltpu.roll(a, 128 - 16 * m, 1))
    return parts


def pack_kernel(
    send_ref, dest_ref, count_ref, coef_ref,
    fields_ref, interp_ref, history_ref, weight_ref, projection_ref, kernels_ref,
    message_ref, on_ref, off_ref,
):
    core = lax.axis_index("c")
    elements = fields_ref.shape[2]
    flat = fields_ref[...].reshape(384, elements).astype(BF16)

    def picked(row):
        rows, lanes = iota((16, elements), 0), iota((16, elements), 1)
        wanted = jnp.zeros((16, elements), jnp.int32)
        for i in range(16):
            wanted = jnp.where(rows == i, send_ref[row, i], wanted)
        return mm(one_hot(lanes == wanted, BF16), flat, NT).astype(BF16)

    on_ref[...] = picked(1 - core)
    off_ref[...] = picked(core)
    mixed = jnp.zeros((64, 128), F32)
    for c in range(6):
        mixed = mixed + coef_ref[c] * fields_ref[c, :, 0:128]
    spread = one_hot(iota((128, 128), 1) // 16 == iota((128, 128), 0))
    chosen = one_hot(iota((16, 128), 1) % 16 == iota((16, 128), 0))
    by_element = mm(mixed, spread, NN, HIGH)
    by_node = mm(interp_ref[5], chosen, TN, HIGH)
    newest = jnp.sum(by_element * by_node, axis=0, keepdims=True)
    old = pltpu.roll(history_ref[...].astype(F32), 63, 0)
    currents = jnp.where(iota((64, 128), 0) == 63, newest, old).astype(BF16)
    lane_patch = iota((16, 128), 1) % 32
    wanted = jnp.full((16, 128), -1, jnp.int32)
    for j in range(16):
        to = jnp.where(j < count_ref[0, 0], dest_ref[0, 0, j], -1)
        wanted = jnp.where(iota((16, 128), 0) == j, to, wanted)
    spread_kernels = mm(kernels_ref[0, 0], one_hot(wanted == lane_patch, BF16), TN)
    group_of = iota((8, 128), 1) // 32
    table = []
    for h in range(2):
        rows = jnp.zeros((8, 128), F32)
        for a in range(4):
            at = 32 * h + 8 * a
            rows = jnp.where(group_of == a, spread_kernels[at : at + 8], rows)
        table.append(rows)
    table = jnp.concatenate(table, axis=0).astype(BF16)
    weights = []
    for level in range(4):
        pick = one_hot(iota((32, 128), 1) == 4 * iota((32, 128), 0) + level, BF16)
        weights.append(mm(pick, weight_ref[...]).astype(BF16))
    for i in range(8):
        z, xh = i // 2, i % 2
        at = 256 * (z // 2)
        message_ref[i, 0:128, :] = projection_ref[:, at : at + 128]
        message_ref[i, 128:256, :] = projection_ref[:, at + 128 : at + 256]
        message_ref[i, ROW_C : ROW_C + 64, :] = currents
        message_ref[i, ROW_W : ROW_W + 32, :] = weights[2 * xh + z % 2]
        message_ref[i, ROW_T:ROWS, :] = table


def rays_kernel(got_ref, on_ref, keep_ref, send_ref, c_ref, w_ref, p_ref):
    core, half = lax.axis_index("c"), lax.axis_index("xh")
    mine = pl.multiple_of(128 * core, 128)
    theirs = pl.multiple_of(128 * (1 - core), 128)
    for i in range(8):
        at = 128 * i
        c_ref[i] = got_ref[i, ROW_C : ROW_C + 64, :].astype(F32)
        w_ref[i] = got_ref[i, ROW_W : ROW_W + 32, :].astype(F32)
        p_ref[at : at + 128, 0:128] = got_ref[i, pl.ds(mine, 128), :]
        p_ref[at : at + 128, 128:256] = got_ref[i, pl.ds(theirs, 128), :]
    for z in range(4):
        send_ref[z, 256:272, :] = got_ref[2 * z + half, ROW_T:ROWS, :]
    for i in range(3):
        send_ref[4 + i, 256:272, :] = on_ref[:, 128 * i : 128 * i + 128]
    for high in range(8):
        rows = []
        for t in range(8 * high, 8 * high + 8):
            row = []
            for i in range(8):
                c = c_ref[i, pl.ds(t, 8, stride=0), :]
                row.append((w_ref[i].reshape(4, 8, 128) * c[None]).reshape(32, 128))
            rows.append(jnp.concatenate(row, axis=1).astype(BF16))
        product = mm(jnp.concatenate(rows, axis=0), p_ref[...])
        part = [product[32 * t : 32 * t + 32] for t in range(8)]
        kept = lane_blocks_swapped([x[:, 0:128] for x in part])
        sent = lane_blocks_swapped([x[:, 128:256].astype(BF16) for x in part])
        for r in range(8):
            keep_ref[r, 32 * high : 32 * high + 32, :] = kept[r]
            send_ref[r, 32 * high : 32 * high + 32, :] = sent[r]


def joined_kernel(keep_ref, send_ref, came_ref, out_ref, on_ref):
    has_tables = lax.axis_index("c") == lax.axis_index("z") % 2
    tables = []
    for z in range(4):
        here, there = send_ref[z, 256:272, :], came_ref[z, 256:272, :]
        tables.append(jnp.where(has_tables, here.astype(F32), there.astype(F32)).astype(BF16))
    tables = jnp.concatenate(tables, axis=0)
    for r in range(8):
        out_ref[r, 0:256, :] = (keep_ref[r] + came_ref[r, 0:256, :].astype(F32)).astype(BF16)
        out_ref[r, 256:320, :] = tables
    for i in range(3):
        on_ref[:, 128 * i : 128 * i + 128] = came_ref[4 + i, 256:272, :]


def translate_kernel(got_ref, out_ref, h_ref, s_ref):
    total = got_ref[0, 0:256, :].astype(F32)
    for r in range(1, 8):
        total = total + got_ref[r, 0:256, :].astype(F32)
    rays = total.astype(BF16).astype(F32)
    for r in range(8):
        y, xl = r // 2, r % 2
        for z in range(4):
            patch = 8 * y + 2 * z + xl
            tile = got_ref[r, 256 + 16 * z : 272 + 16 * z, :].astype(F32)
            for h in range(2):
                h_ref[h, pl.ds(patch, 8, stride=32), :] = tile[8 * h : 8 * h + 8]
    table = jnp.concatenate([h_ref[0], h_ref[1]], axis=1).astype(BF16)
    by_high = [rays[32 * t : 32 * t + 32] for t in range(8)]
    lane = iota((32, 128), 1)
    columns = []
    for t in range(8):
        rows = [by_high[t]]
        for b in range(1, 8):
            here = pltpu.roll(by_high[t], 16 * b, 1)
            before = pltpu.roll(by_high[t - 1], 16 * b, 1) if t > 0 else jnp.zeros((32, 128), F32)
            rows.append(jnp.where(lane < 16 * b, before, here))
        columns.append(jnp.concatenate(rows, axis=0).astype(BF16))
    lagged = [mm(table, column, TN) for column in columns]
    for t in range(8):
        incoming = lagged[t][0:32]
        for a in range(1, t + 1):
            incoming = incoming + lagged[t - a][32 * a : 32 * a + 32]
        s_ref[pl.ds(t, 32, stride=8), :] = incoming
    incoming = s_ref[...].astype(BF16)
    for r in range(8):
        out_ref[r] = incoming


def image_kernel(here_ref, there_ref, got_ref, out_ref, p_ref, w_ref, sum_ref):
    core = lax.axis_index("c")
    mine = pl.multiple_of(128 * core, 128)
    theirs = pl.multiple_of(128 * (1 - core), 128)
    for i in range(8):
        at = 128 * i
        p_ref[at : at + 128, 0:128] = got_ref[i, pl.ds(mine, 128), :]
        p_ref[at : at + 128, 128:256] = got_ref[i, pl.ds(theirs, 128), :]
        w_ref[i] = got_ref[i, ROW_W : ROW_W + 32, :].astype(F32)
    for chunk in range(2):
        at = 128 * chunk
        rows = []
        for ref in (here_ref, there_ref):
            parts = [ref[r, at : at + 128, :] for r in range(8)]
            rows.append(jnp.concatenate(lane_blocks_swapped(parts), axis=0))
        rows = jnp.concatenate(rows, axis=1)
        for i in range(4):
            image = mm(rows, p_ref[256 * i : 256 * i + 256, :], NT)
            weight = [
                jnp.concatenate([w_ref[2 * i + s, pl.ds(q, 8, stride=0), :] for s in range(2)], axis=1)
                for q in range(16 * chunk, 16 * chunk + 16)
            ]
            for t in range(8):
                total = image[128 * t : 128 * t + 8] * weight[0]
                for q in range(1, 16):
                    at = 128 * t + 8 * q
                    total = total + image[at : at + 8] * weight[q]
                for s in range(2):
                    part = total[:, 128 * s : 128 * s + 128]
                    if chunk > 0:
                        part = part + sum_ref[2 * i + s, 8 * t : 8 * t + 8, :]
                    sum_ref[2 * i + s, 8 * t : 8 * t + 8, :] = part
    for i in range(8):
        out_ref[i] = sum_ref[i].astype(BF16)


def element_kernel(
    couple_ref, bound_ref, fields_ref, scale_ref, diff_ref, interp_ref, lift_ref,
    links_ref, time_ref, on_ref, off_ref, out_ref, first_ref, nodes_ref, times_ref, factor_ref,
):
    core = lax.axis_index("c")
    elements = fields_ref.shape[2]
    both = jnp.concatenate([interp_ref[...].reshape(96, 64), diff_ref[...].reshape(192, 64)], axis=0)
    both_high, both_low = halves(both)
    both = jnp.concatenate([both_high, both_high, both_low], axis=1)
    ghosts = jnp.concatenate([on_ref[...], off_ref[...]], axis=0)
    own, ghost, grads = [], [], []
    for c in range(6):
        high, low = halves(fields_ref[c])
        product = mm(both, jnp.concatenate([high, low, high], axis=0))
        own.append(product[0:96])
        grads.append(product[96:288])
        beyond = ghosts[:, 64 * c : 64 * c + 64]
        ghost.append(mm(both_high[0:96], beyond, NT) + mm(both_low[0:96], beyond, NT))
    fluxes = [[] for _ in range(6)]
    bound = iota((16, elements), 1) < 8
    for f in range(6):
        at, to = 16 * f, 16 * (f ^ 1)
        pool = jnp.concatenate([own[c][to : to + 16] for c in range(6)], axis=0)
        beyond = jnp.concatenate([ghost[c][to : to + 16] for c in range(6)], axis=0)
        links = links_ref[f : f + 1, :]
        inside = one_hot(iota((elements, elements), 0) == links, BF16)
        outer = links - elements
        outer = jnp.where(core == 0, outer ^ 16, outer)
        outside = one_hot(iota((32, elements), 0) == outer, BF16)
        across = mm(jnp.concatenate(halves(pool), axis=0), inside)
        across = across + mm(jnp.concatenate(halves(beyond), axis=0), outside)
        across = across[0:96] + across[96:192]
        jumps = []
        for c in range(6):
            there = across[16 * c : 16 * c + 16]
            if f == 5:
                there = jnp.where(bound, 0.0, there)
            jumps.append(there - own[c][at : at + 16])
        for c in range(6):
            flux = couple_ref[f, c, 0] * jumps[0]
            for k in range(1, 6):
                flux = flux + couple_ref[f, c, k] * jumps[k]
            fluxes[c].append(flux)
    lift = lift_ref[...].reshape(96, 64)
    lift_high, lift_low = halves(lift)

    def grad(r, c):
        return grads[c][64 * r : 64 * r + 64]

    curls = (
        grad(1, 5) - grad(2, 4),
        grad(2, 3) - grad(0, 5),
        grad(0, 4) - grad(1, 3),
        grad(2, 1) - grad(1, 2),
        grad(0, 2) - grad(2, 0),
        grad(1, 0) - grad(0, 1),
    )
    scale = scale_ref[...]
    for c in range(6):
        high, low = halves(jnp.concatenate(fluxes[c], axis=0))
        surface = mm(lift_high, high, TN) + mm(lift_high, low, TN) + mm(lift_low, high, TN)
        value = curls[c] * scale + surface
        out_ref[c] = value
        first_ref[c] = value[:, 0:128]
    chosen = one_hot(iota((16, 128), 1) % 16 == iota((16, 128), 0))
    nodes_ref[...] = mm(lift_ref[5], chosen, TN, HIGH)
    row, sample = iota((64, 64), 0), iota((64, 64), 1)
    times = jnp.where(row % 8 * 8 + row // 8 == sample, time_ref[...], 0.0)
    times_ref[...] = jnp.broadcast_to(jnp.sum(times, axis=1, keepdims=True), (64, 128))
    for c in range(6):
        factor = couple_ref[5, c, 0] * bound_ref[0]
        for k in range(1, 6):
            factor = factor + couple_ref[5, c, k] * bound_ref[k]
        factor_ref[c] = jnp.full((8, 128), factor, F32)


def finish_kernel(
    parts_ref, first_ref, nodes_ref, times_ref, factor_ref, rate_ref, rate_out, field_out,
    tile_ref, field_ref, sems,
):
    del rate_ref
    total = parts_ref[0].astype(F32)
    for i in range(1, 8):
        total = total + parts_ref[i].astype(F32)
    total = total * jnp.float32(1.0 / np.sqrt(np.float32(512)))
    for t in range(8):
        field_ref[pl.ds(t, 8, stride=8), :] = total[8 * t : 8 * t + 8]
    copies = [pltpu.make_async_copy(field_ref, field_out, sems.at[6])]
    copies[0].start()
    now = jnp.sum(times_ref[...] * total, axis=0, keepdims=True)
    collect = one_hot(iota((256, 128), 0) % 128 // 16 == iota((256, 128), 1), BF16)
    lifted = mm(jnp.concatenate(halves(nodes_ref[...] * now), axis=1), collect)
    for c in range(6):
        tile_ref[c] = first_ref[c] + factor_ref[c, 0:1, :] * lifted
        copy = pltpu.make_async_copy(tile_ref.at[c], rate_out.at[c, :, pl.ds(0, 128)], sems.at[c])
        copy.start()
        copies.append(copy)
    for copy in copies:
        copy.wait()


def call(kernel, out, in_specs, scratch=(), out_specs=None, grant=24, **options):
    run = pl.pallas_call(
        kernel,
        out_shape=out,
        in_specs=in_specs,
        out_specs=jax.tree.map(lambda _: VMEM, out) if out_specs is None else out_specs,
        scratch_shapes=list(scratch),
        compiler_params=pltpu.CompilerParams(vmem_limit_bytes=grant << 20),
        **options,
    )
    return run


def held(x):
    return pltpu.with_memory_space_constraint(x, pltpu.VMEM)


def shaped(shape, dtype):
    return jax.ShapeDtypeStruct(shape, dtype)


def vmem(shape, dtype):
    return pltpu.VMEM(shape, dtype)


def per_device(
    fields, inv_jacobian, diff_matrix, face_interp, lift_matrix, flux_couple, neighbours,
    send_index, bound_coef, current_coef, time_interp, current_history, group_weight, projection,
    kernels, pair_dest, pair_count,
):
    message, on_chip, off_chip = call(
        pack_kernel,
        (vmem((8, ROWS, 128), BF16), vmem((16, 384), BF16), vmem((16, 384), BF16)),
        [SMEM] * 4 + [VMEM] * 6,
        grant=60,
    )(
        send_index, pair_dest, pair_count, current_coef,
        fields, face_interp, current_history, group_weight, projection, kernels,
    )
    devices = 128
    beside = [(0, 1), (1, 0)]
    across = [(d, (d + 1 if d % 2 else d - 1) % devices) for d in range(devices)]
    anywhere = pl.BlockSpec(memory_space=pl.ANY)
    off_chip = lax.ppermute(off_chip, AXES, across)
    got = lax.all_to_all(message, AXES, 0, 0, axis_index_groups=SETS, tiled=True)
    keep, send = call(
        rays_kernel,
        (vmem((8, 256, 128), F32), vmem((8, 272, 128), BF16)),
        [VMEM] * 2,
        (pltpu.VMEM((8, 64, 128), F32), pltpu.VMEM((8, 32, 128), F32), pltpu.VMEM((1024, 256), BF16)),
    )(held(got), held(on_chip))
    came = lax.ppermute(send, "c", beside)
    partial, on_chip = call(
        joined_kernel,
        (vmem((8, 320, 128), BF16), vmem((16, 384), BF16)),
        [VMEM] * 3,
    )(held(keep), held(send), held(came))
    partial = lax.all_to_all(partial, ("y", "xl"), 0, 0, tiled=True)
    incoming = call(
        translate_kernel,
        vmem((8, 256, 128), BF16),
        [VMEM],
        (pltpu.VMEM((2, 256, 128), F32), pltpu.VMEM((256, 128), F32)),
    )(held(partial))
    incoming = lax.all_to_all(incoming, ("y", "xl"), 0, 0, tiled=True)
    beyond = lax.ppermute(incoming, "c", beside)
    parts = call(
        image_kernel,
        vmem((8, 64, 128), BF16),
        [VMEM] * 3,
        (
            pltpu.VMEM((1024, 256), BF16), pltpu.VMEM((8, 32, 128), F32),
            pltpu.VMEM((8, 64, 128), F32),
        ),
    )(held(incoming), held(beyond), held(got))
    parts, on_chip, off_chip = lax.optimization_barrier((parts, on_chip, off_chip))
    rate, first, nodes, times, factor = call(
        element_kernel,
        (
            shaped((6, 64, 256), F32), vmem((6, 64, 128), F32), vmem((64, 128), F32),
            vmem((64, 128), F32), vmem((6, 8, 128), F32),
        ),
        [SMEM] * 2 + [VMEM] * 9,
    )(
        flux_couple, bound_coef, fields, inv_jacobian.reshape(1, -1), diff_matrix,
        face_interp, lift_matrix.transpose(0, 2, 1), neighbours, time_interp.reshape(1, -1),
        held(on_chip), held(off_chip),
    )
    parts = lax.all_to_all(parts, AXES, 0, 0, axis_index_groups=SETS, tiled=True)
    return call(
        finish_kernel,
        (shaped((6, 64, 256), F32), shaped((64, 128), F32)),
        [VMEM] * 5 + [anywhere],
        (
            pltpu.VMEM((6, 64, 128), F32), pltpu.VMEM((64, 128), F32),
            pltpu.SemaphoreType.DMA((7,)),
        ),
        out_specs=(anywhere, anywhere),
        input_output_aliases={5: 0},
    )(held(parts), held(first), held(nodes), held(times), held(factor), rate)


def solution(mesh):
    mesh = Mesh(np.asarray(mesh.devices).reshape(4, 4, 2, 2, 2), AXES)
    patch, level = ("y", "z", "xl"), ("xh", "c")
    placed = (
        P(None, None, AXES), P(AXES), P(), P(), P(), P(), P(None, AXES), P(None, AXES), P(), P(),
        P(), P(None, AXES), P(None, AXES), P(AXES, None), P(level, patch, None, None),
        P(level, patch, None), P(level, patch),
    )
    return jax.shard_map(
        per_device,
        mesh=mesh,
        in_specs=placed,
        out_specs=(P(None, None, AXES), P(None, AXES)),
        check_vma=False,
    )
```

```python
import jax
import jax.numpy as jnp
import numpy as np
from jax import lax
from jax.experimental import pallas as pl
from jax.experimental.pallas import tpu as pltpu
from jax.sharding import Mesh, PartitionSpec as P


F32 = jnp.float32
BF16 = jnp.bfloat16
HIGH = lax.Precision.HIGHEST
AXES = ("y", "z", "xl", "xh", "c")
VMEM = pl.BlockSpec(memory_space=pltpu.VMEM)
SMEM = pl.BlockSpec(memory_space=pltpu.SMEM)
ROW_C, ROW_W, ROW_T, ROWS = 256, 320, 352, 368
SETS = [
    [((((y * 4 + z) * 2 + (s ^ xh)) * 2 + xh) * 2) + c for y in range(4) for xh in range(2)]
    for z in range(4)
    for s in range(2)
    for c in range(2)
]
NN = (((1,), (0,)), ((), ()))
NT = (((1,), (1,)), ((), ()))
TN = (((0,), (0,)), ((), ()))


def iota(shape, dim):
    return lax.broadcasted_iota(jnp.int32, shape, dim)


def mm(a, b, dims=NN, precision=None):
    return lax.dot_general(a, b, dims, precision=precision, preferred_element_type=F32)


def one_hot(mask, dtype=F32):
    return jnp.where(mask, 1.0, 0.0).astype(dtype)


def halves(x):
    high = x.astype(BF16)
    return high, (x - high.astype(F32)).astype(BF16)


def lane_blocks_swapped(parts):
    parts = list(parts)
    shape = parts[0].shape
    block = iota(shape, 1) // 16
    for m in (4, 2, 1):
        upper = (block & m) != 0
        for j in range(8):
            if j & m:
                continue
            a, b = parts[j], parts[j + m]
            parts[j] = jnp.where(upper, pltpu.roll(b, 16 * m, 1), a)
            parts[j + m] = jnp.where(upper, b, pltpu.roll(a, 128 - 16 * m, 1))
    return parts


def pack_kernel(
    send_ref, dest_ref, count_ref, coef_ref,
    fields_ref, interp_ref, history_ref, weight_ref, projection_ref, kernels_ref,
    message_ref, on_ref, off_ref,
):
    core = lax.axis_index("c")
    elements = fields_ref.shape[2]
    flat = fields_ref[...].reshape(384, elements).astype(BF16)

    def picked(row):
        rows, lanes = iota((16, elements), 0), iota((16, elements), 1)
        wanted = jnp.zeros((16, elements), jnp.int32)
        for i in range(16):
            wanted = jnp.where(rows == i, send_ref[row, i], wanted)
        return mm(one_hot(lanes == wanted, BF16), flat, NT).astype(BF16)

    on_ref[...] = picked(1 - core)
    off_ref[...] = picked(core)
    mixed = jnp.zeros((64, 128), F32)
    for c in range(6):
        mixed = mixed + coef_ref[c] * fields_ref[c, :, 0:128]
    spread = one_hot(iota((128, 128), 1) // 16 == iota((128, 128), 0))
    chosen = one_hot(iota((16, 128), 1) % 16 == iota((16, 128), 0))
    by_element = mm(mixed, spread, NN, HIGH)
    by_node = mm(interp_ref[5], chosen, TN, HIGH)
    newest = jnp.sum(by_element * by_node, axis=0, keepdims=True)
    old = pltpu.roll(history_ref[...].astype(F32), 63, 0)
    currents = jnp.where(iota((64, 128), 0) == 63, newest, old).astype(BF16)
    lane_patch = iota((16, 128), 1) % 32
    wanted = jnp.full((16, 128), -1, jnp.int32)
    for j in range(16):
        to = jnp.where(j < count_ref[0, 0], dest_ref[0, 0, j], -1)
        wanted = jnp.where(iota((16, 128), 0) == j, to, wanted)
    spread_kernels = mm(kernels_ref[0, 0], one_hot(wanted == lane_patch, BF16), TN)
    group_of = iota((8, 128), 1) // 32
    table = []
    for h in range(2):
        rows = jnp.zeros((8, 128), F32)
        for a in range(4):
            at = 32 * h + 8 * a
            rows = jnp.where(group_of == a, spread_kernels[at : at + 8], rows)
        table.append(rows)
    table = jnp.concatenate(table, axis=0).astype(BF16)
    weights = []
    for level in range(4):
        pick = one_hot(iota((32, 128), 1) == 4 * iota((32, 128), 0) + level, BF16)
        weights.append(mm(pick, weight_ref[...]).astype(BF16))
    for i in range(8):
        y, xh = i // 2, i % 2
        at = 256 * (y // 2)
        message_ref[i, 0:128, :] = projection_ref[:, at : at + 128]
        message_ref[i, 128:256, :] = projection_ref[:, at + 128 : at + 256]
        message_ref[i, ROW_C : ROW_C + 64, :] = currents
        message_ref[i, ROW_W : ROW_W + 32, :] = weights[2 * xh + y % 2]
        message_ref[i, ROW_T:ROWS, :] = table


def rays_kernel(got_ref, on_ref, keep_ref, send_ref, c_ref, w_ref, p_ref):
    core, half = lax.axis_index("c"), lax.axis_index("xh")
    mine = pl.multiple_of(128 * core, 128)
    theirs = pl.multiple_of(128 * (1 - core), 128)
    for i in range(8):
        at = 128 * i
        c_ref[i] = got_ref[i, ROW_C : ROW_C + 64, :].astype(F32)
        w_ref[i] = got_ref[i, ROW_W : ROW_W + 32, :].astype(F32)
        p_ref[at : at + 128, 0:128] = got_ref[i, pl.ds(mine, 128), :]
        p_ref[at : at + 128, 128:256] = got_ref[i, pl.ds(theirs, 128), :]
    for y in range(4):
        send_ref[y, 256:272, :] = got_ref[2 * y + half, ROW_T:ROWS, :]
    for i in range(3):
        send_ref[4 + i, 256:272, :] = on_ref[:, 128 * i : 128 * i + 128]
    for high in range(8):
        rows = []
        for t in range(8 * high, 8 * high + 8):
            row = []
            for i in range(8):
                c = c_ref[i, pl.ds(t, 8, stride=0), :]
                row.append((w_ref[i].reshape(4, 8, 128) * c[None]).reshape(32, 128))
            rows.append(jnp.concatenate(row, axis=1).astype(BF16))
        product = mm(jnp.concatenate(rows, axis=0), p_ref[...])
        part = [product[32 * t : 32 * t + 32] for t in range(8)]
        kept = lane_blocks_swapped([x[:, 0:128] for x in part])
        sent = lane_blocks_swapped([x[:, 128:256].astype(BF16) for x in part])
        for r in range(8):
            keep_ref[r, 32 * high : 32 * high + 32, :] = kept[r]
            send_ref[r, 32 * high : 32 * high + 32, :] = sent[r]


def joined_kernel(keep_ref, send_ref, came_ref, out_ref, on_ref):
    has_tables = lax.axis_index("c") == lax.axis_index("y") % 2
    tables = []
    for y in range(4):
        here, there = send_ref[y, 256:272, :], came_ref[y, 256:272, :]
        tables.append(jnp.where(has_tables, here.astype(F32), there.astype(F32)).astype(BF16))
    tables = jnp.concatenate(tables, axis=0)
    for r in range(8):
        out_ref[r, 0:256, :] = (keep_ref[r] + came_ref[r, 0:256, :].astype(F32)).astype(BF16)
        out_ref[r, 256:320, :] = tables
    for i in range(3):
        on_ref[:, 128 * i : 128 * i + 128] = came_ref[4 + i, 256:272, :]


def translate_kernel(got_ref, out_ref, h_ref, s_ref):
    total = got_ref[0, 0:256, :].astype(F32)
    for r in range(1, 8):
        total = total + got_ref[r, 0:256, :].astype(F32)
    rays = total.astype(BF16).astype(F32)
    for r in range(8):
        for y in range(4):
            patch = 8 * y + r
            tile = got_ref[r, 256 + 16 * y : 272 + 16 * y, :].astype(F32)
            for h in range(2):
                h_ref[h, pl.ds(patch, 8, stride=32), :] = tile[8 * h : 8 * h + 8]
    table = jnp.concatenate([h_ref[0], h_ref[1]], axis=1).astype(BF16)
    by_high = [rays[32 * t : 32 * t + 32] for t in range(8)]
    lane = iota((32, 128), 1)
    columns = []
    for t in range(8):
        rows = [by_high[t]]
        for b in range(1, 8):
            here = pltpu.roll(by_high[t], 16 * b, 1)
            before = pltpu.roll(by_high[t - 1], 16 * b, 1) if t > 0 else jnp.zeros((32, 128), F32)
            rows.append(jnp.where(lane < 16 * b, before, here))
        columns.append(jnp.concatenate(rows, axis=0).astype(BF16))
    lagged = [mm(table, column, TN) for column in columns]
    for t in range(8):
        incoming = lagged[t][0:32]
        for a in range(1, t + 1):
            incoming = incoming + lagged[t - a][32 * a : 32 * a + 32]
        s_ref[pl.ds(t, 32, stride=8), :] = incoming
    incoming = s_ref[...].astype(BF16)
    for r in range(8):
        out_ref[r] = incoming


def image_kernel(here_ref, there_ref, got_ref, out_ref, p_ref, w_ref, sum_ref):
    core = lax.axis_index("c")
    mine = pl.multiple_of(128 * core, 128)
    theirs = pl.multiple_of(128 * (1 - core), 128)
    for i in range(8):
        at = 128 * i
        p_ref[at : at + 128, 0:128] = got_ref[i, pl.ds(mine, 128), :]
        p_ref[at : at + 128, 128:256] = got_ref[i, pl.ds(theirs, 128), :]
        w_ref[i] = got_ref[i, ROW_W : ROW_W + 32, :].astype(F32)
    for chunk in range(2):
        at = 128 * chunk
        rows = []
        for ref in (here_ref, there_ref):
            parts = [ref[r, at : at + 128, :] for r in range(8)]
            rows.append(jnp.concatenate(lane_blocks_swapped(parts), axis=0))
        rows = jnp.concatenate(rows, axis=1)
        for i in range(4):
            image = mm(rows, p_ref[256 * i : 256 * i + 256, :], NT)
            weight = [
                jnp.concatenate([w_ref[2 * i + s, pl.ds(q, 8, stride=0), :] for s in range(2)], axis=1)
                for q in range(16 * chunk, 16 * chunk + 16)
            ]
            for t in range(8):
                total = image[128 * t : 128 * t + 8] * weight[0]
                for q in range(1, 16):
                    at = 128 * t + 8 * q
                    total = total + image[at : at + 8] * weight[q]
                for s in range(2):
                    part = total[:, 128 * s : 128 * s + 128]
                    if chunk > 0:
                        part = part + sum_ref[2 * i + s, 8 * t : 8 * t + 8, :]
                    sum_ref[2 * i + s, 8 * t : 8 * t + 8, :] = part
    for i in range(8):
        out_ref[i] = sum_ref[i].astype(BF16)


def element_kernel(
    couple_ref, bound_ref, fields_ref, scale_ref, diff_ref, interp_ref, lift_ref,
    links_ref, time_ref, on_ref, off_ref, out_ref, first_ref, nodes_ref, times_ref, factor_ref,
):
    core = lax.axis_index("c")
    elements = fields_ref.shape[2]
    both = jnp.concatenate([interp_ref[...].reshape(96, 64), diff_ref[...].reshape(192, 64)], axis=0)
    both_high, both_low = halves(both)
    both = jnp.concatenate([both_high, both_high, both_low], axis=1)
    ghosts = jnp.concatenate([on_ref[...], off_ref[...]], axis=0)
    own, ghost, grads = [], [], []
    for c in range(6):
        high, low = halves(fields_ref[c])
        product = mm(both, jnp.concatenate([high, low, high], axis=0))
        own.append(product[0:96])
        grads.append(product[96:288])
        beyond = ghosts[:, 64 * c : 64 * c + 64]
        ghost.append(mm(both_high[0:96], beyond, NT) + mm(both_low[0:96], beyond, NT))
    fluxes = [[] for _ in range(6)]
    bound = iota((16, elements), 1) < 8
    for f in range(6):
        at, to = 16 * f, 16 * (f ^ 1)
        pool = jnp.concatenate([own[c][to : to + 16] for c in range(6)], axis=0)
        beyond = jnp.concatenate([ghost[c][to : to + 16] for c in range(6)], axis=0)
        links = links_ref[f : f + 1, :]
        inside = one_hot(iota((elements, elements), 0) == links, BF16)
        outer = links - elements
        outer = jnp.where(core == 0, outer ^ 16, outer)
        outside = one_hot(iota((32, elements), 0) == outer, BF16)
        across = mm(jnp.concatenate(halves(pool), axis=0), inside)
        across = across + mm(jnp.concatenate(halves(beyond), axis=0), outside)
        across = across[0:96] + across[96:192]
        jumps = []
        for c in range(6):
            there = across[16 * c : 16 * c + 16]
            if f == 5:
                there = jnp.where(bound, 0.0, there)
            jumps.append(there - own[c][at : at + 16])
        for c in range(6):
            flux = couple_ref[f, c, 0] * jumps[0]
            for k in range(1, 6):
                flux = flux + couple_ref[f, c, k] * jumps[k]
            fluxes[c].append(flux)
    lift = lift_ref[...].reshape(96, 64)
    lift_high, lift_low = halves(lift)

    def grad(r, c):
        return grads[c][64 * r : 64 * r + 64]

    curls = (
        grad(1, 5) - grad(2, 4),
        grad(2, 3) - grad(0, 5),
        grad(0, 4) - grad(1, 3),
        grad(2, 1) - grad(1, 2),
        grad(0, 2) - grad(2, 0),
        grad(1, 0) - grad(0, 1),
    )
    scale = scale_ref[...]
    for c in range(6):
        high, low = halves(jnp.concatenate(fluxes[c], axis=0))
        surface = mm(lift_high, high, TN) + mm(lift_high, low, TN) + mm(lift_low, high, TN)
        value = curls[c] * scale + surface
        out_ref[c] = value
        first_ref[c] = value[:, 0:128]
    chosen = one_hot(iota((16, 128), 1) % 16 == iota((16, 128), 0))
    nodes_ref[...] = mm(lift_ref[5], chosen, TN, HIGH)
    row, sample = iota((64, 64), 0), iota((64, 64), 1)
    times = jnp.where(row % 8 * 8 + row // 8 == sample, time_ref[...], 0.0)
    times_ref[...] = jnp.broadcast_to(jnp.sum(times, axis=1, keepdims=True), (64, 128))
    for c in range(6):
        factor = couple_ref[5, c, 0] * bound_ref[0]
        for k in range(1, 6):
            factor = factor + couple_ref[5, c, k] * bound_ref[k]
        factor_ref[c] = jnp.full((8, 128), factor, F32)


def finish_kernel(
    parts_ref, first_ref, nodes_ref, times_ref, factor_ref, rate_ref, rate_out, field_out,
    tile_ref, field_ref, sems,
):
    del rate_ref
    total = parts_ref[0].astype(F32)
    for i in range(1, 8):
        total = total + parts_ref[i].astype(F32)
    total = total * jnp.float32(1.0 / np.sqrt(np.float32(512)))
    for t in range(8):
        field_ref[pl.ds(t, 8, stride=8), :] = total[8 * t : 8 * t + 8]
    copies = [pltpu.make_async_copy(field_ref, field_out, sems.at[6])]
    copies[0].start()
    now = jnp.sum(times_ref[...] * total, axis=0, keepdims=True)
    collect = one_hot(iota((256, 128), 0) % 128 // 16 == iota((256, 128), 1), BF16)
    lifted = mm(jnp.concatenate(halves(nodes_ref[...] * now), axis=1), collect)
    for c in range(6):
        tile_ref[c] = first_ref[c] + factor_ref[c, 0:1, :] * lifted
        copy = pltpu.make_async_copy(tile_ref.at[c], rate_out.at[c, :, pl.ds(0, 128)], sems.at[c])
        copy.start()
        copies.append(copy)
    for copy in copies:
        copy.wait()


def call(kernel, out, in_specs, scratch=(), out_specs=None, grant=24, **options):
    run = pl.pallas_call(
        kernel,
        out_shape=out,
        in_specs=in_specs,
        out_specs=jax.tree.map(lambda _: VMEM, out) if out_specs is None else out_specs,
        scratch_shapes=list(scratch),
        compiler_params=pltpu.CompilerParams(vmem_limit_bytes=grant << 20),
        **options,
    )
    return run


def held(x):
    return pltpu.with_memory_space_constraint(x, pltpu.VMEM)


def shaped(shape, dtype):
    return jax.ShapeDtypeStruct(shape, dtype)


def vmem(shape, dtype):
    return pltpu.VMEM(shape, dtype)


def per_device(
    fields, inv_jacobian, diff_matrix, face_interp, lift_matrix, flux_couple, neighbours,
    send_index, bound_coef, current_coef, time_interp, current_history, group_weight, projection,
    kernels, pair_dest, pair_count,
):
    message, on_chip, off_chip = call(
        pack_kernel,
        (vmem((8, ROWS, 128), BF16), vmem((16, 384), BF16), vmem((16, 384), BF16)),
        [SMEM] * 4 + [VMEM] * 6,
        grant=60,
    )(
        send_index, pair_dest, pair_count, current_coef,
        fields, face_interp, current_history, group_weight, projection, kernels,
    )
    devices = 128
    beside = [(0, 1), (1, 0)]
    across = [(d, (d + 1 if d % 2 else d - 1) % devices) for d in range(devices)]
    anywhere = pl.BlockSpec(memory_space=pl.ANY)
    off_chip = lax.ppermute(off_chip, AXES, across)
    got = lax.all_to_all(message, AXES, 0, 0, axis_index_groups=SETS, tiled=True)
    keep, send = call(
        rays_kernel,
        (vmem((8, 256, 128), F32), vmem((8, 272, 128), BF16)),
        [VMEM] * 2,
        (pltpu.VMEM((8, 64, 128), F32), pltpu.VMEM((8, 32, 128), F32), pltpu.VMEM((1024, 256), BF16)),
    )(held(got), held(on_chip))
    came = lax.ppermute(send, "c", beside)
    partial, on_chip = call(
        joined_kernel,
        (vmem((8, 320, 128), BF16), vmem((16, 384), BF16)),
        [VMEM] * 3,
    )(held(keep), held(send), held(came))
    partial = lax.all_to_all(partial, ("z", "xl"), 0, 0, tiled=True)
    incoming = call(
        translate_kernel,
        vmem((8, 256, 128), BF16),
        [VMEM],
        (pltpu.VMEM((2, 256, 128), F32), pltpu.VMEM((256, 128), F32)),
    )(held(partial))
    incoming = lax.all_to_all(incoming, ("z", "xl"), 0, 0, tiled=True)
    beyond = lax.ppermute(incoming, "c", beside)
    parts = call(
        image_kernel,
        vmem((8, 64, 128), BF16),
        [VMEM] * 3,
        (
            pltpu.VMEM((1024, 256), BF16), pltpu.VMEM((8, 32, 128), F32),
            pltpu.VMEM((8, 64, 128), F32),
        ),
    )(held(incoming), held(beyond), held(got))
    parts, on_chip, off_chip = lax.optimization_barrier((parts, on_chip, off_chip))
    rate, first, nodes, times, factor = call(
        element_kernel,
        (
            shaped((6, 64, 256), F32), vmem((6, 64, 128), F32), vmem((64, 128), F32),
            vmem((64, 128), F32), vmem((6, 8, 128), F32),
        ),
        [SMEM] * 2 + [VMEM] * 9,
    )(
        flux_couple, bound_coef, fields, inv_jacobian.reshape(1, -1), diff_matrix,
        face_interp, lift_matrix.transpose(0, 2, 1), neighbours, time_interp.reshape(1, -1),
        held(on_chip), held(off_chip),
    )
    parts = lax.all_to_all(parts, AXES, 0, 0, axis_index_groups=SETS, tiled=True)
    return call(
        finish_kernel,
        (shaped((6, 64, 256), F32), shaped((64, 128), F32)),
        [VMEM] * 5 + [anywhere],
        (
            pltpu.VMEM((6, 64, 128), F32), pltpu.VMEM((64, 128), F32),
            pltpu.SemaphoreType.DMA((7,)),
        ),
        out_specs=(anywhere, anywhere),
        input_output_aliases={5: 0},
    )(held(parts), held(first), held(nodes), held(times), held(factor), rate)


def solution(mesh):
    mesh = Mesh(np.asarray(mesh.devices).reshape(4, 4, 2, 2, 2), AXES)
    patch, level = ("y", "z", "xl"), ("xh", "c")
    placed = (
        P(None, None, AXES), P(AXES), P(), P(), P(), P(), P(None, AXES), P(None, AXES), P(), P(),
        P(), P(None, AXES), P(None, AXES), P(AXES, None), P(level, patch, None, None),
        P(level, patch, None), P(level, patch),
    )
    return jax.shard_map(
        per_device,
        mesh=mesh,
        in_specs=placed,
        out_specs=(P(None, None, AXES), P(None, AXES)),
        check_vma=False,
    )
```

```python
import jax
import jax.numpy as jnp
import numpy as np
from jax import lax
from jax.experimental import pallas as pl
from jax.experimental.pallas import tpu as pltpu
from jax.sharding import Mesh, PartitionSpec as P


F32 = jnp.float32
BF16 = jnp.bfloat16
HIGH = lax.Precision.HIGHEST
AXES = ("y", "z", "xl", "xh", "c")
VMEM = pl.BlockSpec(memory_space=pltpu.VMEM)
SMEM = pl.BlockSpec(memory_space=pltpu.SMEM)
ROW_C, ROW_W, ROW_T, ROWS = 128, 192, 256, 272
SETS = [
    [((((y * 4 + z) * 2 + (s ^ xh)) * 2 + xh) * 2) + c for z in range(4) for xh in range(2)]
    for y in range(4)
    for s in range(2)
    for c in range(2)
]
NN = (((1,), (0,)), ((), ()))
NT = (((1,), (1,)), ((), ()))
TN = (((0,), (0,)), ((), ()))


def iota(shape, dim):
    return lax.broadcasted_iota(jnp.int32, shape, dim)


def mm(a, b, dims=NN, precision=None):
    return lax.dot_general(a, b, dims, precision=precision, preferred_element_type=F32)


def one_hot(mask, dtype=F32):
    return jnp.where(mask, 1.0, 0.0).astype(dtype)


def halves(x):
    high = x.astype(BF16)
    return high, (x - high.astype(F32)).astype(BF16)


def lane_blocks_swapped(parts):
    parts = list(parts)
    shape = parts[0].shape
    block = iota(shape, 1) // 16
    for m in (4, 2, 1):
        upper = (block & m) != 0
        for j in range(8):
            if j & m:
                continue
            a, b = parts[j], parts[j + m]
            parts[j] = jnp.where(upper, pltpu.roll(b, 16 * m, 1), a)
            parts[j + m] = jnp.where(upper, b, pltpu.roll(a, 128 - 16 * m, 1))
    return parts


def pack_kernel(
    send_ref, dest_ref, count_ref, coef_ref,
    fields_ref, interp_ref, history_ref, weight_ref, projection_ref, kernels_ref,
    message_ref, on_ref, off_ref,
):
    core = lax.axis_index("c")
    elements = fields_ref.shape[2]
    flat = fields_ref[...].reshape(384, elements).astype(BF16)

    def picked(row):
        rows, lanes = iota((16, elements), 0), iota((16, elements), 1)
        wanted = jnp.zeros((16, elements), jnp.int32)
        for i in range(16):
            wanted = jnp.where(rows == i, send_ref[row, i], wanted)
        return mm(one_hot(lanes == wanted, BF16), flat, NT).astype(BF16)

    on_ref[...] = picked(1 - core)
    off_ref[...] = picked(core)
    mixed = jnp.zeros((64, 128), F32)
    for c in range(6):
        mixed = mixed + coef_ref[c] * fields_ref[c, :, 0:128]
    spread = one_hot(iota((128, 128), 1) // 16 == iota((128, 128), 0))
    chosen = one_hot(iota((16, 128), 1) % 16 == iota((16, 128), 0))
    by_element = mm(mixed, spread, NN, HIGH)
    by_node = mm(interp_ref[5], chosen, TN, HIGH)
    newest = jnp.sum(by_element * by_node, axis=0, keepdims=True)
    old = pltpu.roll(history_ref[...].astype(F32), 63, 0)
    currents = jnp.where(iota((64, 128), 0) == 63, newest, old).astype(BF16)
    lane_patch = iota((16, 128), 1) % 32
    wanted = jnp.full((16, 128), -1, jnp.int32)
    for j in range(16):
        to = jnp.where(j < count_ref[0, 0], dest_ref[0, 0, j], -1)
        wanted = jnp.where(iota((16, 128), 0) == j, to, wanted)
    spread_kernels = mm(kernels_ref[0, 0], one_hot(wanted == lane_patch, BF16), TN)
    group_of = iota((8, 128), 1) // 32
    table = []
    for h in range(2):
        rows = jnp.zeros((8, 128), F32)
        for a in range(4):
            at = 32 * h + 8 * a
            rows = jnp.where(group_of == a, spread_kernels[at : at + 8], rows)
        table.append(rows)
    table = jnp.concatenate(table, axis=0).astype(BF16)
    weights = []
    for level in range(4):
        pick = one_hot(iota((32, 128), 1) == 4 * iota((32, 128), 0) + level, BF16)
        weights.append(mm(pick, weight_ref[...]).astype(BF16))
    for i in range(8):
        z, xh = i // 2, i % 2
        message_ref[i, 0:128, :] = projection_ref[:, 128 * z : 128 * z + 128]
        message_ref[i, ROW_C : ROW_C + 64, :] = currents
        message_ref[i, ROW_W : ROW_W + 32, :] = weights[2 * xh]
        message_ref[i, ROW_W + 32 : ROW_W + 64, :] = weights[2 * xh + 1]
        message_ref[i, ROW_T:ROWS, :] = table


def level_weights(got_ref, i, level):
    return got_ref[i, pl.ds(pl.multiple_of(ROW_W + 32 * level, 32), 32), :].astype(F32)


def partial_rays(got_ref, level, out_ref, c_ref, w_ref, p_ref):
    for i in range(8):
        c_ref[i] = got_ref[i, ROW_C : ROW_C + 64, :].astype(F32)
        w_ref[i] = level_weights(got_ref, i, level)
        p_ref[128 * i : 128 * i + 128, :] = got_ref[i, 0:128, :]
    for high in range(8):
        rows = []
        for t in range(8 * high, 8 * high + 8):
            row = []
            for i in range(8):
                c = c_ref[i, pl.ds(t, 8, stride=0), :]
                row.append((w_ref[i].reshape(4, 8, 128) * c[None]).reshape(32, 128))
            rows.append(jnp.concatenate(row, axis=1).astype(BF16))
        product = mm(jnp.concatenate(rows, axis=0), p_ref[...])
        parts = [product[32 * t : 32 * t + 32].astype(out_ref.dtype) for t in range(8)]
        parts = lane_blocks_swapped(parts)
        for r in range(8):
            out_ref[r, 32 * high : 32 * high + 32, :] = parts[r]


def sent_kernel(got_ref, on_ref, send_ref, c_ref, w_ref, p_ref):
    for i in range(3):
        send_ref[i, 256:272, :] = on_ref[:, 128 * i : 128 * i + 128]
    partial_rays(got_ref, 1 - lax.axis_index("c"), send_ref, c_ref, w_ref, p_ref)


def kept_kernel(got_ref, keep_ref, table_ref, c_ref, w_ref, p_ref):
    half = lax.axis_index("xh")
    for z in range(4):
        table_ref[16 * z : 16 * z + 16, :] = got_ref[2 * z + half, ROW_T:ROWS, :]
    partial_rays(got_ref, lax.axis_index("c"), keep_ref, c_ref, w_ref, p_ref)


def joined_kernel(keep_ref, table_ref, came_ref, out_ref, on_ref):
    for r in range(8):
        out_ref[r, 0:256, :] = (keep_ref[r] + came_ref[r, 0:256, :].astype(F32)).astype(BF16)
        out_ref[r, 256:320, :] = table_ref[...]
    for i in range(3):
        on_ref[:, 128 * i : 128 * i + 128] = came_ref[i, 256:272, :]


def translate_kernel(got_ref, out_ref, h_ref, s_ref):
    total = got_ref[0, 0:256, :].astype(F32)
    for r in range(1, 8):
        total = total + got_ref[r, 0:256, :].astype(F32)
    rays = total.astype(BF16).astype(F32)
    for r in range(8):
        y, xl = r // 2, r % 2
        for z in range(4):
            patch = 8 * y + 2 * z + xl
            tile = got_ref[r, 256 + 16 * z : 272 + 16 * z, :].astype(F32)
            for h in range(2):
                h_ref[h, pl.ds(patch, 8, stride=32), :] = tile[8 * h : 8 * h + 8]
    table = jnp.concatenate([h_ref[0], h_ref[1]], axis=1).astype(BF16)
    by_high = [rays[32 * t : 32 * t + 32] for t in range(8)]
    lane = iota((32, 128), 1)
    columns = []
    for t in range(8):
        rows = [by_high[t]]
        for b in range(1, 8):
            here = pltpu.roll(by_high[t], 16 * b, 1)
            before = pltpu.roll(by_high[t - 1], 16 * b, 1) if t > 0 else jnp.zeros((32, 128), F32)
            rows.append(jnp.where(lane < 16 * b, before, here))
        columns.append(jnp.concatenate(rows, axis=0).astype(BF16))
    lagged = [mm(table, column, TN) for column in columns]
    for t in range(8):
        incoming = lagged[t][0:32]
        for a in range(1, t + 1):
            incoming = incoming + lagged[t - a][32 * a : 32 * a + 32]
        s_ref[pl.ds(t, 32, stride=8), :] = incoming
    incoming = s_ref[...].astype(BF16)
    for r in range(8):
        out_ref[r] = incoming


def add_images(incoming_ref, got_ref, level, before_ref, sum_ref, p_ref, w_ref):
    for i in range(8):
        p_ref[128 * i : 128 * i + 128, :] = got_ref[i, 0:128, :]
        w_ref[i] = level_weights(got_ref, i, level)
    for chunk in range(2):
        at = 128 * chunk
        parts = [incoming_ref[r, at : at + 128, :] for r in range(8)]
        rows = jnp.concatenate(lane_blocks_swapped(parts), axis=0)
        start = sum_ref if chunk > 0 else before_ref
        for i in range(4):
            image = mm(rows, p_ref[256 * i : 256 * i + 256, :], NT)
            weight = [
                jnp.concatenate(
                    [w_ref[2 * i + s, pl.ds(q, 8, stride=0), :] for s in range(2)], axis=1
                )
                for q in range(16 * chunk, 16 * chunk + 16)
            ]
            for t in range(8):
                total = image[128 * t : 128 * t + 8] * weight[0]
                for q in range(1, 16):
                    at = 128 * t + 8 * q
                    total = total + image[at : at + 8] * weight[q]
                for s in range(2):
                    part = total[:, 128 * s : 128 * s + 128]
                    if start is not None:
                        part = part + start[2 * i + s, 8 * t : 8 * t + 8, :]
                    sum_ref[2 * i + s, 8 * t : 8 * t + 8, :] = part


def near_kernel(here_ref, got_ref, sum_ref, p_ref, w_ref):
    add_images(here_ref, got_ref, lax.axis_index("c"), None, sum_ref, p_ref, w_ref)


def far_kernel(there_ref, got_ref, before_ref, out_ref, p_ref, w_ref, sum_ref):
    add_images(there_ref, got_ref, 1 - lax.axis_index("c"), before_ref, sum_ref, p_ref, w_ref)
    for i in range(8):
        out_ref[i] = sum_ref[i].astype(BF16)


def element_kernel(
    couple_ref, bound_ref, fields_ref, scale_ref, diff_ref, interp_ref, lift_ref,
    links_ref, time_ref, on_ref, off_ref, out_ref, first_ref, nodes_ref, times_ref, factor_ref,
):
    core = lax.axis_index("c")
    elements = fields_ref.shape[2]
    both = jnp.concatenate([interp_ref[...].reshape(96, 64), diff_ref[...].reshape(192, 64)], axis=0)
    both_high, both_low = halves(both)
    both = jnp.concatenate([both_high, both_high, both_low], axis=1)
    ghosts = jnp.concatenate([on_ref[...], off_ref[...]], axis=0)
    own, ghost, grads = [], [], []
    for c in range(6):
        high, low = halves(fields_ref[c])
        product = mm(both, jnp.concatenate([high, low, high], axis=0))
        own.append(product[0:96])
        grads.append(product[96:288])
        beyond = ghosts[:, 64 * c : 64 * c + 64]
        ghost.append(mm(both_high[0:96], beyond, NT) + mm(both_low[0:96], beyond, NT))
    fluxes = [[] for _ in range(6)]
    bound = iota((16, elements), 1) < 8
    for f in range(6):
        at, to = 16 * f, 16 * (f ^ 1)
        pool = jnp.concatenate([own[c][to : to + 16] for c in range(6)], axis=0)
        beyond = jnp.concatenate([ghost[c][to : to + 16] for c in range(6)], axis=0)
        links = links_ref[f : f + 1, :]
        inside = one_hot(iota((elements, elements), 0) == links, BF16)
        outer = links - elements
        outer = jnp.where(core == 0, outer ^ 16, outer)
        outside = one_hot(iota((32, elements), 0) == outer, BF16)
        across = mm(jnp.concatenate(halves(pool), axis=0), inside)
        across = across + mm(jnp.concatenate(halves(beyond), axis=0), outside)
        across = across[0:96] + across[96:192]
        jumps = []
        for c in range(6):
            there = across[16 * c : 16 * c + 16]
            if f == 5:
                there = jnp.where(bound, 0.0, there)
            jumps.append(there - own[c][at : at + 16])
        for c in range(6):
            flux = couple_ref[f, c, 0] * jumps[0]
            for k in range(1, 6):
                flux = flux + couple_ref[f, c, k] * jumps[k]
            fluxes[c].append(flux)
    lift = lift_ref[...].reshape(96, 64)
    lift_high, lift_low = halves(lift)

    def grad(r, c):
        return grads[c][64 * r : 64 * r + 64]

    curls = (
        grad(1, 5) - grad(2, 4),
        grad(2, 3) - grad(0, 5),
        grad(0, 4) - grad(1, 3),
        grad(2, 1) - grad(1, 2),
        grad(0, 2) - grad(2, 0),
        grad(1, 0) - grad(0, 1),
    )
    scale = scale_ref[...]
    for c in range(6):
        high, low = halves(jnp.concatenate(fluxes[c], axis=0))
        surface = mm(lift_high, high, TN) + mm(lift_high, low, TN) + mm(lift_low, high, TN)
        value = curls[c] * scale + surface
        out_ref[c] = value
        first_ref[c] = value[:, 0:128]
    chosen = one_hot(iota((16, 128), 1) % 16 == iota((16, 128), 0))
    nodes_ref[...] = mm(lift_ref[5], chosen, TN, HIGH)
    row, sample = iota((64, 64), 0), iota((64, 64), 1)
    times = jnp.where(row % 8 * 8 + row // 8 == sample, time_ref[...], 0.0)
    times_ref[...] = jnp.broadcast_to(jnp.sum(times, axis=1, keepdims=True), (64, 128))
    for c in range(6):
        factor = couple_ref[5, c, 0] * bound_ref[0]
        for k in range(1, 6):
            factor = factor + couple_ref[5, c, k] * bound_ref[k]
        factor_ref[c] = jnp.full((8, 128), factor, F32)


def finish_kernel(
    parts_ref, first_ref, nodes_ref, times_ref, factor_ref, rate_ref, rate_out, field_out,
    tile_ref, field_ref, sems,
):
    del rate_ref
    total = parts_ref[0].astype(F32)
    for i in range(1, 8):
        total = total + parts_ref[i].astype(F32)
    total = total * jnp.float32(1.0 / np.sqrt(np.float32(512)))
    for t in range(8):
        field_ref[pl.ds(t, 8, stride=8), :] = total[8 * t : 8 * t + 8]
    copies = [pltpu.make_async_copy(field_ref, field_out, sems.at[6])]
    copies[0].start()
    now = jnp.sum(times_ref[...] * total, axis=0, keepdims=True)
    collect = one_hot(iota((256, 128), 0) % 128 // 16 == iota((256, 128), 1), BF16)
    lifted = mm(jnp.concatenate(halves(nodes_ref[...] * now), axis=1), collect)
    for c in range(6):
        tile_ref[c] = first_ref[c] + factor_ref[c, 0:1, :] * lifted
        copy = pltpu.make_async_copy(tile_ref.at[c], rate_out.at[c, :, pl.ds(0, 128)], sems.at[c])
        copy.start()
        copies.append(copy)
    for copy in copies:
        copy.wait()


def call(kernel, out, in_specs, scratch=(), out_specs=None, grant=24, **options):
    run = pl.pallas_call(
        kernel,
        out_shape=out,
        in_specs=in_specs,
        out_specs=jax.tree.map(lambda _: VMEM, out) if out_specs is None else out_specs,
        scratch_shapes=list(scratch),
        compiler_params=pltpu.CompilerParams(vmem_limit_bytes=grant << 20),
        **options,
    )
    return run


def held(x):
    return pltpu.with_memory_space_constraint(x, pltpu.VMEM)


def shaped(shape, dtype):
    return jax.ShapeDtypeStruct(shape, dtype)


def vmem(shape, dtype):
    return pltpu.VMEM(shape, dtype)


def per_device(
    fields, inv_jacobian, diff_matrix, face_interp, lift_matrix, flux_couple, neighbours,
    send_index, bound_coef, current_coef, time_interp, current_history, group_weight, projection,
    kernels, pair_dest, pair_count,
):
    message, on_chip, off_chip = call(
        pack_kernel,
        (vmem((8, ROWS, 128), BF16), vmem((16, 384), BF16), vmem((16, 384), BF16)),
        [SMEM] * 4 + [VMEM] * 6,
        grant=60,
    )(
        send_index, pair_dest, pair_count, current_coef,
        fields, face_interp, current_history, group_weight, projection, kernels,
    )
    devices = 128
    beside = [(0, 1), (1, 0)]
    across = [(d, (d + 1 if d % 2 else d - 1) % devices) for d in range(devices)]
    anywhere = pl.BlockSpec(memory_space=pl.ANY)
    off_chip = lax.ppermute(off_chip, AXES, across)
    got = lax.all_to_all(message, AXES, 0, 0, axis_index_groups=SETS, tiled=True)
    blocks = (pltpu.VMEM((1024, 128), BF16), pltpu.VMEM((8, 32, 128), F32))
    send = call(
        sent_kernel, vmem((8, 272, 128), BF16), [VMEM] * 2,
        (pltpu.VMEM((8, 64, 128), F32),) + blocks[::-1],
    )(held(got), held(on_chip))
    came = lax.ppermute(send, "c", beside)
    got, send = lax.optimization_barrier((got, send))
    keep, table = call(
        kept_kernel, (vmem((8, 256, 128), F32), vmem((64, 128), BF16)), [VMEM],
        (pltpu.VMEM((8, 64, 128), F32),) + blocks[::-1],
    )(held(got))
    partial, on_chip = call(
        joined_kernel,
        (vmem((8, 320, 128), BF16), vmem((16, 384), BF16)),
        [VMEM] * 3,
    )(held(keep), held(table), held(came))
    partial = lax.all_to_all(partial, ("y", "xl"), 0, 0, tiled=True)
    incoming = call(
        translate_kernel,
        vmem((8, 256, 128), BF16),
        [VMEM],
        (pltpu.VMEM((2, 256, 128), F32), pltpu.VMEM((256, 128), F32)),
    )(held(partial))
    incoming = lax.all_to_all(incoming, ("y", "xl"), 0, 0, tiled=True)
    beyond = lax.ppermute(incoming, "c", beside)
    near = call(near_kernel, vmem((8, 64, 128), F32), [VMEM] * 2, blocks)(
        held(incoming), held(got)
    )
    parts = call(
        far_kernel, vmem((8, 64, 128), BF16), [VMEM] * 3,
        blocks + (pltpu.VMEM((8, 64, 128), F32),),
    )(held(beyond), held(got), held(near))
    parts, on_chip, off_chip = lax.optimization_barrier((parts, on_chip, off_chip))
    rate, first, nodes, times, factor = call(
        element_kernel,
        (
            shaped((6, 64, 256), F32), vmem((6, 64, 128), F32), vmem((64, 128), F32),
            vmem((64, 128), F32), vmem((6, 8, 128), F32),
        ),
        [SMEM] * 2 + [VMEM] * 9,
    )(
        flux_couple, bound_coef, fields, inv_jacobian.reshape(1, -1), diff_matrix,
        face_interp, lift_matrix.transpose(0, 2, 1), neighbours, time_interp.reshape(1, -1),
        held(on_chip), held(off_chip),
    )
    parts = lax.all_to_all(parts, AXES, 0, 0, axis_index_groups=SETS, tiled=True)
    return call(
        finish_kernel,
        (shaped((6, 64, 256), F32), shaped((64, 128), F32)),
        [VMEM] * 5 + [anywhere],
        (
            pltpu.VMEM((6, 64, 128), F32), pltpu.VMEM((64, 128), F32),
            pltpu.SemaphoreType.DMA((7,)),
        ),
        out_specs=(anywhere, anywhere),
        input_output_aliases={5: 0},
    )(held(parts), held(first), held(nodes), held(times), held(factor), rate)


def solution(mesh):
    mesh = Mesh(np.asarray(mesh.devices).reshape(4, 4, 2, 2, 2), AXES)
    patch, level = ("y", "z", "xl"), ("xh", "c")
    placed = (
        P(None, None, AXES), P(AXES), P(), P(), P(), P(), P(None, AXES), P(None, AXES), P(), P(),
        P(), P(None, AXES), P(None, AXES), P(AXES, None), P(level, patch, None, None),
        P(level, patch, None), P(level, patch),
    )
    return jax.shard_map(
        per_device,
        mesh=mesh,
        in_specs=placed,
        out_specs=(P(None, None, AXES), P(None, AXES)),
        check_vma=False,
    )
```

```python
import jax
import jax.numpy as jnp
import numpy as np
from jax import lax
from jax.experimental import pallas as pl
from jax.experimental.pallas import tpu as pltpu
from jax.sharding import Mesh, PartitionSpec as P


F32 = jnp.float32
BF16 = jnp.bfloat16
HIGH = lax.Precision.HIGHEST
AXES = ("y", "z", "xl", "xh", "c")
VMEM = pl.BlockSpec(memory_space=pltpu.VMEM)
SMEM = pl.BlockSpec(memory_space=pltpu.SMEM)
ROW_C, ROW_W, ROW_T, ROWS = 128, 192, 256, 272
SETS = [
    [((((y * 4 + z) * 2 + (s ^ xh)) * 2 + xh) * 2) + c for z in range(4) for xh in range(2)]
    for y in range(4)
    for s in range(2)
    for c in range(2)
]
NN = (((1,), (0,)), ((), ()))
NT = (((1,), (1,)), ((), ()))
TN = (((0,), (0,)), ((), ()))


def iota(shape, dim):
    return lax.broadcasted_iota(jnp.int32, shape, dim)


def mm(a, b, dims=NN, precision=None):
    return lax.dot_general(a, b, dims, precision=precision, preferred_element_type=F32)


def one_hot(mask, dtype=F32):
    return jnp.where(mask, 1.0, 0.0).astype(dtype)


def halves(x):
    high = x.astype(BF16)
    return high, (x - high.astype(F32)).astype(BF16)


def lane_blocks_swapped(parts):
    parts = list(parts)
    shape = parts[0].shape
    block = iota(shape, 1) // 16
    for m in (4, 2, 1):
        upper = (block & m) != 0
        for j in range(8):
            if j & m:
                continue
            a, b = parts[j], parts[j + m]
            parts[j] = jnp.where(upper, pltpu.roll(b, 16 * m, 1), a)
            parts[j + m] = jnp.where(upper, b, pltpu.roll(a, 128 - 16 * m, 1))
    return parts


def pack_kernel(
    send_ref, dest_ref, count_ref, coef_ref,
    fields_ref, interp_ref, history_ref, weight_ref, projection_ref, kernels_ref,
    message_ref, on_ref, off_ref,
):
    core = lax.axis_index("c")
    elements = fields_ref.shape[2]
    flat = fields_ref[...].reshape(384, elements).astype(BF16)

    def picked(row):
        rows, lanes = iota((16, elements), 0), iota((16, elements), 1)
        wanted = jnp.zeros((16, elements), jnp.int32)
        for i in range(16):
            wanted = jnp.where(rows == i, send_ref[row, i], wanted)
        return mm(one_hot(lanes == wanted, BF16), flat, NT).astype(BF16)

    on_ref[...] = picked(1 - core)
    off_ref[...] = picked(core)
    mixed = jnp.zeros((64, 128), F32)
    for c in range(6):
        mixed = mixed + coef_ref[c] * fields_ref[c, :, 0:128]
    spread = one_hot(iota((128, 128), 1) // 16 == iota((128, 128), 0))
    chosen = one_hot(iota((16, 128), 1) % 16 == iota((16, 128), 0))
    by_element = mm(mixed, spread, NN, HIGH)
    by_node = mm(interp_ref[5], chosen, TN, HIGH)
    newest = jnp.sum(by_element * by_node, axis=0, keepdims=True)
    old = pltpu.roll(history_ref[...].astype(F32), 63, 0)
    currents = jnp.where(iota((64, 128), 0) == 63, newest, old).astype(BF16)
    lane_patch = iota((16, 128), 1) % 32
    wanted = jnp.full((16, 128), -1, jnp.int32)
    for j in range(16):
        to = jnp.where(j < count_ref[0, 0], dest_ref[0, 0, j], -1)
        wanted = jnp.where(iota((16, 128), 0) == j, to, wanted)
    spread_kernels = mm(kernels_ref[0, 0], one_hot(wanted == lane_patch, BF16), TN)
    group_of = iota((8, 128), 1) // 32
    table = []
    for h in range(2):
        rows = jnp.zeros((8, 128), F32)
        for a in range(4):
            at = 32 * h + 8 * a
            rows = jnp.where(group_of == a, spread_kernels[at : at + 8], rows)
        table.append(rows)
    table = jnp.concatenate(table, axis=0).astype(BF16)
    weights = []
    for level in range(4):
        pick = one_hot(iota((32, 128), 1) == 4 * iota((32, 128), 0) + level, BF16)
        weights.append(mm(pick, weight_ref[...]).astype(BF16))
    for i in range(8):
        z, xh = i // 2, i % 2
        message_ref[i, 0:128, :] = projection_ref[:, 128 * z : 128 * z + 128]
        message_ref[i, ROW_C : ROW_C + 64, :] = currents
        message_ref[i, ROW_W : ROW_W + 32, :] = weights[2 * xh]
        message_ref[i, ROW_W + 32 : ROW_W + 64, :] = weights[2 * xh + 1]
        message_ref[i, ROW_T:ROWS, :] = table


def level_weights(got_ref, i, level):
    return got_ref[i, pl.ds(pl.multiple_of(ROW_W + 32 * level, 32), 32), :].astype(F32)


def partial_rays(got_ref, level, out_ref, c_ref, w_ref, p_ref):
    for i in range(8):
        c_ref[i] = got_ref[i, ROW_C : ROW_C + 64, :].astype(F32)
        w_ref[i] = level_weights(got_ref, i, level)
        p_ref[128 * i : 128 * i + 128, :] = got_ref[i, 0:128, :]
    for high in range(8):
        rows = []
        for t in range(8 * high, 8 * high + 8):
            row = []
            for i in range(8):
                c = c_ref[i, pl.ds(t, 8, stride=0), :]
                row.append((w_ref[i].reshape(4, 8, 128) * c[None]).reshape(32, 128))
            rows.append(jnp.concatenate(row, axis=1).astype(BF16))
        product = mm(jnp.concatenate(rows, axis=0), p_ref[...])
        parts = [product[32 * t : 32 * t + 32].astype(out_ref.dtype) for t in range(8)]
        parts = lane_blocks_swapped(parts)
        for r in range(8):
            out_ref[r, 32 * high : 32 * high + 32, :] = parts[r]


def sent_kernel(got_ref, on_ref, send_ref, c_ref, w_ref, p_ref):
    for i in range(3):
        send_ref[i, 256:272, :] = on_ref[:, 128 * i : 128 * i + 128]
    partial_rays(got_ref, 1 - lax.axis_index("c"), send_ref, c_ref, w_ref, p_ref)


def kept_kernel(got_ref, keep_ref, table_ref, c_ref, w_ref, p_ref):
    half = lax.axis_index("xh")
    for z in range(4):
        table_ref[16 * z : 16 * z + 16, :] = got_ref[2 * z + half, ROW_T:ROWS, :]
    partial_rays(got_ref, lax.axis_index("c"), keep_ref, c_ref, w_ref, p_ref)


def joined_kernel(keep_ref, table_ref, came_ref, out_ref, on_ref):
    for r in range(8):
        out_ref[r, 0:256, :] = (keep_ref[r] + came_ref[r, 0:256, :].astype(F32)).astype(BF16)
        out_ref[r, 256:320, :] = table_ref[...]
    for i in range(3):
        on_ref[:, 128 * i : 128 * i + 128] = came_ref[i, 256:272, :]


def translate_kernel(got_ref, out_ref, h_ref, s_ref):
    total = got_ref[0, 0:256, :].astype(F32)
    for r in range(1, 8):
        total = total + got_ref[r, 0:256, :].astype(F32)
    rays = total.astype(BF16)
    for r in range(8):
        y, xl = r // 2, r % 2
        for z in range(4):
            patch = 8 * y + 2 * z + xl
            tile = got_ref[r, 256 + 16 * z : 272 + 16 * z, :].astype(F32)
            for h in range(2):
                h_ref[h, pl.ds(patch, 8, stride=32), :] = tile[8 * h : 8 * h + 8]
    table = jnp.concatenate([h_ref[0], h_ref[1]], axis=1).astype(BF16)
    by_high = [rays[32 * t : 32 * t + 32] for t in range(8)]
    lane = iota((32, 128), 1)
    columns = []
    for t in range(8):
        rows = [by_high[t]]
        for b in range(1, 8):
            here = pltpu.roll(by_high[t], 16 * b, 1)
            before = pltpu.roll(by_high[t - 1], 16 * b, 1) if t > 0 else jnp.zeros((32, 128), BF16)
            rows.append(jnp.where(lane < 16 * b, before, here))
        columns.append(jnp.concatenate(rows, axis=0))
    lagged = [mm(table, column, TN) for column in columns]
    for t in range(8):
        incoming = lagged[t][0:32]
        for a in range(1, t + 1):
            incoming = incoming + lagged[t - a][32 * a : 32 * a + 32]
        s_ref[pl.ds(t, 32, stride=8), :] = incoming
    incoming = s_ref[...].astype(BF16)
    for r in range(8):
        out_ref[r] = incoming


def add_images(incoming_ref, got_ref, level, before_ref, sum_ref, p_ref, w_ref, done=None):
    for i in range(8):
        p_ref[128 * i : 128 * i + 128, :] = got_ref[i, 0:128, :]
        w_ref[i] = level_weights(got_ref, i, level)
    for chunk in range(2):
        at = 128 * chunk
        parts = [incoming_ref[r, at : at + 128, :] for r in range(8)]
        rows = jnp.concatenate(lane_blocks_swapped(parts), axis=0)
        start = sum_ref if chunk > 0 else before_ref
        for i in range(4):
            image = mm(rows, p_ref[256 * i : 256 * i + 256, :], NT)
            weight = [
                jnp.concatenate(
                    [w_ref[2 * i + s, pl.ds(q, 8, stride=0), :] for s in range(2)], axis=1
                )
                for q in range(16 * chunk, 16 * chunk + 16)
            ]
            for t in range(8):
                total = image[128 * t : 128 * t + 8] * weight[0]
                for q in range(1, 16):
                    at = 128 * t + 8 * q
                    total = total + image[at : at + 8] * weight[q]
                for s in range(2):
                    part = total[:, 128 * s : 128 * s + 128]
                    if start is not None:
                        part = part + start[2 * i + s, 8 * t : 8 * t + 8, :]
                    sum_ref[2 * i + s, 8 * t : 8 * t + 8, :] = part
            if done is not None and chunk == 1:
                done(i)


def near_kernel(here_ref, got_ref, sum_ref, p_ref, w_ref):
    add_images(here_ref, got_ref, lax.axis_index("c"), None, sum_ref, p_ref, w_ref)


def far_kernel(
    there_ref, got_ref, before_ref, out_ref, p_ref, w_ref, sum_ref, stage_ref, sems,
):
    copies = []

    def done(i):
        at = pl.ds(2 * i, 2)
        stage_ref[at] = sum_ref[at].astype(BF16)
        copies.append(pltpu.make_async_copy(stage_ref.at[at], out_ref.at[at], sems.at[i]))
        copies[-1].start()

    level = 1 - lax.axis_index("c")
    add_images(there_ref, got_ref, level, before_ref, sum_ref, p_ref, w_ref, done)
    for copy in copies:
        copy.wait()


def element_kernel(
    couple_ref, bound_ref, fields_ref, scale_ref, diff_ref, interp_ref, lift_ref,
    links_ref, time_ref, on_ref, off_ref, out_ref, first_ref, nodes_ref, times_ref, factor_ref,
):
    core = lax.axis_index("c")
    elements = fields_ref.shape[2]
    both = jnp.concatenate([interp_ref[...].reshape(96, 64), diff_ref[...].reshape(192, 64)], axis=0)
    both_high, both_low = halves(both)
    both = jnp.concatenate([both_high, both_high, both_low], axis=1)
    ghosts = jnp.concatenate([on_ref[...], off_ref[...]], axis=0)
    own, ghost, grads = [], [], []
    for c in range(6):
        high, low = halves(fields_ref[c])
        product = mm(both, jnp.concatenate([high, low, high], axis=0))
        own.append(product[0:96])
        grads.append(product[96:288])
        beyond = ghosts[:, 64 * c : 64 * c + 64]
        ghost.append(mm(both_high[0:96], beyond, NT) + mm(both_low[0:96], beyond, NT))
    fluxes = [[] for _ in range(6)]
    bound = iota((16, elements), 1) < 8
    for f in range(6):
        at, to = 16 * f, 16 * (f ^ 1)
        pool = jnp.concatenate([own[c][to : to + 16] for c in range(6)], axis=0)
        beyond = jnp.concatenate([ghost[c][to : to + 16] for c in range(6)], axis=0)
        links = links_ref[f : f + 1, :]
        inside = one_hot(iota((elements, elements), 0) == links, BF16)
        outer = links - elements
        outer = jnp.where(core == 0, outer ^ 16, outer)
        outside = one_hot(iota((32, elements), 0) == outer, BF16)
        across = mm(jnp.concatenate(halves(pool), axis=0), inside)
        across = across + mm(jnp.concatenate(halves(beyond), axis=0), outside)
        across = across[0:96] + across[96:192]
        jumps = []
        for c in range(6):
            there = across[16 * c : 16 * c + 16]
            if f == 5:
                there = jnp.where(bound, 0.0, there)
            jumps.append(there - own[c][at : at + 16])
        for c in range(6):
            flux = couple_ref[f, c, 0] * jumps[0]
            for k in range(1, 6):
                flux = flux + couple_ref[f, c, k] * jumps[k]
            fluxes[c].append(flux)
    lift = lift_ref[...].reshape(96, 64)
    lift_high, lift_low = halves(lift)

    def grad(r, c):
        return grads[c][64 * r : 64 * r + 64]

    curls = (
        grad(1, 5) - grad(2, 4),
        grad(2, 3) - grad(0, 5),
        grad(0, 4) - grad(1, 3),
        grad(2, 1) - grad(1, 2),
        grad(0, 2) - grad(2, 0),
        grad(1, 0) - grad(0, 1),
    )
    scale = scale_ref[...]
    for c in range(6):
        high, low = halves(jnp.concatenate(fluxes[c], axis=0))
        surface = mm(lift_high, high, TN) + mm(lift_high, low, TN) + mm(lift_low, high, TN)
        value = curls[c] * scale + surface
        out_ref[c] = value
        first_ref[c] = value[:, 0:128]
    chosen = one_hot(iota((16, 128), 1) % 16 == iota((16, 128), 0))
    nodes_ref[...] = mm(lift_ref[5], chosen, TN, HIGH)
    row, sample = iota((64, 64), 0), iota((64, 64), 1)
    times = jnp.where(row % 8 * 8 + row // 8 == sample, time_ref[...], 0.0)
    times_ref[...] = jnp.broadcast_to(jnp.sum(times, axis=1, keepdims=True), (64, 128))
    for c in range(6):
        factor = couple_ref[5, c, 0] * bound_ref[0]
        for k in range(1, 6):
            factor = factor + couple_ref[5, c, k] * bound_ref[k]
        factor_ref[c] = jnp.full((8, 128), factor, F32)


def finish_kernel(
    parts_ref, first_ref, nodes_ref, times_ref, factor_ref, rate_ref, rate_out, field_out,
    tile_ref, field_ref, sems,
):
    del rate_ref
    total = parts_ref[0].astype(F32)
    for i in range(1, 8):
        total = total + parts_ref[i].astype(F32)
    total = total * jnp.float32(1.0 / np.sqrt(np.float32(512)))
    for t in range(8):
        field_ref[pl.ds(t, 8, stride=8), :] = total[8 * t : 8 * t + 8]
    copies = [pltpu.make_async_copy(field_ref, field_out, sems.at[6])]
    copies[0].start()
    now = jnp.sum(times_ref[...] * total, axis=0, keepdims=True)
    collect = one_hot(iota((256, 128), 0) % 128 // 16 == iota((256, 128), 1), BF16)
    lifted = mm(jnp.concatenate(halves(nodes_ref[...] * now), axis=1), collect)
    for c in range(6):
        tile_ref[c] = first_ref[c] + factor_ref[c, 0:1, :] * lifted
        copy = pltpu.make_async_copy(tile_ref.at[c], rate_out.at[c, :, pl.ds(0, 128)], sems.at[c])
        copy.start()
        copies.append(copy)
    for copy in copies:
        copy.wait()


def call(kernel, out, in_specs, scratch=(), out_specs=None, grant=24, **options):
    run = pl.pallas_call(
        kernel,
        out_shape=out,
        in_specs=in_specs,
        out_specs=jax.tree.map(lambda _: VMEM, out) if out_specs is None else out_specs,
        scratch_shapes=list(scratch),
        compiler_params=pltpu.CompilerParams(vmem_limit_bytes=grant << 20),
        **options,
    )
    return run


def held(x):
    return pltpu.with_memory_space_constraint(x, pltpu.VMEM)


def shaped(shape, dtype):
    return jax.ShapeDtypeStruct(shape, dtype)


def vmem(shape, dtype):
    return pltpu.VMEM(shape, dtype)


def per_device(
    fields, inv_jacobian, diff_matrix, face_interp, lift_matrix, flux_couple, neighbours,
    send_index, bound_coef, current_coef, time_interp, current_history, group_weight, projection,
    kernels, pair_dest, pair_count,
):
    message, on_chip, off_chip = call(
        pack_kernel,
        (vmem((8, ROWS, 128), BF16), vmem((16, 384), BF16), vmem((16, 384), BF16)),
        [SMEM] * 4 + [VMEM] * 6,
        grant=60,
    )(
        send_index, pair_dest, pair_count, current_coef,
        fields, face_interp, current_history, group_weight, projection, kernels,
    )
    devices = 128
    beside = [(0, 1), (1, 0)]
    across = [(d, (d + 1 if d % 2 else d - 1) % devices) for d in range(devices)]
    anywhere = pl.BlockSpec(memory_space=pl.ANY)
    off_chip = lax.ppermute(off_chip, AXES, across)
    got = lax.all_to_all(message, AXES, 0, 0, axis_index_groups=SETS, tiled=True)
    blocks = (pltpu.VMEM((1024, 128), BF16), pltpu.VMEM((8, 32, 128), F32))
    send = call(
        sent_kernel, vmem((8, 272, 128), BF16), [VMEM] * 2,
        (pltpu.VMEM((8, 64, 128), F32),) + blocks[::-1],
    )(held(got), held(on_chip))
    came = lax.ppermute(send, "c", beside)
    got, send = lax.optimization_barrier((got, send))
    keep, table = call(
        kept_kernel, (vmem((8, 256, 128), F32), vmem((64, 128), BF16)), [VMEM],
        (pltpu.VMEM((8, 64, 128), F32),) + blocks[::-1],
    )(held(got))
    partial, on_chip = call(
        joined_kernel,
        (vmem((8, 320, 128), BF16), vmem((16, 384), BF16)),
        [VMEM] * 3,
    )(held(keep), held(table), held(came))
    partial = lax.all_to_all(partial, ("y", "xl"), 0, 0, tiled=True)
    incoming = call(
        translate_kernel,
        vmem((8, 256, 128), BF16),
        [VMEM],
        (pltpu.VMEM((2, 256, 128), F32), pltpu.VMEM((256, 128), F32)),
    )(held(partial))
    incoming = lax.all_to_all(incoming, ("y", "xl"), 0, 0, tiled=True)
    beyond = lax.ppermute(incoming, "c", beside)
    near = call(near_kernel, vmem((8, 64, 128), F32), [VMEM] * 2, blocks)(
        held(incoming), held(got)
    )
    parts = call(
        far_kernel, shaped((8, 64, 128), BF16), [VMEM] * 3,
        blocks + (
            pltpu.VMEM((8, 64, 128), F32), pltpu.VMEM((8, 64, 128), BF16),
            pltpu.SemaphoreType.DMA((4,)),
        ),
        out_specs=anywhere,
    )(held(beyond), held(got), held(near))
    parts, on_chip, off_chip = lax.optimization_barrier((parts, on_chip, off_chip))
    rate, first, nodes, times, factor = call(
        element_kernel,
        (
            shaped((6, 64, 256), F32), vmem((6, 64, 128), F32), vmem((64, 128), F32),
            vmem((64, 128), F32), vmem((6, 8, 128), F32),
        ),
        [SMEM] * 2 + [VMEM] * 9,
    )(
        flux_couple, bound_coef, fields, inv_jacobian.reshape(1, -1), diff_matrix,
        face_interp, lift_matrix.transpose(0, 2, 1), neighbours, time_interp.reshape(1, -1),
        held(on_chip), held(off_chip),
    )
    parts = lax.all_to_all(parts, AXES, 0, 0, axis_index_groups=SETS, tiled=True)
    return call(
        finish_kernel,
        (shaped((6, 64, 256), F32), shaped((64, 128), F32)),
        [VMEM] * 5 + [anywhere],
        (
            pltpu.VMEM((6, 64, 128), F32), pltpu.VMEM((64, 128), F32),
            pltpu.SemaphoreType.DMA((7,)),
        ),
        out_specs=(anywhere, anywhere),
        input_output_aliases={5: 0},
    )(held(parts), held(first), held(nodes), held(times), held(factor), rate)


def solution(mesh):
    mesh = Mesh(np.asarray(mesh.devices).reshape(4, 4, 2, 2, 2), AXES)
    patch, level = ("y", "z", "xl"), ("xh", "c")
    placed = (
        P(None, None, AXES), P(AXES), P(), P(), P(), P(), P(None, AXES), P(None, AXES), P(), P(),
        P(), P(None, AXES), P(None, AXES), P(AXES, None), P(level, patch, None, None),
        P(level, patch, None), P(level, patch),
    )
    return jax.shard_map(
        per_device,
        mesh=mesh,
        in_specs=placed,
        out_specs=(P(None, None, AXES), P(None, AXES)),
        check_vma=False,
    )
```

```python
import jax
import jax.numpy as jnp
import numpy as np
from jax import lax
from jax.experimental import pallas as pl
from jax.experimental.pallas import tpu as pltpu
from jax.sharding import Mesh, PartitionSpec as P


F32 = jnp.float32
BF16 = jnp.bfloat16
HIGH = lax.Precision.HIGHEST
AXES = ("y", "z", "xl", "xh", "c")
VMEM = pl.BlockSpec(memory_space=pltpu.VMEM)
SMEM = pl.BlockSpec(memory_space=pltpu.SMEM)
ROW_C, ROW_W, ROW_T, ROWS = 128, 192, 256, 272
SETS = [
    [((((y * 4 + z) * 2 + (s ^ xh)) * 2 + xh) * 2) + c for z in range(4) for xh in range(2)]
    for y in range(4)
    for s in range(2)
    for c in range(2)
]
NN = (((1,), (0,)), ((), ()))
NT = (((1,), (1,)), ((), ()))
TN = (((0,), (0,)), ((), ()))


def iota(shape, dim):
    return lax.broadcasted_iota(jnp.int32, shape, dim)


def mm(a, b, dims=NN, precision=None):
    return lax.dot_general(a, b, dims, precision=precision, preferred_element_type=F32)


def one_hot(mask, dtype=F32):
    return jnp.where(mask, 1.0, 0.0).astype(dtype)


def halves(x):
    high = x.astype(BF16)
    return high, (x - high.astype(F32)).astype(BF16)


def lane_blocks_swapped(parts):
    parts = list(parts)
    shape = parts[0].shape
    block = iota(shape, 1) // 16
    for m in (4, 2, 1):
        upper = (block & m) != 0
        for j in range(8):
            if j & m:
                continue
            a, b = parts[j], parts[j + m]
            parts[j] = jnp.where(upper, pltpu.roll(b, 16 * m, 1), a)
            parts[j + m] = jnp.where(upper, b, pltpu.roll(a, 128 - 16 * m, 1))
    return parts


def pack_kernel(
    send_ref, dest_ref, count_ref, coef_ref,
    fields_ref, interp_ref, history_ref, weight_ref, projection_ref, kernels_ref,
    message_ref, on_ref, off_ref,
):
    core = lax.axis_index("c")
    elements = fields_ref.shape[2]
    flat = fields_ref[...].reshape(384, elements).astype(BF16)

    def picked(row):
        rows, lanes = iota((16, elements), 0), iota((16, elements), 1)
        wanted = jnp.zeros((16, elements), jnp.int32)
        for i in range(16):
            wanted = jnp.where(rows == i, send_ref[row, i], wanted)
        return mm(one_hot(lanes == wanted, BF16), flat, NT).astype(BF16)

    on_ref[...] = picked(1 - core)
    off_ref[...] = picked(core)
    mixed = jnp.zeros((64, 128), F32)
    for c in range(6):
        mixed = mixed + coef_ref[c] * fields_ref[c, :, 0:128]
    spread = one_hot(iota((128, 128), 1) // 16 == iota((128, 128), 0))
    chosen = one_hot(iota((16, 128), 1) % 16 == iota((16, 128), 0))
    by_element = mm(mixed, spread, NN, HIGH)
    by_node = mm(interp_ref[5], chosen, TN, HIGH)
    newest = jnp.sum(by_element * by_node, axis=0, keepdims=True)
    old = pltpu.roll(history_ref[...].astype(F32), 63, 0)
    currents = jnp.where(iota((64, 128), 0) == 63, newest, old).astype(BF16)
    lane_patch = iota((16, 128), 1) % 32
    wanted = jnp.full((16, 128), -1, jnp.int32)
    for j in range(16):
        to = jnp.where(j < count_ref[0, 0], dest_ref[0, 0, j], -1)
        wanted = jnp.where(iota((16, 128), 0) == j, to, wanted)
    spread_kernels = mm(kernels_ref[0, 0], one_hot(wanted == lane_patch, BF16), TN)
    group_of = iota((8, 128), 1) // 32
    table = []
    for h in range(2):
        rows = jnp.zeros((8, 128), F32)
        for a in range(4):
            at = 32 * h + 8 * a
            rows = jnp.where(group_of == a, spread_kernels[at : at + 8], rows)
        table.append(rows)
    table = jnp.concatenate(table, axis=0).astype(BF16)
    weights = []
    for level in range(4):
        pick = one_hot(iota((32, 128), 1) == 4 * iota((32, 128), 0) + level, BF16)
        weights.append(mm(pick, weight_ref[...]).astype(BF16))
    for i in range(8):
        z, xh = i // 2, i % 2
        message_ref[i, 0:128, :] = projection_ref[:, 128 * z : 128 * z + 128]
        message_ref[i, ROW_C : ROW_C + 64, :] = currents
        message_ref[i, ROW_W : ROW_W + 32, :] = weights[2 * xh]
        message_ref[i, ROW_W + 32 : ROW_W + 64, :] = weights[2 * xh + 1]
        message_ref[i, ROW_T:ROWS, :] = table


def level_weights(got_ref, i, level):
    return got_ref[i, pl.ds(pl.multiple_of(ROW_W + 32 * level, 32), 32), :].astype(F32)


def partial_rays(got_ref, level, out_ref, c_ref, w_ref, p_ref):
    for i in range(8):
        c_ref[i, 0:64, :] = got_ref[i, ROW_C : ROW_C + 64, :].astype(F32)
        w_ref[i, 0:32, :] = level_weights(got_ref, i, level)
        p_ref[128 * i : 128 * i + 128, :] = got_ref[i, 0:128, :]
    for high in range(8):
        rows = []
        for t in range(8 * high, 8 * high + 8):
            row = []
            for i in range(8):
                c = c_ref[i, pl.ds(t, 8, stride=0), :]
                row.append((w_ref[i, 0:32, :].reshape(4, 8, 128) * c[None]).reshape(32, 128))
            rows.append(jnp.concatenate(row, axis=1).astype(BF16))
        product = mm(jnp.concatenate(rows, axis=0), p_ref[...])
        parts = [product[32 * t : 32 * t + 32].astype(out_ref.dtype) for t in range(8)]
        parts = lane_blocks_swapped(parts)
        for r in range(8):
            out_ref[r, 32 * high : 32 * high + 32, :] = parts[r]


def sent_kernel(got_ref, on_ref, send_ref, c_ref, w_ref, p_ref):
    for i in range(3):
        send_ref[i, 256:272, :] = on_ref[:, 128 * i : 128 * i + 128]
    partial_rays(got_ref, 1 - lax.axis_index("c"), send_ref, c_ref, w_ref, p_ref)


def kept_kernel(got_ref, keep_ref, table_ref, c_ref, w_ref, p_ref):
    half = lax.axis_index("xh")
    for z in range(4):
        table_ref[16 * z : 16 * z + 16, :] = got_ref[2 * z + half, ROW_T:ROWS, :]
    partial_rays(got_ref, lax.axis_index("c"), keep_ref, c_ref, w_ref, p_ref)


def joined_kernel(keep_ref, table_ref, came_ref, out_ref, on_ref):
    for r in range(8):
        out_ref[r, 0:256, :] = (keep_ref[r] + came_ref[r, 0:256, :].astype(F32)).astype(BF16)
        out_ref[r, 256:320, :] = table_ref[...]
    for i in range(3):
        on_ref[:, 128 * i : 128 * i + 128] = came_ref[i, 256:272, :]


def translate_kernel(got_ref, out_ref, h_ref, s_ref):
    total = got_ref[0, 0:256, :].astype(F32)
    for r in range(1, 8):
        total = total + got_ref[r, 0:256, :].astype(F32)
    rays = total.astype(BF16).astype(F32)
    for r in range(8):
        y, xl = r // 2, r % 2
        for z in range(4):
            patch = 8 * y + 2 * z + xl
            tile = got_ref[r, 256 + 16 * z : 272 + 16 * z, :].astype(F32)
            for h in range(2):
                h_ref[h, pl.ds(patch, 8, stride=32), :] = tile[8 * h : 8 * h + 8]
    table = jnp.concatenate([h_ref[0, 0:256, :], h_ref[1, 0:256, :]], axis=1).astype(BF16)
    by_high = [rays[32 * t : 32 * t + 32] for t in range(8)]
    lane = iota((32, 128), 1)
    columns = []
    for t in range(8):
        rows = [by_high[t]]
        for b in range(1, 8):
            here = pltpu.roll(by_high[t], 16 * b, 1)
            before = pltpu.roll(by_high[t - 1], 16 * b, 1) if t > 0 else jnp.zeros((32, 128), F32)
            rows.append(jnp.where(lane < 16 * b, before, here))
        columns.append(jnp.concatenate(rows, axis=0).astype(BF16))
    lagged = [mm(table, column, TN) for column in columns]
    for t in range(8):
        incoming = lagged[t][0:32]
        for a in range(1, t + 1):
            incoming = incoming + lagged[t - a][32 * a : 32 * a + 32]
        s_ref[pl.ds(t, 32, stride=8), :] = incoming
    incoming = s_ref[0:256, :].astype(BF16)
    for r in range(8):
        out_ref[r] = incoming


def add_images(incoming_ref, got_ref, level, before_ref, sum_ref, p_ref, w_ref):
    for i in range(8):
        p_ref[128 * i : 128 * i + 128, :] = got_ref[i, 0:128, :]
        w_ref[i, 0:32, :] = level_weights(got_ref, i, level)
    for chunk in range(2):
        at = 128 * chunk
        parts = [incoming_ref[r, at : at + 128, :] for r in range(8)]
        rows = jnp.concatenate(lane_blocks_swapped(parts), axis=0)
        start = sum_ref if chunk > 0 else before_ref
        for i in range(4):
            image = mm(rows, p_ref[256 * i : 256 * i + 256, :], NT)
            weight = [
                jnp.concatenate(
                    [w_ref[2 * i + s, pl.ds(q, 8, stride=0), :] for s in range(2)], axis=1
                )
                for q in range(16 * chunk, 16 * chunk + 16)
            ]
            for t in range(8):
                total = image[128 * t : 128 * t + 8] * weight[0]
                for q in range(1, 16):
                    at = 128 * t + 8 * q
                    total = total + image[at : at + 8] * weight[q]
                for s in range(2):
                    part = total[:, 128 * s : 128 * s + 128]
                    if start is not None:
                        part = part + start[2 * i + s, 8 * t : 8 * t + 8, :]
                    sum_ref[2 * i + s, 8 * t : 8 * t + 8, :] = part


def near_kernel(here_ref, got_ref, sum_ref, p_ref, w_ref):
    add_images(here_ref, got_ref, lax.axis_index("c"), None, sum_ref, p_ref, w_ref)


def far_kernel(there_ref, got_ref, before_ref, out_ref, p_ref, w_ref, sum_ref):
    add_images(there_ref, got_ref, 1 - lax.axis_index("c"), before_ref, sum_ref, p_ref, w_ref)
    for i in range(8):
        out_ref[i] = sum_ref[i].astype(BF16)


def element_kernel(
    couple_ref, bound_ref, fields_ref, scale_ref, diff_ref, interp_ref, lift_ref,
    links_ref, time_ref, on_ref, off_ref, out_ref, first_ref, nodes_ref, times_ref, factor_ref,
):
    core = lax.axis_index("c")
    elements = fields_ref.shape[2]
    both = jnp.concatenate([interp_ref[...].reshape(96, 64), diff_ref[...].reshape(192, 64)], axis=0)
    both_high, both_low = halves(both)
    both = jnp.concatenate([both_high, both_high, both_low], axis=1)
    ghosts = jnp.concatenate([on_ref[...], off_ref[...]], axis=0)
    own, ghost, grads = [], [], []
    for c in range(6):
        high, low = halves(fields_ref[c])
        product = mm(both, jnp.concatenate([high, low, high], axis=0))
        own.append(product[0:96])
        grads.append(product[96:288])
        beyond = ghosts[:, 64 * c : 64 * c + 64]
        ghost.append(mm(both_high[0:96], beyond, NT) + mm(both_low[0:96], beyond, NT))
    fluxes = [[] for _ in range(6)]
    bound = iota((16, elements), 1) < 8
    for f in range(6):
        at, to = 16 * f, 16 * (f ^ 1)
        pool = jnp.concatenate([own[c][to : to + 16] for c in range(6)], axis=0)
        beyond = jnp.concatenate([ghost[c][to : to + 16] for c in range(6)], axis=0)
        links = links_ref[f : f + 1, :]
        inside = one_hot(iota((elements, elements), 0) == links, BF16)
        outer = links - elements
        outer = jnp.where(core == 0, outer ^ 16, outer)
        outside = one_hot(iota((32, elements), 0) == outer, BF16)
        across = mm(jnp.concatenate(halves(pool), axis=0), inside)
        across = across + mm(jnp.concatenate(halves(beyond), axis=0), outside)
        across = across[0:96] + across[96:192]
        jumps = []
        for c in range(6):
            there = across[16 * c : 16 * c + 16]
            if f == 5:
                there = jnp.where(bound, 0.0, there)
            jumps.append(there - own[c][at : at + 16])
        for c in range(6):
            flux = couple_ref[f, c, 0] * jumps[0]
            for k in range(1, 6):
                flux = flux + couple_ref[f, c, k] * jumps[k]
            fluxes[c].append(flux)
    lift = lift_ref[...].reshape(96, 64)
    lift_high, lift_low = halves(lift)

    def grad(r, c):
        return grads[c][64 * r : 64 * r + 64]

    curls = (
        grad(1, 5) - grad(2, 4),
        grad(2, 3) - grad(0, 5),
        grad(0, 4) - grad(1, 3),
        grad(2, 1) - grad(1, 2),
        grad(0, 2) - grad(2, 0),
        grad(1, 0) - grad(0, 1),
    )
    scale = scale_ref[...]
    for c in range(6):
        high, low = halves(jnp.concatenate(fluxes[c], axis=0))
        surface = mm(lift_high, high, TN) + mm(lift_high, low, TN) + mm(lift_low, high, TN)
        value = curls[c] * scale + surface
        out_ref[c] = value
        first_ref[c] = value[:, 0:128]
    chosen = one_hot(iota((16, 128), 1) % 16 == iota((16, 128), 0))
    nodes_ref[...] = mm(lift_ref[5], chosen, TN, HIGH)
    row, sample = iota((64, 64), 0), iota((64, 64), 1)
    times = jnp.where(row % 8 * 8 + row // 8 == sample, time_ref[...], 0.0)
    times_ref[...] = jnp.broadcast_to(jnp.sum(times, axis=1, keepdims=True), (64, 128))
    for c in range(6):
        factor = couple_ref[5, c, 0] * bound_ref[0]
        for k in range(1, 6):
            factor = factor + couple_ref[5, c, k] * bound_ref[k]
        factor_ref[c] = jnp.full((8, 128), factor, F32)


def finish_kernel(
    parts_ref, first_ref, nodes_ref, times_ref, factor_ref, rate_ref, rate_out, field_out,
    tile_ref, field_ref, sems,
):
    del rate_ref
    total = parts_ref[0].astype(F32)
    for i in range(1, 8):
        total = total + parts_ref[i].astype(F32)
    total = total * jnp.float32(1.0 / np.sqrt(np.float32(512)))
    for t in range(8):
        field_ref[pl.ds(t, 8, stride=8), :] = total[8 * t : 8 * t + 8]
    copies = [pltpu.make_async_copy(field_ref.at[pl.ds(0, 64)], field_out, sems.at[6])]
    copies[0].start()
    now = jnp.sum(times_ref[...] * total, axis=0, keepdims=True)
    collect = one_hot(iota((256, 128), 0) % 128 // 16 == iota((256, 128), 1), BF16)
    lifted = mm(jnp.concatenate(halves(nodes_ref[...] * now), axis=1), collect)
    for c in range(6):
        tile_ref[c] = first_ref[c] + factor_ref[c, 0:1, :] * lifted
        copy = pltpu.make_async_copy(tile_ref.at[c], rate_out.at[c, :, pl.ds(0, 128)], sems.at[c])
        copy.start()
        copies.append(copy)
    for copy in copies:
        copy.wait()


def call(kernel, out, in_specs, scratch=(), out_specs=None, grant=24, **options):
    run = pl.pallas_call(
        kernel,
        out_shape=out,
        in_specs=in_specs,
        out_specs=jax.tree.map(lambda _: VMEM, out) if out_specs is None else out_specs,
        scratch_shapes=list(scratch),
        compiler_params=pltpu.CompilerParams(vmem_limit_bytes=grant << 20),
        **options,
    )
    return run


def held(x):
    return pltpu.with_memory_space_constraint(x, pltpu.VMEM)


def shaped(shape, dtype):
    return jax.ShapeDtypeStruct(shape, dtype)


def vmem(shape, dtype):
    return pltpu.VMEM(shape, dtype)


def per_device(
    fields, inv_jacobian, diff_matrix, face_interp, lift_matrix, flux_couple, neighbours,
    send_index, bound_coef, current_coef, time_interp, current_history, group_weight, projection,
    kernels, pair_dest, pair_count,
):
    message, on_chip, off_chip = call(
        pack_kernel,
        (vmem((8, ROWS, 128), BF16), vmem((16, 384), BF16), vmem((16, 384), BF16)),
        [SMEM] * 4 + [VMEM] * 6,
        grant=60,
    )(
        send_index, pair_dest, pair_count, current_coef,
        fields, face_interp, current_history, group_weight, projection, kernels,
    )
    devices = 128
    beside = [(0, 1), (1, 0)]
    across = [(d, (d + 1 if d % 2 else d - 1) % devices) for d in range(devices)]
    anywhere = pl.BlockSpec(memory_space=pl.ANY)
    off_chip = lax.ppermute(off_chip, AXES, across)
    got = lax.all_to_all(message, AXES, 0, 0, axis_index_groups=SETS, tiled=True)
    blocks = (pltpu.VMEM((1024, 128), BF16), pltpu.VMEM((8, 40, 128), F32))
    send = call(
        sent_kernel, vmem((8, 272, 128), BF16), [VMEM] * 2,
        (pltpu.VMEM((8, 72, 128), F32),) + blocks[::-1],
    )(held(got), held(on_chip))
    came = lax.ppermute(send, "c", beside)
    got, send = lax.optimization_barrier((got, send))
    keep, table = call(
        kept_kernel, (vmem((8, 256, 128), F32), vmem((64, 128), BF16)), [VMEM],
        (pltpu.VMEM((8, 72, 128), F32),) + blocks[::-1],
    )(held(got))
    partial, on_chip = call(
        joined_kernel,
        (vmem((8, 320, 128), BF16), vmem((16, 384), BF16)),
        [VMEM] * 3,
    )(held(keep), held(table), held(came))
    partial = lax.all_to_all(partial, ("y", "xl"), 0, 0, tiled=True)
    incoming = call(
        translate_kernel,
        vmem((8, 256, 128), BF16),
        [VMEM],
        (pltpu.VMEM((2, 288, 128), F32), pltpu.VMEM((264, 128), F32)),
    )(held(partial))
    incoming = lax.all_to_all(incoming, ("y", "xl"), 0, 0, tiled=True)
    beyond = lax.ppermute(incoming, "c", beside)
    near = call(near_kernel, vmem((8, 64, 128), F32), [VMEM] * 2, blocks)(
        held(incoming), held(got)
    )
    parts = call(
        far_kernel, vmem((8, 64, 128), BF16), [VMEM] * 3,
        blocks + (pltpu.VMEM((8, 64, 128), F32),),
    )(held(beyond), held(got), held(near))
    parts, on_chip, off_chip = lax.optimization_barrier((parts, on_chip, off_chip))
    rate, first, nodes, times, factor = call(
        element_kernel,
        (
            shaped((6, 64, 256), F32), vmem((6, 64, 128), F32), vmem((64, 128), F32),
            vmem((64, 128), F32), vmem((6, 8, 128), F32),
        ),
        [SMEM] * 2 + [VMEM] * 9,
    )(
        flux_couple, bound_coef, fields, inv_jacobian.reshape(1, -1), diff_matrix,
        face_interp, lift_matrix.transpose(0, 2, 1), neighbours, time_interp.reshape(1, -1),
        held(on_chip), held(off_chip),
    )
    parts = lax.all_to_all(parts, AXES, 0, 0, axis_index_groups=SETS, tiled=True)
    return call(
        finish_kernel,
        (shaped((6, 64, 256), F32), shaped((64, 128), F32)),
        [VMEM] * 5 + [anywhere],
        (
            pltpu.VMEM((6, 64, 128), F32), pltpu.VMEM((72, 128), F32),
            pltpu.SemaphoreType.DMA((7,)),
        ),
        out_specs=(anywhere, anywhere),
        input_output_aliases={5: 0},
    )(held(parts), held(first), held(nodes), held(times), held(factor), rate)


def solution(mesh):
    mesh = Mesh(np.asarray(mesh.devices).reshape(4, 4, 2, 2, 2), AXES)
    patch, level = ("y", "z", "xl"), ("xh", "c")
    placed = (
        P(None, None, AXES), P(AXES), P(), P(), P(), P(), P(None, AXES), P(None, AXES), P(), P(),
        P(), P(None, AXES), P(None, AXES), P(AXES, None), P(level, patch, None, None),
        P(level, patch, None), P(level, patch),
    )
    return jax.shard_map(
        per_device,
        mesh=mesh,
        in_specs=placed,
        out_specs=(P(None, None, AXES), P(None, AXES)),
        check_vma=False,
    )
```
